32 devices in a mesh: groups: 2 (over x), dom: 16 (over z, y, core).
Axes of the slice: x: 2, y: 2, z: 4, core: 2. Of those that a mesh axis runs over, the one named last changes fastest.
Arguments:
- points: bfloat16 [655360, 256], P(('groups', 'dom')), parts along dimension 0
- counts: int32 [32], P(('groups', 'dom')), parts along dimension 0, may hold values from 0 to 160, as said below
- destination: int32 [5120], P(('groups', 'dom')), parts along dimension 0, may hold values from -1 to 1279, as said below
- proj_weight: bfloat16 [256, 256], replicated, may hold values from -0.375 to 0.375
- proj_bias: float32 [256], replicated, may hold values from -3 to 3
- slice_weight: bfloat16 [32, 32], replicated, may hold values from -1 to 1
- softness_matrix: bfloat16 [32], replicated, may hold values from -1 to 1
- token_qkv_weight: float32 [3, 32, 32], replicated, may hold values from -1 to 1
- out_weight: bfloat16 [256, 256], replicated, may hold values from -0.375 to 0.375
- out_bias: float32 [256], replicated, may hold values from -2 to 2
Outputs:
- result: bfloat16 [327680, 256], P(('groups', 'dom')), parts along dimension 0
The draws below stay inside these ranges and needn't reach their ends.
There are 2 independent parts, one for each index of `groups`. The reference program is written for one: setup_inputs(seed, part) draws one part's arguments, and reference() takes and returns one part's arrays. A program takes and returns all parts, laid end to end along the dimension named above; an argument that names none is the same for every part. Nothing has to cross between parts.
Inputs may be any that keep to these rules, and one draw needn't show every extreme that they name: `counts`: the entries sum to 1280; each is at most 160, and some owner holds exactly 160. `destination`: slot t of owner o holds a placed tile index when t < counts[o], else -1. Placed indices of live slots are distinct and cover all 1280 placed tiles; placed tile p lies on device p // 80. At most 10 live tiles of one owner go to one device, and this is reached in every draw.
All inputs are finite; a program needn't handle non-finite values.
Results may differ from the reference program's by a relative error of at most 0.0014.
The reference program's roundings to bfloat16 on the way count: a program that leaves them out, or rounds other values in their place, can miss the bound.
Values may be sent and summed in bfloat16 or wider, within the bound.
A program may use at most 128 MiB of HBM per device.

```python
import jax
import jax.numpy as jnp
from jax import lax

MODEL_WIDTH = 256
FOCUS_GROUPS = 8
HEAD_FEATURES = 32
PARTITION_TALLY = 32
TILE = 128
LAND = 80
CAP = 160
PEER = 10
N_DOM = 16


def placement_plan(key):
    base = jax.random.fold_in(key, 7)
    slice_keys = jax.random.split(base, 5)
    order = jax.random.permutation(slice_keys[0], N_DOM)
    shifts = jax.random.randint(slice_keys[1], (N_DOM,), 0, LAND + 1)
    shifts = shifts.at[0].set(LAND).at[N_DOM - 1].set(0)
    by_place = LAND + shifts - jnp.roll(shifts, 1)
    counts = jnp.zeros((N_DOM,), jnp.int32).at[order].set(by_place.astype(jnp.int32))
    starts = jnp.cumsum(counts) - counts
    total = N_DOM * LAND
    offset = jax.random.randint(slice_keys[2], (), 0, total)
    device_order = jax.random.permutation(slice_keys[3], N_DOM)
    tile_index = jnp.arange(CAP, dtype=jnp.int32)
    scores = jax.random.randint(slice_keys[4], (N_DOM, CAP), 0, 1 << 20) * CAP + tile_index[None, :]
    live_mask = tile_index[None, :] < counts[:, None]
    scores = jnp.where(live_mask, scores, (1 << 20) * CAP + tile_index[None, :])
    ranking = jnp.argsort(jnp.argsort(scores, axis=1, stable=True), axis=1, stable=True).astype(jnp.int32)
    global_pos = (starts[:, None] + ranking + offset) % total
    placed_device = device_order[global_pos // PEER % N_DOM]
    placed_slot = global_pos // (N_DOM * PEER) * PEER + global_pos % PEER
    destination = jnp.where(live_mask, placed_device * LAND + placed_slot, -1).astype(jnp.int32)
    return (counts, destination.reshape(N_DOM * CAP))


def draw_counts(key, part):
    return placement_plan(key)[0]


def draw_destination(key, part):
    return placement_plan(key)[1]


def draw_points(key, part):
    slice_keys = jax.random.split(jax.random.fold_in(key, 11), 2)
    noise = jax.random.normal(slice_keys[0], (N_DOM * CAP, TILE, MODEL_WIDTH), jnp.float32)
    region = 0.8 * jax.random.normal(slice_keys[1], (N_DOM * CAP, 1, MODEL_WIDTH), jnp.float32)
    values = noise + region
    return values.reshape(N_DOM * CAP * TILE, MODEL_WIDTH).astype(jnp.bfloat16)


def normal_values(own_key, shape, deviation, reach, kind=jnp.bfloat16):
    return jnp.clip(deviation * jax.random.normal(own_key, shape, jnp.float32), -reach, reach).astype(kind)


def setup_inputs(seed: int = 0, part: int = 0) -> dict:
    keys = jax.random.split(jax.random.key(seed), 11)
    part_keys = jax.random.split(jax.random.fold_in(keys[10], part), 11)
    points = draw_points(jax.random.fold_in(jax.random.fold_in(keys[10], part), 71), part)
    counts = draw_counts(jax.random.fold_in(jax.random.fold_in(keys[10], part), 71), part)
    destination = draw_destination(jax.random.fold_in(jax.random.fold_in(keys[10], part), 71), part)
    proj_weight = normal_values(keys[3], (MODEL_WIDTH, MODEL_WIDTH), MODEL_WIDTH ** -0.5, 0.375)
    proj_bias = normal_values(keys[4], (MODEL_WIDTH,), 0.5, 3.0, jnp.float32)
    slice_weight = normal_values(keys[5], (HEAD_FEATURES, PARTITION_TALLY), HEAD_FEATURES ** -0.5, 1.0)
    softness_matrix = normal_values(keys[6], (HEAD_FEATURES,), HEAD_FEATURES ** -0.5, 1.0)
    token_qkv_weight = normal_values(keys[7], (3, HEAD_FEATURES, HEAD_FEATURES), HEAD_FEATURES ** -0.5, 1.0, jnp.float32)
    out_weight = normal_values(keys[8], (MODEL_WIDTH, MODEL_WIDTH), MODEL_WIDTH ** -0.5, 0.375)
    out_bias = normal_values(keys[9], (MODEL_WIDTH,), 0.3, 2.0, jnp.float32)
    return dict(points=points, counts=counts, destination=destination, proj_weight=proj_weight, proj_bias=proj_bias, slice_weight=slice_weight, softness_matrix=softness_matrix, token_qkv_weight=token_qkv_weight, out_weight=out_weight, out_bias=out_bias)


def normalize(values):
    widened = values.astype(jnp.float32)
    centred = widened - lax.optimization_barrier(jnp.mean(widened, axis=-1, keepdims=True))
    spread = lax.optimization_barrier(jnp.mean(centred * centred, axis=-1, keepdims=True))
    return (centred * lax.rsqrt(spread + 1e-05)).astype(jnp.bfloat16)

def encode(values, proj_weight, proj_bias, slice_weight, softness_matrix):
    tally_per_line = values.shape[0]
    normed = normalize(values)
    mapped_surface_vectors = (jnp.dot(normed, proj_weight, preferred_element_type=jnp.float32) + proj_bias).astype(jnp.bfloat16)
    slice_full = jnp.kron(jnp.eye(FOCUS_GROUPS, dtype=jnp.float32), slice_weight.astype(jnp.float32)).astype(jnp.bfloat16)
    softness_broadcast = jnp.kron(jnp.eye(FOCUS_GROUPS, dtype=jnp.float32), softness_matrix.astype(jnp.float32)[:, None]).astype(jnp.bfloat16)
    partition_logits = jnp.dot(mapped_surface_vectors, slice_full, preferred_element_type=jnp.float32)
    partition_softness = 0.5 + jax.nn.softplus(jnp.dot(mapped_surface_vectors, softness_broadcast, preferred_element_type=jnp.float32))
    tempered_logits = partition_logits.reshape(tally_per_line, FOCUS_GROUPS, PARTITION_TALLY) / partition_softness[:, :, None]
    raised = jnp.exp(tempered_logits)
    slice_assignment = (raised / lax.optimization_barrier(jnp.sum(raised, axis=-1, keepdims=True))).reshape(tally_per_line, FOCUS_GROUPS * PARTITION_TALLY)
    return (mapped_surface_vectors, slice_assignment.astype(jnp.bfloat16))

def partial_sums(mapped_surface_vectors, slice_assignment, live_mask):
    tally_per_line = mapped_surface_vectors.shape[0]
    masked_scores = slice_assignment * live_mask[:, None]
    numerator_sums = jnp.einsum('lzi,lzt->zit', masked_scores.reshape(tally_per_line, FOCUS_GROUPS, PARTITION_TALLY).astype(jnp.float32), mapped_surface_vectors.reshape(tally_per_line, FOCUS_GROUPS, HEAD_FEATURES).astype(jnp.float32))
    denom = lax.optimization_barrier(jnp.sum(masked_scores.astype(jnp.float32), axis=0))
    return (numerator_sums, denom)

def mix_slices(numerator_sums, denom, token_qkv_weight):
    slice_tokens = numerator_sums / (denom.reshape(FOCUS_GROUPS, PARTITION_TALLY)[:, :, None] + 1e-05)
    highest_precision = lax.Precision.HIGHEST
    slice_query = jnp.einsum('ijt,tk->ijk', slice_tokens, token_qkv_weight[0], precision=highest_precision)
    slice_keys = jnp.einsum('ijt,tk->ijk', slice_tokens, token_qkv_weight[1], precision=highest_precision)
    slice_values = jnp.einsum('ijt,tk->ijk', slice_tokens, token_qkv_weight[2], precision=highest_precision)
    scores = jnp.einsum('hme,hne->hmn', slice_query, slice_keys, precision=highest_precision) * HEAD_FEATURES ** (-0.5)
    raised = jnp.exp(scores)
    attend = raised / lax.optimization_barrier(jnp.sum(raised, axis=-1, keepdims=True))
    return jnp.einsum('hmn,hne->hme', attend, slice_values, precision=highest_precision).astype(jnp.bfloat16)

def decode(slice_assignment, mixed_tokens, out_weight, out_bias):
    tally_per_line = slice_assignment.shape[0]
    unslice_tokens = jnp.einsum('sxw,xwk->sxk', slice_assignment.reshape(tally_per_line, FOCUS_GROUPS, PARTITION_TALLY).astype(jnp.float32), mixed_tokens.astype(jnp.float32)).reshape(tally_per_line, MODEL_WIDTH).astype(jnp.bfloat16)
    return (jnp.dot(unslice_tokens, out_weight, preferred_element_type=jnp.float32) + out_bias).astype(jnp.bfloat16)

def reference(points, counts, destination, proj_weight, proj_bias, slice_weight, softness_matrix, token_qkv_weight, out_weight, out_bias):
    grouped = points.reshape(N_DOM, CAP * TILE, MODEL_WIDTH)
    row_tiles = jnp.arange(CAP * TILE, dtype=jnp.int32) // TILE
    live_all = (row_tiles[None, :] < counts[:, None]).astype(jnp.bfloat16)

    def gather_stats(pair):
        block, live_mask = pair
        mapped_surface_vectors, slice_assignment = encode(block, proj_weight, proj_bias, slice_weight, softness_matrix)
        return partial_sums(mapped_surface_vectors, slice_assignment, live_mask)
    numer_all, denom_all = lax.map(gather_stats, (grouped, live_all))
    mixed_tokens = mix_slices(lax.optimization_barrier(jnp.sum(numer_all, axis=0)), lax.optimization_barrier(jnp.sum(denom_all, axis=0)), token_qkv_weight)

    def finish(block):
        mapped_surface_vectors, slice_assignment = encode(block, proj_weight, proj_bias, slice_weight, softness_matrix)
        return decode(slice_assignment, mixed_tokens, out_weight, out_bias)
    outputs = lax.map(finish, grouped).reshape(N_DOM * CAP, TILE, MODEL_WIDTH)
    target = jnp.where(destination >= 0, destination, N_DOM * LAND).astype(jnp.int32)
    landed = jnp.zeros((N_DOM * LAND + 1, TILE, MODEL_WIDTH), outputs.dtype).at[target].set(outputs)
    return landed[:N_DOM * LAND].reshape(N_DOM * LAND * TILE, MODEL_WIDTH)
```

```python
import functools

import jax
import jax.numpy as jnp
from jax import lax
from jax.experimental import pallas as pl
from jax.experimental.pallas import tpu as pltpu
from jax.sharding import PartitionSpec as P

WIDTH = 256
HEADS = 8
FEAT = 32
TILE = 128
LAND = 80
HALF = 128
PLANE = 4
LINE = 4
CHUNK = 5
STEP = 2
HOP = 2
RING = 4
LIMITS = (104, 112, 120)
ROOM = LIMITS[-1]
ENCODE_ORDER = (0, 2, 3, 1)
PLANE_DUE = {0: (4, 0), 1: (4, 4), 2: (5, 4), 3: (5, 7)}
DEST_ORDER = ((3, 2, 1, 0), (3, 2, 0, 1), (0, 1, 3, 2), (0, 1, 2, 3))
LANES = (
    ((0, 0, 3), (0, 0, 2), (0, 1, 3), (0, 2, 3), (0, 3, 3), (0, 1, 2), (0, 3, 2), (0, 1, 1), (0, 2, 2), (0, 0, 1), (0, 2, 1), (0, 3, 1)),
    ((1, 0, 3), (0, 0, 3), (1, 1, 3), (1, 2, 3), (0, 0, 2), (1, 3, 3), (0, 1, 3), (0, 3, 3), (0, 2, 3), (0, 1, 2), (1, 3, 2), (1, 2, 2), (0, 3, 2), (1, 0, 2), (1, 1, 2), (0, 2, 2)),
    ((0, 0, 3), (1, 1, 3), (1, 0, 3), (1, 2, 3), (1, 3, 3), (2, 0, 3), (0, 1, 3), (2, 1, 3), (2, 2, 3), (0, 2, 3), (2, 3, 3), (0, 3, 3)),
)
MESH = pl.DeviceIdType.MESH
HIGHEST = lax.Precision.HIGHEST
F32 = jnp.float32
BF16 = jnp.bfloat16


def split(x):
    high = x.astype(BF16)
    return high, x - high.astype(F32)


def encode_rows(x, wp, bp, ws, wt, spread_ones, ones):
    x = x.astype(F32)
    centred = x - jnp.sum(x, axis=-1, keepdims=True) * (1.0 / WIDTH)
    spread = jnp.sum(centred * centred, axis=-1, keepdims=True) * (1.0 / WIDTH)
    normed = (centred * lax.rsqrt(spread + 1e-05)).astype(BF16)
    dot = functools.partial(jnp.dot, preferred_element_type=F32)
    proj = (dot(normed, wp) + bp).astype(BF16)
    logits = dot(proj, ws)
    soft = dot(proj, wt)
    temper = 0.5 + (jnp.maximum(soft, 0.0) + jnp.log1p(jnp.exp(-jnp.abs(soft))))
    first, rest = split(1.0 / temper)
    second, rest = split(rest)
    scale = dot(first, spread_ones) + (dot(second, spread_ones) + dot(rest.astype(BF16), spread_ones))
    raised = jnp.exp(logits * scale)
    first, rest = split(raised)
    total = dot(first, ones) + dot(rest.astype(BF16), ones)
    return proj, (raised / total).astype(BF16)


def diagonal(block, times):
    wide = jnp.concatenate([block] * times, axis=1)
    full = jnp.concatenate([wide] * times, axis=0)
    size = times * FEAT
    row = lax.broadcasted_iota(jnp.int32, (size, size), 0) // FEAT
    lane = lax.broadcasted_iota(jnp.int32, (size, size), 1) // FEAT
    return jnp.where(row == lane, full, 0.0)


def build(slice_weight, softness, qkv_small, ws, wt, spread_ones, ones, head_ones, qkv):
    ws[...] = diagonal(slice_weight[...].astype(F32), HEADS).astype(BF16)
    for i in range(3):
        qkv[i] = diagonal(qkv_small[i], 4)
    unity = jnp.ones((FEAT, FEAT), F32)
    ones[...] = diagonal(unity, HEADS).astype(BF16)
    head_ones[...] = diagonal(unity, 4)
    row = lax.broadcasted_iota(jnp.int32, (HALF, WIDTH), 0)
    lane = lax.broadcasted_iota(jnp.int32, (HALF, WIDTH), 1) // FEAT
    spread_ones[...] = jnp.where(row == lane, 1.0, 0.0).astype(BF16)
    flat = jnp.concatenate([softness[...].astype(F32)] * 4, axis=1)
    tall = jnp.transpose(jnp.broadcast_to(flat, (HALF, HALF)))
    tall = jnp.concatenate([tall, tall], axis=0)
    row = lax.broadcasted_iota(jnp.int32, (WIDTH, HALF), 0) // FEAT
    lane = lax.broadcasted_iota(jnp.int32, (WIDTH, HALF), 1)
    wt[...] = jnp.where(row == lane, tall, 0.0).astype(BF16)


def move_kernel(
    n, per_peer, unit, source, label, points, labels, wp, bp, slice_weight, softness, qkv_small,
    wo, bo, result, labels_out,
    held_points, sending, arrived, numer, denom, sums, inbox, mixed,
    ws, wt, spread_ones, ones, head_ones, qkv,
    point_sem, send_sem, recv_sem, lab_send, lab_recv, own_sem, out_sem, red_send, red_recv,
):
    me = lax.axis_index("dom")
    pieces = per_peer // unit
    rows = unit * TILE
    fetch = pltpu.make_async_copy(points, held_points, point_sem)
    fetch.start()

    def partner(x):
        peer, bit = 0, 1
        while bit < n:
            mine, flip = me // bit % 2, x // bit % 2
            peer = peer + bit * (mine + flip - 2 * mine * flip)
            bit = bit * 2
        return peer

    barrier = pltpu.get_barrier_semaphore()
    for x in range(1, n):
        pl.semaphore_signal(barrier, inc=1, device_id={"dom": partner(x)}, device_id_type=MESH)
    numer[...] = jnp.zeros_like(numer)
    denom[...] = jnp.zeros_like(denom)
    build(slice_weight, softness, qkv_small, ws, wt, spread_ones, ones, head_ones, qkv)
    pl.semaphore_wait(barrier, n - 1)

    def order(i):
        quarter = n // 4
        near = lax.rem(i, 2) * 2 * quarter
        early = 3 * quarter + i // 2 - near
        late = jnp.where(i < 3 * quarter, i, n - 1 - i)
        return jnp.where(i < 2 * quarter, early, late)

    def lab_copy(x):
        peer = partner(x)
        return pltpu.make_async_remote_copy(
            src_ref=labels.at[peer], dst_ref=labels_out.at[me], send_sem=lab_send.at[x],
            recv_sem=lab_recv.at[x], device_id={"dom": peer}, device_id_type=MESH,
        )

    def piece_copy(x, s):
        at = pl.ds(pl.multiple_of(s * rows, rows), rows)
        return pltpu.make_async_remote_copy(
            src_ref=sending.at[x, at], dst_ref=arrived.at[x, at], send_sem=send_sem.at[x, s],
            recv_sem=recv_sem.at[x, s], device_id={"dom": partner(x)}, device_id_type=MESH,
        )

    def lab_start(x, _):
        lab_copy(x).start()
        return 0

    lax.fori_loop(1, n, lab_start, 0)
    own_lab = pltpu.make_async_copy(labels.at[me], labels_out.at[me], own_sem)
    own_lab.start()
    fetch.wait()

    def compute(x, peer, s):
        first = peer * per_peer + s * unit
        tiles = jnp.concatenate([held_points[source[first + j]] for j in range(unit)], axis=0)
        proj, weights = encode_rows(
            tiles, wp[...], bp[...], ws[...], wt[...], spread_ones[...], ones[...]
        )
        live = jnp.concatenate(
            [jnp.full((TILE, WIDTH), label[first + j], jnp.int32) for j in range(unit)], axis=0
        ) >= 0
        kept = jnp.where(live, weights.astype(F32), 0.0)
        weights = kept.astype(BF16)
        sending[x, pl.ds(pl.multiple_of(s * rows, rows), rows), :] = weights
        numer[...] += lax.dot_general(
            weights, proj, (((0,), (0,)), ((), ())), preferred_element_type=F32
        )
        denom[...] += jnp.sum(kept.reshape(rows // 8, 8, WIDTH), axis=0)

    steps = (n - 1) * pieces
    held_from = (n - 1) * (pieces - 1)

    def encode_step(i, _):
        x = order(i % (n - 1))
        compute(x, partner(x), i // (n - 1))

        @pl.when((i > 0) & (i <= held_from))
        def _():
            piece_copy(order((i - 1) % (n - 1)), (i - 1) // (n - 1)).start()

        return 0

    lax.fori_loop(0, steps, encode_step, 0)

    def own_step(s, _):
        compute(0, me, s)
        return 0

    lax.fori_loop(0, pieces, own_step, 0)

    lane_head = lax.broadcasted_iota(jnp.int32, (FEAT, HALF), 1) // FEAT
    for a in range(2):
        acc = jnp.zeros((FEAT, HALF), F32)
        for j in range(4):
            part = numer[pl.ds((a * 4 + j) * FEAT, FEAT), pl.ds(a * HALF, HALF)]
            acc = acc + jnp.where(lane_head == j, part, 0.0)
        sums[0, pl.ds(a * FEAT, FEAT), :] = acc
        total = jnp.sum(denom[:, pl.ds(a * HALF, HALF)], axis=0, keepdims=True)
        sums[0, pl.ds(2 * FEAT + a * 8, 8), :] = jnp.broadcast_to(total, (8, HALF))

    def release(i, _):
        piece_copy(order(i - held_from), pieces - 1).start()
        return 0

    level, bit = 0, n // 2
    while bit > 0:
        swap = pltpu.make_async_remote_copy(
            src_ref=sums.at[level], dst_ref=inbox.at[level], send_sem=red_send.at[level],
            recv_sem=red_recv.at[level], device_id={"dom": partner(bit)}, device_id_type=MESH,
        )
        swap.start()
        swap.wait()
        sums[level + 1] = sums[level] + inbox[level]
        level, bit = level + 1, bit // 2
        if level == max(1, (n - 1).bit_length() - 2):
            lax.fori_loop(held_from, steps, release, 0)
    mixed[...] = mix(sums[level], qkv, head_ones[...])

    def out_copy(x, s):
        at = pl.ds(pl.multiple_of(s * rows, rows), rows)
        return pltpu.make_async_copy(arrived.at[x, at], result.at[partner(x), at], out_sem.at[x, s])

    def decode(read, x, s):
        at = pl.ds(pl.multiple_of(s * rows, rows), rows)
        deslice = jnp.dot(read[x, at, :], mixed[...], preferred_element_type=F32).astype(BF16)
        y = (jnp.dot(deslice, wo[...], preferred_element_type=F32) + bo[...]).astype(BF16)
        arrived[x, at, :] = y
        out_copy(x, s).start()

    def decode_own(s, _):
        decode(sending, 0, s)
        return 0

    lax.fori_loop(0, pieces, decode_own, 0)

    def from_peer(i, _):
        x, s = order(i % (n - 1)), i // (n - 1)
        piece_copy(x, s).wait_recv()
        decode(arrived, x, s)
        return 0

    lax.fori_loop(0, steps, from_peer, 0)

    def finish(x, _):
        def one(s, _):
            piece_copy(x, s).wait_send()
            return 0

        lax.fori_loop(0, pieces, one, 0)
        lab_copy(x).wait()
        return 0

    lax.fori_loop(1, n, finish, 0)
    own_lab.wait()

    def drain(i, _):
        out_copy(i // pieces, i % pieces).wait()
        return 0

    lax.fori_loop(0, n * pieces, drain, 0)


def mix(stats, qkv, ones):
    row_head = lax.broadcasted_iota(jnp.int32, (HALF, HALF), 0) // FEAT
    lane_head = lax.broadcasted_iota(jnp.int32, (HALF, HALF), 1) // FEAT
    same = row_head == lane_head
    blocks = []
    for a in range(2):
        numer = stats[a * FEAT:(a + 1) * FEAT, :]
        row = stats[2 * FEAT + a * 8:2 * FEAT + (a + 1) * 8, :]
        col = jnp.transpose(jnp.broadcast_to(row[:1], (HALF, HALF)))
        spread = jnp.zeros((FEAT, HALF), F32)
        for j in range(4):
            spread = spread + jnp.where(
                lane_head[:FEAT] == j, col[j * FEAT:(j + 1) * FEAT, :], 0.0
            )
        tokens = numer / (spread + 1e-05)
        dot = functools.partial(jnp.dot, preferred_element_type=F32, precision=HIGHEST)
        query, keys, values = (dot(tokens, qkv[i]) for i in range(3))
        spread_keys = jnp.where(same, jnp.concatenate([keys] * 4, axis=0), 0.0)
        scores = lax.dot_general(
            query, spread_keys, (((1,), (1,)), ((), ())), preferred_element_type=F32, precision=HIGHEST
        ) * FEAT ** (-0.5)
        raised = jnp.exp(scores)
        attend = raised / dot(raised, ones)
        spread_values = jnp.where(same, jnp.concatenate([values] * 4, axis=0), 0.0)
        mixed = dot(attend, spread_values)
        blocks.append(jnp.where(same, jnp.concatenate([mixed] * 4, axis=0), 0.0))
    nil = jnp.zeros((HALF, HALF), F32)
    return jnp.concatenate(
        [jnp.concatenate([blocks[0], nil], axis=1), jnp.concatenate([nil, blocks[1]], axis=1)], axis=0
    ).astype(BF16)


def place_kernel(n, per_peer, chunks, per_chunk, labels, tiles, out, held, in_sem, out_sem):
    def load(k, _):
        def one(t, _):
            slot = labels[k, t]

            @pl.when(slot >= 0)
            def _():
                pltpu.make_async_copy(
                    tiles.at[k * per_peer + t], held.at[slot], in_sem.at[slot // per_chunk]
                ).start()

            return 0

        return lax.fori_loop(0, per_peer, one, 0)

    lax.fori_loop(0, n, load, 0)

    def step(c, _):
        part = pl.ds(c * per_chunk, per_chunk)
        pltpu.make_async_copy(tiles.at[pl.ds(0, per_chunk)], held.at[part], in_sem.at[c]).wait()
        pltpu.make_async_copy(held.at[part], out.at[part], out_sem.at[c]).start()
        return 0

    lax.fori_loop(0, chunks, step, 0)

    def finish(c, _):
        part = pl.ds(c * per_chunk, per_chunk)
        pltpu.make_async_copy(held.at[part], out.at[part], out_sem.at[c]).wait()
        return 0

    lax.fori_loop(0, chunks, finish, 0)


def plan(destination, own_count, n):
    slots = destination.shape[0]
    per_peer = slots // n
    index = jnp.arange(slots, dtype=jnp.int32)
    live = index < own_count
    target = jnp.where(live, destination // LAND, -1)
    slot = jnp.where(live, destination % LAND, -1)
    earlier = (target[:, None] == target[None, :]) & live[None, :] & (index[None, :] < index[:, None])
    rank = jnp.sum(earlier.astype(jnp.int32), axis=1)
    place = target * per_peer + rank
    matches = live[None, :] & (place[None, :] == index[:, None])
    source = jnp.sum(jnp.where(matches, index[None, :], 0), axis=1)
    label = jnp.sum(jnp.where(matches, slot[None, :] + 1, 0), axis=1) - 1
    return source, label


def direct(n, points, counts, destination, wp, bp, slice_weight, softness, qkv, wo, bo):
    slots = points.shape[0] // TILE
    per_peer = slots // n
    any_spec = pl.BlockSpec(memory_space=pl.ANY)
    vmem = pl.BlockSpec(memory_space=pltpu.VMEM)
    smem = pl.BlockSpec(memory_space=pltpu.SMEM)
    source, label = plan(destination, counts[0], n)
    rows = per_peer * TILE
    labels = jnp.pad(label.reshape(n, 1, per_peer), ((0, 0), (0, 0), (0, HALF - per_peer)))
    unit = 2 if per_peer % 2 == 0 else 1
    pieces = per_peer // unit
    levels = (n - 1).bit_length()
    stat_rows = 2 * FEAT + 16
    dma = pltpu.SemaphoreType.DMA
    tiles, arrived_lab = pl.pallas_call(
        functools.partial(move_kernel, n, per_peer, unit),
        out_shape=(
            jax.ShapeDtypeStruct((n, rows, WIDTH), BF16),
            jax.ShapeDtypeStruct((n, 1, HALF), jnp.int32),
        ),
        in_specs=[smem, smem, any_spec, any_spec] + [vmem] * 7,
        out_specs=(any_spec, any_spec),
        scratch_shapes=[
            pltpu.VMEM((slots, TILE, WIDTH), BF16),
            pltpu.VMEM((n, rows, WIDTH), BF16),
            pltpu.VMEM((n, rows, WIDTH), BF16),
            pltpu.VMEM((WIDTH, WIDTH), F32),
            pltpu.VMEM((8, WIDTH), F32),
            pltpu.VMEM((levels + 1, stat_rows, HALF), F32),
            pltpu.VMEM((levels, stat_rows, HALF), F32),
            pltpu.VMEM((WIDTH, WIDTH), BF16),
            pltpu.VMEM((WIDTH, WIDTH), BF16),
            pltpu.VMEM((WIDTH, HALF), BF16),
            pltpu.VMEM((HALF, WIDTH), BF16),
            pltpu.VMEM((WIDTH, WIDTH), BF16),
            pltpu.VMEM((HALF, HALF), F32),
            pltpu.VMEM((3, HALF, HALF), F32),
            dma, dma((n, pieces)), dma((n, pieces)), dma((n,)), dma((n,)), dma, dma((n, pieces)),
            dma((levels,)), dma((levels,)),
        ],
        compiler_params=pltpu.CompilerParams(
            collective_id=9, has_side_effects=True, vmem_limit_bytes=60 << 20
        ),
        name="move",
    )(
        source, label, points.reshape(slots, TILE, WIDTH), labels, wp, bp.reshape(1, WIDTH),
        slice_weight, softness.reshape(1, FEAT), qkv, wo, bo.reshape(1, WIDTH),
    )

    per_chunk = 8
    chunks = LAND // per_chunk
    placed = pl.pallas_call(
        functools.partial(place_kernel, n, per_peer, chunks, per_chunk),
        out_shape=jax.ShapeDtypeStruct((LAND, TILE, WIDTH), BF16),
        grid_spec=pltpu.PrefetchScalarGridSpec(
            num_scalar_prefetch=1, grid=(), in_specs=[any_spec], out_specs=any_spec,
            scratch_shapes=[pltpu.VMEM((LAND, TILE, WIDTH), BF16), dma((chunks,)), dma((chunks,))],
        ),
        compiler_params=pltpu.CompilerParams(vmem_limit_bytes=60 << 20),
        name="place",
    )(arrived_lab.reshape(n, HALF), tiles.reshape(slots, TILE, WIDTH))
    return placed.reshape(LAND * TILE, WIDTH)


def partner(me, x, n):
    peer, bit = 0, 1
    while bit < n:
        mine, flip = me // bit % 2, x // bit % 2
        peer = peer + bit * (mine + flip - 2 * mine * flip)
        bit = bit * 2
    return peer


def tell_kernel(n, groups, rows, got, send_sem, recv_sem, own_sem):
    me, group = lax.axis_index("dom"), lax.axis_index("groups")
    mine = me // PLANE * PLANE
    barrier = pltpu.get_barrier_semaphore()

    def place(x):
        return x // n, x % n

    def signal(x, _):
        g, y = place(x)
        pl.semaphore_signal(
            barrier, inc=1, device_id={"groups": (group + g) % groups, "dom": partner(me, y, n)},
            device_id_type=MESH,
        )
        return 0

    lax.fori_loop(1, n * groups, signal, 0)
    own = pltpu.make_async_copy(rows.at[0], got.at[mine], own_sem)
    own.start()
    pl.semaphore_wait(barrier, n * groups - 1)

    def tell(x):
        g, y = place(x)
        w = y % PLANE
        return pltpu.make_async_remote_copy(
            src_ref=rows.at[w], dst_ref=got.at[g * n + mine + w], send_sem=send_sem.at[x],
            recv_sem=recv_sem.at[x], device_id={"groups": (group + g) % groups, "dom": partner(me, y, n)},
            device_id_type=MESH,
        )

    def start(x, _):
        tell(x).start()
        return 0

    def finish(x, _):
        tell(x).wait()
        return 0

    lax.fori_loop(1, n * groups, start, 0)
    lax.fori_loop(1, n * groups, finish, 0)
    own.wait()


def table_kernel(n, groups, per_peer, got, sends, slots, branch, starts):
    z = lax.axis_index("dom") // PLANE
    flow = LINE * per_peer
    table = ROOM + per_peer

    def clear(i, _):
        sends[0, i] = 0
        sends[1, i] = 0
        return 0

    lax.fori_loop(0, table, clear, 0)

    def schedule(g, column, keep):
        longest = jnp.int32(0)
        for way in range(2):
            def plane(p):
                return LINE - 1 - p if way else p

            def count(cl):
                zo, w, zd = plane(cl[0]), cl[1], plane(cl[2])
                return got[g * n + zo * PLANE + (column ^ w), flow + w * LINE + zd]

            before = {}
            for lane, order in enumerate(LANES):
                first = {}
                for w in range(PLANE):
                    total = jnp.int32(0)
                    for real in DEST_ORDER[plane(lane)]:
                        cl = (lane, w, plane(real))
                        first[cl] = total
                        total = total + count(cl)
                pos, now = jnp.int32(0), {}
                for at, cl in enumerate(order):
                    size = count(cl)
                    if cl[0] == lane:
                        begin = first[cl]
                        last = ((begin + size - 1) * 13) >> 6
                        slope, offset = PLANE_DUE[cl[1]]
                        ready = STEP * (slope * last + offset) - jnp.maximum(0, CHUNK * last - begin)
                    else:
                        ready = before[cl] + HOP * STEP
                    start = jnp.where(size > 0, jnp.maximum(pos, ready), pos)
                    now[cl] = start
                    if keep:
                        starts[way, lane, at] = start
                    pos = start + size
                before = now
                longest = jnp.maximum(longest, pos)
        return longest

    longest = schedule(0, 0, True)

    def others(i, most):
        return jnp.maximum(most, schedule(i // PLANE, i % PLANE, False))

    longest = lax.fori_loop(1, groups * PLANE, others, longest)
    choice = jnp.int32(0)
    for limit in LIMITS:
        choice = choice + jnp.where(longest > limit, 1, 0)
    branch[0] = choice

    def fill(me):
        def row(zo, w):
            return zo * PLANE + w

        def size_of(zo, w, zd):
            return got[row(zo, w), flow + w * LINE + zd]

        def first_of(zo, w, zd):
            total = jnp.int32(0)
            for real in DEST_ORDER[zo]:
                if real == zd:
                    return total
                total = total + size_of(zo, w, real)

        for way in range(2):
            def plane(p):
                return LINE - 1 - p if way else p

            lane = plane(me)
            if lane == LINE - 1:
                continue
            landed = PLANE * flow + way * ROOM
            for at, cl in enumerate(LANES[lane]):
                zo, w, zd = plane(cl[0]), cl[1], plane(cl[2])
                if zo == me:
                    source = w * flow + first_of(zo, w, zd)
                else:
                    source = landed + starts[way, lane - 1, LANES[lane - 1].index(cl)]
                size = size_of(zo, w, zd)
                start = jnp.minimum(starts[way, lane, at], ROOM)
                for k in range(per_peer):
                    sends[way, start + k] = jnp.where(k < size, source + k, 0)
        for zo in range(LINE):
            for w in range(PLANE):
                first = first_of(zo, w, me)
                size = size_of(zo, w, me)
                if zo == me:
                    source = w * flow + first
                else:
                    way = 0 if zo < me else 1
                    lane = me - 1 if zo < me else LINE - 2 - me
                    cl = (zo, w, me) if zo < me else (LINE - 1 - zo, w, LINE - 1 - me)
                    source = PLANE * flow + way * ROOM + starts[way, lane, LANES[lane].index(cl)]
                for k in range(per_peer):
                    label = got[row(zo, w), first + k]
                    slots[jnp.where(k < size, label + 1, 0)] = source + k

    for me in range(LINE):
        @pl.when(z == me)
        def _():
            fill(me)


def relay_kernel(
    n, per_peer, limit, source, label, sends, slots, points, wp, bp, slice_weight, softness, qkv_small,
    wo, bo, result,
    held, pool, sending, landed, stage, landing, numer, denom, sums, inbox, mixed,
    ws, wt, spread_ones, ones, head_ones, qkv,
    point_sem, plane_send, plane_recv, line_send, line_recv, red_send, red_recv, out_sem,
):
    me = lax.axis_index("dom")
    z = me // PLANE
    flow = LINE * per_peer
    chunks = flow // CHUNK
    rounds = limit // STEP
    fetch = pltpu.make_async_copy(points, held, point_sem)
    fetch.start()
    barrier = pltpu.get_barrier_semaphore()
    for x in range(1, n):
        pl.semaphore_signal(barrier, inc=1, device_id={"dom": partner(me, x, n)}, device_id_type=MESH)
    numer[...] = jnp.zeros_like(numer)
    denom[...] = jnp.zeros_like(denom)
    build(slice_weight, softness, qkv_small, ws, wt, spread_ones, ones, head_ones, qkv)
    pl.semaphore_wait(barrier, n - 1)
    fetch.wait()

    def plane_copy(w, j):
        return pltpu.make_async_remote_copy(
            src_ref=sending.at[w, j % RING], dst_ref=landed.at[w, j], send_sem=plane_send.at[w, j],
            recv_sem=plane_recv.at[w, j], device_id={"dom": partner(me, w, PLANE) + z * PLANE},
            device_id_type=MESH,
        )

    def line_copy(way, r):
        slot = r % RING
        peer = me + PLANE if way == 0 else me - PLANE
        return pltpu.make_async_remote_copy(
            src_ref=stage.at[way, slot], dst_ref=landing.at[way, slot], send_sem=line_send.at[way, slot],
            recv_sem=line_recv.at[way, slot], device_id={"dom": peer}, device_id_type=MESH,
        )

    can_send = (z < LINE - 1, z > 0)
    can_recv = (z > 0, z < LINE - 1)

    def encode(r):
        j, turn = r // PLANE, r % PLANE
        w = jnp.where(turn == 0, 0, jnp.where(turn == 3, 1, turn + 1))
        first = w * flow + j * CHUNK
        tiles = jnp.concatenate([held[source[first + k]] for k in range(CHUNK)], axis=0)
        proj, weights = encode_rows(
            tiles, wp[...], bp[...], ws[...], wt[...], spread_ones[...], ones[...]
        )
        live = jnp.concatenate(
            [jnp.full((TILE, WIDTH), label[first + k], jnp.int32) for k in range(CHUNK)], axis=0
        ) >= 0
        kept = jnp.where(live, weights.astype(F32), 0.0)
        weights = kept.astype(BF16)
        numer[...] += lax.dot_general(
            weights, proj, (((0,), (0,)), ((), ())), preferred_element_type=F32
        )
        denom[...] += jnp.sum(kept.reshape(CHUNK * TILE // 8, 8, WIDTH), axis=0)
        weights = weights.reshape(CHUNK, TILE, WIDTH)

        @pl.when(turn == 0)
        def _():
            pool[pl.ds(j * CHUNK, CHUNK)] = weights

        @pl.when(turn > 0)
        def _():
            @pl.when(j >= RING)
            def _():
                plane_copy(w, j - RING).wait_send()

            sending[w, j % RING] = weights
            plane_copy(w, j).start()

    def line_arrive(way, m):
        line_copy(way, m).wait_recv()
        pool[pl.ds(PLANE * flow + way * ROOM + m * STEP, STEP)] = landing[way, m % RING]

    def relay(r):
        for way in range(2):
            @pl.when(can_recv[way] & (r >= HOP))
            def _():
                line_arrive(way, r - HOP)
        for w in range(1, PLANE):
            slope, offset = PLANE_DUE[w]
            since = r - offset

            @pl.when((since >= 0) & (since < slope * chunks))
            def _():
                @pl.when(since % slope == 0)
                def _():
                    j = since // slope
                    plane_copy(w, j).wait_recv()
                    pool[pl.ds(w * flow + j * CHUNK, CHUNK)] = landed[w, j]
        for way in range(2):
            @pl.when(can_send[way])
            def _():
                @pl.when(r >= RING)
                def _():
                    line_copy(way, r - RING).wait_send()

                for k in range(STEP):
                    stage[way, r % RING, k] = pool[sends[way, r * STEP + k]]
                line_copy(way, r).start()

    def first_rounds(r, _):
        encode(r)
        relay(r)
        return 0

    def more_rounds(r, _):
        relay(r)
        return 0

    reached = PLANE * chunks
    lax.fori_loop(0, reached, first_rounds, 0)

    lane_head = lax.broadcasted_iota(jnp.int32, (FEAT, HALF), 1) // FEAT
    for a in range(2):
        acc = jnp.zeros((FEAT, HALF), F32)
        for j in range(4):
            part = numer[pl.ds((a * 4 + j) * FEAT, FEAT), pl.ds(a * HALF, HALF)]
            acc = acc + jnp.where(lane_head == j, part, 0.0)
        sums[0, pl.ds(a * FEAT, FEAT), :] = acc
        total = jnp.sum(denom[:, pl.ds(a * HALF, HALF)], axis=0, keepdims=True)
        sums[0, pl.ds(2 * FEAT + a * 8, 8), :] = jnp.broadcast_to(total, (8, HALF))
    level, bit = 0, n // 2
    while bit > 0:
        swap = pltpu.make_async_remote_copy(
            src_ref=sums.at[level], dst_ref=inbox.at[level], send_sem=red_send.at[level],
            recv_sem=red_recv.at[level], device_id={"dom": partner(me, bit, n)}, device_id_type=MESH,
        )
        swap.start()
        lax.fori_loop(reached, reached + 4, more_rounds, 0)
        reached = reached + 4
        swap.wait()
        sums[level + 1] = sums[level] + inbox[level]
        level, bit = level + 1, bit // 2
    mixed[...] = mix(sums[level], qkv, head_ones[...])
    lax.fori_loop(reached, rounds, more_rounds, 0)

    for way in range(2):
        @pl.when(can_recv[way])
        def _():
            def arrive(m, _):
                line_arrive(way, m)
                return 0

            lax.fori_loop(rounds - HOP, rounds, arrive, 0)

    group = 8

    def out_copy(i):
        at = pl.ds(i * group, group)
        return pltpu.make_async_copy(held.at[at], result.at[at], out_sem.at[i])

    def decode(i, _):
        rows = jnp.concatenate([pool[slots[i * group + k + 1]] for k in range(group)], axis=0)
        deslice = jnp.dot(rows, mixed[...], preferred_element_type=F32).astype(BF16)
        y = (jnp.dot(deslice, wo[...], preferred_element_type=F32) + bo[...]).astype(BF16)
        held[pl.ds(i * group, group)] = y.reshape(group, TILE, WIDTH)
        out_copy(i).start()
        return 0

    lax.fori_loop(0, LAND // group, decode, 0)

    for way in range(2):
        @pl.when(can_send[way])
        def _():
            def sent(r, _):
                line_copy(way, r).wait_send()
                return 0

            lax.fori_loop(rounds - RING, rounds, sent, 0)

    def plane_sent(i, _):
        plane_copy(1 + i % (PLANE - 1), chunks - RING + i // (PLANE - 1)).wait_send()
        return 0

    lax.fori_loop(0, (PLANE - 1) * RING, plane_sent, 0)

    def drain(i, _):
        out_copy(i).wait()
        return 0

    lax.fori_loop(0, LAND // group, drain, 0)


def arrange(destination, own_count, n, me):
    slots = destination.shape[0]
    flow = slots // PLANE
    index = jnp.arange(slots, dtype=jnp.int32)
    live = index < own_count
    target, slot = destination // LAND, destination % LAND
    w = (target % PLANE) ^ (me % PLANE)
    line, own = target // PLANE, me // PLANE
    upper = own >= LINE // 2
    far = jnp.where(upper, LINE - 1 - line, line)
    near = jnp.where(upper, LINE - 1 - own, own)
    rank = jnp.where(
        far > near, LINE - 1 - far, jnp.where(far < near, LINE - 1 - near + far, LINE - 1)
    )
    w = jnp.where(live, w, -1)
    key = rank * slots + index
    earlier = (w[:, None] == w[None, :]) & (key[None, :] < key[:, None])
    place = w * flow + jnp.sum(earlier.astype(jnp.int32), axis=1)
    matches = live[None, :] & (place[None, :] == index[:, None])
    source = jnp.sum(jnp.where(matches, index[None, :], 0), axis=1)
    label = jnp.sum(jnp.where(matches, slot[None, :] + 1, 0), axis=1) - 1
    kind = jnp.where(live, w * LINE + line, -1)
    kinds = jnp.arange(PLANE * LINE, dtype=jnp.int32)
    sizes = jnp.sum((kind[None, :] == kinds[:, None]).astype(jnp.int32), axis=1)
    return source, label, sizes


def relayed(n, groups, points, counts, destination, wp, bp, slice_weight, softness, qkv, wo, bo):
    slots = points.shape[0] // TILE
    per_peer = slots // n
    flow = slots // PLANE
    any_spec = pl.BlockSpec(memory_space=pl.ANY)
    vmem = pl.BlockSpec(memory_space=pltpu.VMEM)
    smem = pl.BlockSpec(memory_space=pltpu.SMEM)
    dma = pltpu.SemaphoreType.DMA
    source, label, sizes = arrange(destination, counts[0], n, lax.axis_index("dom"))
    rows = jnp.concatenate(
        [label.reshape(PLANE, flow), jnp.broadcast_to(sizes[None], (PLANE, PLANE * LINE))], axis=1
    )
    rows = jnp.pad(rows, ((0, 0), (0, HALF - rows.shape[1]))).reshape(PLANE, 1, HALF)
    got = pl.pallas_call(
        functools.partial(tell_kernel, n, groups),
        out_shape=jax.ShapeDtypeStruct((groups * n, 1, HALF), jnp.int32),
        in_specs=[any_spec], out_specs=any_spec,
        scratch_shapes=[dma((n * groups,)), dma((n * groups,)), dma],
        compiler_params=pltpu.CompilerParams(collective_id=0, has_side_effects=True),
        name="tell",
    )(rows)
    sends, places, branch = pl.pallas_call(
        functools.partial(table_kernel, n, groups, per_peer),
        out_shape=(
            jax.ShapeDtypeStruct((2, ROOM + per_peer), jnp.int32),
            jax.ShapeDtypeStruct((LAND + 1,), jnp.int32),
            jax.ShapeDtypeStruct((1,), jnp.int32),
        ),
        in_specs=[smem], out_specs=(smem, smem, smem),
        scratch_shapes=[pltpu.SMEM((2, LINE - 1, PLANE * LINE), jnp.int32)],
        name="table",
    )(got.reshape(groups * n, HALF))

    levels = (n - 1).bit_length()
    stat_rows = 2 * FEAT + 16
    tile = (TILE, WIDTH)

    def relay(limit, at, *_):
        placed = pl.pallas_call(
            functools.partial(relay_kernel, n, per_peer, limit),
            out_shape=jax.ShapeDtypeStruct((LAND,) + tile, BF16),
            in_specs=[smem] * 4 + [any_spec] + [vmem] * 7,
            out_specs=any_spec,
            scratch_shapes=[
                pltpu.VMEM((slots,) + tile, BF16),
                pltpu.VMEM((slots + 2 * ROOM,) + tile, BF16),
                pltpu.VMEM((PLANE, RING, CHUNK) + tile, BF16),
                pltpu.VMEM((PLANE, flow // CHUNK, CHUNK) + tile, BF16),
                pltpu.VMEM((2, RING, STEP) + tile, BF16),
                pltpu.VMEM((2, RING, STEP) + tile, BF16),
                pltpu.VMEM((WIDTH, WIDTH), F32),
                pltpu.VMEM((8, WIDTH), F32),
                pltpu.VMEM((levels + 1, stat_rows, HALF), F32),
                pltpu.VMEM((levels, stat_rows, HALF), F32),
                pltpu.VMEM((WIDTH, WIDTH), BF16),
                pltpu.VMEM((WIDTH, WIDTH), BF16),
                pltpu.VMEM((WIDTH, HALF), BF16),
                pltpu.VMEM((HALF, WIDTH), BF16),
                pltpu.VMEM((WIDTH, WIDTH), BF16),
                pltpu.VMEM((HALF, HALF), F32),
                pltpu.VMEM((3, HALF, HALF), F32),
                dma, dma((PLANE, flow // CHUNK)), dma((PLANE, flow // CHUNK)),
                dma((2, RING)), dma((2, RING)), dma((levels,)), dma((levels,)), dma((LAND // 8,)),
            ],
            compiler_params=pltpu.CompilerParams(
                collective_id=1 + at, has_side_effects=True, vmem_limit_bytes=62 << 20
            ),
            name="relay" + str(limit),
        )(
            source, label, sends, places, points.reshape((slots,) + tile), wp, bp.reshape(1, WIDTH),
            slice_weight, softness.reshape(1, FEAT), qkv, wo, bo.reshape(1, WIDTH),
        )
        return placed.reshape(LAND * TILE, WIDTH)

    def fallback():
        return direct(n, points, counts, destination, wp, bp, slice_weight, softness, qkv, wo, bo)

    branches = [functools.partial(relay, limit, at) for at, limit in enumerate(LIMITS)]
    return lax.switch(branch[0], branches + [fallback])


def solution(mesh):
    spec = P(("groups", "dom"))
    wide = P(("groups", "dom"), None)
    n, groups = mesh.shape["dom"], mesh.shape["groups"]
    if n == PLANE * LINE and groups == 2:
        body = functools.partial(relayed, n, groups)
    else:
        body = functools.partial(direct, n)
    return jax.shard_map(
        body, mesh=mesh, in_specs=(wide, spec, spec) + (P(),) * 7, out_specs=wide, check_vma=False,
    )
```

```python
import functools

import jax
import jax.numpy as jnp
from jax import lax
from jax.experimental import pallas as pl
from jax.experimental.pallas import tpu as pltpu
from jax.sharding import PartitionSpec as P

WIDTH = 256
HEADS = 8
FEAT = 32
TILE = 128
LAND = 80
HALF = 128
PLANE = 4
LINE = 4
CHUNK = 5
STEP = 2
HOP = 2
RING = 4
LIMITS = (96, 104, 118)
ROOM = LIMITS[-1]
ENCODE_ORDER = (0, 1, 2, 3)
LAST = 5
DEST_ORDER = ((3, 2, 1, 0), (3, 2, 0, 1), (0, 1, 3, 2), (0, 1, 2, 3))
LANES = (
    ((0, 0, 3), (0, 0, 2), (0, 1, 3), (0, 2, 3), (0, 3, 3), (0, 1, 2), (0, 2, 2), (0, 3, 2), (0, 2, 1), (0, 0, 1), (0, 1, 1), (0, 3, 1)),
    ((1, 0, 3), (1, 0, 2), (1, 1, 3), (0, 0, 3), (0, 0, 2), (0, 1, 3), (1, 2, 3), (1, 3, 3), (1, 1, 2), (0, 2, 3), (0, 3, 3), (1, 3, 2), (1, 2, 2), (0, 2, 2), (0, 3, 2), (0, 1, 2)),
    ((1, 0, 3), (1, 1, 3), (2, 0, 3), (2, 1, 3), (0, 0, 3), (0, 1, 3), (1, 2, 3), (1, 3, 3), (0, 2, 3), (2, 3, 3), (0, 3, 3), (2, 2, 3)),
)
MESH = pl.DeviceIdType.MESH
HIGHEST = lax.Precision.HIGHEST
F32 = jnp.float32
BF16 = jnp.bfloat16


def split(x):
    high = x.astype(BF16)
    return high, x - high.astype(F32)


def encode_rows(x, wp, bp, ws, wt, spread_ones, ones):
    x = x.astype(F32)
    centred = x - jnp.sum(x, axis=-1, keepdims=True) * (1.0 / WIDTH)
    spread = jnp.sum(centred * centred, axis=-1, keepdims=True) * (1.0 / WIDTH)
    normed = (centred * lax.rsqrt(spread + 1e-05)).astype(BF16)
    dot = functools.partial(jnp.dot, preferred_element_type=F32)
    proj = (dot(normed, wp) + bp).astype(BF16)
    logits = dot(proj, ws)
    soft = dot(proj, wt)
    temper = 0.5 + (jnp.maximum(soft, 0.0) + jnp.log1p(jnp.exp(-jnp.abs(soft))))
    first, rest = split(1.0 / temper)
    second, rest = split(rest)
    lane = lax.broadcasted_iota(jnp.int32, soft.shape, 1)
    parts = jnp.where(lane < HEADS, first.astype(F32), jnp.where(lane < 2 * HEADS, second.astype(F32), rest))
    scale = dot(parts.astype(BF16), spread_ones)
    raised = jnp.exp(logits * scale)
    first, rest = split(raised)
    total = dot(first, ones) + dot(rest.astype(BF16), ones)
    return proj, (raised / total).astype(BF16)


def diagonal(block, times):
    wide = jnp.concatenate([block] * times, axis=1)
    full = jnp.concatenate([wide] * times, axis=0)
    size = times * FEAT
    row = lax.broadcasted_iota(jnp.int32, (size, size), 0) // FEAT
    lane = lax.broadcasted_iota(jnp.int32, (size, size), 1) // FEAT
    return jnp.where(row == lane, full, 0.0)


def build(slice_weight, softness, qkv_small, ws, wt, spread_ones, ones, head_ones, qkv):
    ws[...] = diagonal(slice_weight[...].astype(F32), HEADS).astype(BF16)
    for i in range(3):
        qkv[i] = diagonal(qkv_small[i], 4)
    unity = jnp.ones((FEAT, FEAT), F32)
    ones[...] = diagonal(unity, HEADS).astype(BF16)
    head_ones[...] = diagonal(unity, 4)
    row = lax.broadcasted_iota(jnp.int32, (HALF, WIDTH), 0)
    lane = lax.broadcasted_iota(jnp.int32, (HALF, WIDTH), 1) // FEAT
    spread_ones[...] = jnp.where((row % HEADS == lane) & (row < 3 * HEADS), 1.0, 0.0).astype(BF16)
    flat = jnp.concatenate([softness[...].astype(F32)] * 4, axis=1)
    tall = jnp.transpose(jnp.broadcast_to(flat, (HALF, HALF)))
    tall = jnp.concatenate([tall, tall], axis=0)
    row = lax.broadcasted_iota(jnp.int32, (WIDTH, HALF), 0) // FEAT
    lane = lax.broadcasted_iota(jnp.int32, (WIDTH, HALF), 1)
    wt[...] = jnp.where((row == lane % HEADS) & (lane < 3 * HEADS), tall, 0.0).astype(BF16)


def move_kernel(
    n, per_peer, unit, source, label, points, labels, wp, bp, slice_weight, softness, qkv_small,
    wo, bo, result, labels_out,
    held_points, sending, arrived, numer, denom, sums, inbox, mixed,
    ws, wt, spread_ones, ones, head_ones, qkv,
    point_sem, send_sem, recv_sem, lab_send, lab_recv, own_sem, out_sem, red_send, red_recv,
):
    me = lax.axis_index("dom")
    pieces = per_peer // unit
    rows = unit * TILE
    fetch = pltpu.make_async_copy(points, held_points, point_sem)
    fetch.start()

    def partner(x):
        peer, bit = 0, 1
        while bit < n:
            mine, flip = me // bit % 2, x // bit % 2
            peer = peer + bit * (mine + flip - 2 * mine * flip)
            bit = bit * 2
        return peer

    barrier = pltpu.get_barrier_semaphore()
    for x in range(1, n):
        pl.semaphore_signal(barrier, inc=1, device_id={"dom": partner(x)}, device_id_type=MESH)
    numer[...] = jnp.zeros_like(numer)
    denom[...] = jnp.zeros_like(denom)
    build(slice_weight, softness, qkv_small, ws, wt, spread_ones, ones, head_ones, qkv)
    pl.semaphore_wait(barrier, n - 1)

    def order(i):
        quarter = n // 4
        near = lax.rem(i, 2) * 2 * quarter
        early = 3 * quarter + i // 2 - near
        late = jnp.where(i < 3 * quarter, i, n - 1 - i)
        return jnp.where(i < 2 * quarter, early, late)

    def lab_copy(x):
        peer = partner(x)
        return pltpu.make_async_remote_copy(
            src_ref=labels.at[peer], dst_ref=labels_out.at[me], send_sem=lab_send.at[x],
            recv_sem=lab_recv.at[x], device_id={"dom": peer}, device_id_type=MESH,
        )

    def piece_copy(x, s):
        at = pl.ds(pl.multiple_of(s * rows, rows), rows)
        return pltpu.make_async_remote_copy(
            src_ref=sending.at[x, at], dst_ref=arrived.at[x, at], send_sem=send_sem.at[x, s],
            recv_sem=recv_sem.at[x, s], device_id={"dom": partner(x)}, device_id_type=MESH,
        )

    def lab_start(x, _):
        lab_copy(x).start()
        return 0

    lax.fori_loop(1, n, lab_start, 0)
    own_lab = pltpu.make_async_copy(labels.at[me], labels_out.at[me], own_sem)
    own_lab.start()
    fetch.wait()

    def compute(x, peer, s):
        first = peer * per_peer + s * unit
        tiles = jnp.concatenate([held_points[source[first + j]] for j in range(unit)], axis=0)
        proj, weights = encode_rows(
            tiles, wp[...], bp[...], ws[...], wt[...], spread_ones[...], ones[...]
        )
        live = jnp.concatenate(
            [jnp.full((TILE, WIDTH), label[first + j], jnp.int32) for j in range(unit)], axis=0
        ) >= 0
        kept = jnp.where(live, weights.astype(F32), 0.0)
        weights = kept.astype(BF16)
        sending[x, pl.ds(pl.multiple_of(s * rows, rows), rows), :] = weights
        numer[...] += lax.dot_general(
            weights, proj, (((0,), (0,)), ((), ())), preferred_element_type=F32
        )
        denom[...] += jnp.sum(kept.reshape(rows // 8, 8, WIDTH), axis=0)

    steps = (n - 1) * pieces
    held_from = (n - 1) * (pieces - 1)

    def encode_step(i, _):
        x = order(i % (n - 1))
        compute(x, partner(x), i // (n - 1))

        @pl.when((i > 0) & (i <= held_from))
        def _():
            piece_copy(order((i - 1) % (n - 1)), (i - 1) // (n - 1)).start()

        return 0

    lax.fori_loop(0, steps, encode_step, 0)

    def own_step(s, _):
        compute(0, me, s)
        return 0

    lax.fori_loop(0, pieces, own_step, 0)

    lane_head = lax.broadcasted_iota(jnp.int32, (FEAT, HALF), 1) // FEAT
    for a in range(2):
        acc = jnp.zeros((FEAT, HALF), F32)
        for j in range(4):
            part = numer[pl.ds((a * 4 + j) * FEAT, FEAT), pl.ds(a * HALF, HALF)]
            acc = acc + jnp.where(lane_head == j, part, 0.0)
        sums[0, pl.ds(a * FEAT, FEAT), :] = acc
        total = jnp.sum(denom[:, pl.ds(a * HALF, HALF)], axis=0, keepdims=True)
        sums[0, pl.ds(2 * FEAT + a * 8, 8), :] = jnp.broadcast_to(total, (8, HALF))

    def release(i, _):
        piece_copy(order(i - held_from), pieces - 1).start()
        return 0

    level, bit = 0, n // 2
    while bit > 0:
        swap = pltpu.make_async_remote_copy(
            src_ref=sums.at[level], dst_ref=inbox.at[level], send_sem=red_send.at[level],
            recv_sem=red_recv.at[level], device_id={"dom": partner(bit)}, device_id_type=MESH,
        )
        swap.start()
        swap.wait()
        sums[level + 1] = sums[level] + inbox[level]
        level, bit = level + 1, bit // 2
        if level == max(1, (n - 1).bit_length() - 2):
            lax.fori_loop(held_from, steps, release, 0)
    mixed[...] = mix(sums[level], qkv, head_ones[...])

    def out_copy(x, s):
        at = pl.ds(pl.multiple_of(s * rows, rows), rows)
        return pltpu.make_async_copy(arrived.at[x, at], result.at[partner(x), at], out_sem.at[x, s])

    def decode(read, x, s):
        at = pl.ds(pl.multiple_of(s * rows, rows), rows)
        deslice = jnp.dot(read[x, at, :], mixed[...], preferred_element_type=F32).astype(BF16)
        y = (jnp.dot(deslice, wo[...], preferred_element_type=F32) + bo[...]).astype(BF16)
        arrived[x, at, :] = y
        out_copy(x, s).start()

    def decode_own(s, _):
        decode(sending, 0, s)
        return 0

    lax.fori_loop(0, pieces, decode_own, 0)

    def from_peer(i, _):
        x, s = order(i % (n - 1)), i // (n - 1)
        piece_copy(x, s).wait_recv()
        decode(arrived, x, s)
        return 0

    lax.fori_loop(0, steps, from_peer, 0)

    def finish(x, _):
        def one(s, _):
            piece_copy(x, s).wait_send()
            return 0

        lax.fori_loop(0, pieces, one, 0)
        lab_copy(x).wait()
        return 0

    lax.fori_loop(1, n, finish, 0)
    own_lab.wait()

    def drain(i, _):
        out_copy(i // pieces, i % pieces).wait()
        return 0

    lax.fori_loop(0, n * pieces, drain, 0)


def mix(stats, qkv, ones):
    row_head = lax.broadcasted_iota(jnp.int32, (HALF, HALF), 0) // FEAT
    lane_head = lax.broadcasted_iota(jnp.int32, (HALF, HALF), 1) // FEAT
    same = row_head == lane_head
    blocks = []
    for a in range(2):
        numer = stats[a * FEAT:(a + 1) * FEAT, :]
        row = stats[2 * FEAT + a * 8:2 * FEAT + (a + 1) * 8, :]
        col = jnp.transpose(jnp.broadcast_to(row[:1], (HALF, HALF)))
        spread = jnp.zeros((FEAT, HALF), F32)
        for j in range(4):
            spread = spread + jnp.where(
                lane_head[:FEAT] == j, col[j * FEAT:(j + 1) * FEAT, :], 0.0
            )
        tokens = numer / (spread + 1e-05)
        dot = functools.partial(jnp.dot, preferred_element_type=F32, precision=HIGHEST)
        query, keys, values = (dot(tokens, qkv[i]) for i in range(3))
        spread_keys = jnp.where(same, jnp.concatenate([keys] * 4, axis=0), 0.0)
        scores = lax.dot_general(
            query, spread_keys, (((1,), (1,)), ((), ())), preferred_element_type=F32, precision=HIGHEST
        ) * FEAT ** (-0.5)
        raised = jnp.exp(scores)
        attend = raised / dot(raised, ones)
        spread_values = jnp.where(same, jnp.concatenate([values] * 4, axis=0), 0.0)
        mixed = dot(attend, spread_values)
        blocks.append(jnp.where(same, jnp.concatenate([mixed] * 4, axis=0), 0.0))
    nil = jnp.zeros((HALF, HALF), F32)
    return jnp.concatenate(
        [jnp.concatenate([blocks[0], nil], axis=1), jnp.concatenate([nil, blocks[1]], axis=1)], axis=0
    ).astype(BF16)


def place_kernel(n, per_peer, chunks, per_chunk, labels, tiles, out, held, in_sem, out_sem):
    def load(k, _):
        def one(t, _):
            slot = labels[k, t]

            @pl.when(slot >= 0)
            def _():
                pltpu.make_async_copy(
                    tiles.at[k * per_peer + t], held.at[slot], in_sem.at[slot // per_chunk]
                ).start()

            return 0

        return lax.fori_loop(0, per_peer, one, 0)

    lax.fori_loop(0, n, load, 0)

    def step(c, _):
        part = pl.ds(c * per_chunk, per_chunk)
        pltpu.make_async_copy(tiles.at[pl.ds(0, per_chunk)], held.at[part], in_sem.at[c]).wait()
        pltpu.make_async_copy(held.at[part], out.at[part], out_sem.at[c]).start()
        return 0

    lax.fori_loop(0, chunks, step, 0)

    def finish(c, _):
        part = pl.ds(c * per_chunk, per_chunk)
        pltpu.make_async_copy(held.at[part], out.at[part], out_sem.at[c]).wait()
        return 0

    lax.fori_loop(0, chunks, finish, 0)


def plan(destination, own_count, n):
    slots = destination.shape[0]
    per_peer = slots // n
    index = jnp.arange(slots, dtype=jnp.int32)
    live = index < own_count
    target = jnp.where(live, destination // LAND, -1)
    slot = jnp.where(live, destination % LAND, -1)
    earlier = (target[:, None] == target[None, :]) & live[None, :] & (index[None, :] < index[:, None])
    rank = jnp.sum(earlier.astype(jnp.int32), axis=1)
    place = target * per_peer + rank
    matches = live[None, :] & (place[None, :] == index[:, None])
    source = jnp.sum(jnp.where(matches, index[None, :], 0), axis=1)
    label = jnp.sum(jnp.where(matches, slot[None, :] + 1, 0), axis=1) - 1
    return source, label


def direct(n, points, counts, destination, wp, bp, slice_weight, softness, qkv, wo, bo):
    slots = points.shape[0] // TILE
    per_peer = slots // n
    any_spec = pl.BlockSpec(memory_space=pl.ANY)
    vmem = pl.BlockSpec(memory_space=pltpu.VMEM)
    smem = pl.BlockSpec(memory_space=pltpu.SMEM)
    source, label = plan(destination, counts[0], n)
    rows = per_peer * TILE
    labels = jnp.pad(label.reshape(n, 1, per_peer), ((0, 0), (0, 0), (0, HALF - per_peer)))
    unit = 2 if per_peer % 2 == 0 else 1
    pieces = per_peer // unit
    levels = (n - 1).bit_length()
    stat_rows = 2 * FEAT + 16
    dma = pltpu.SemaphoreType.DMA
    tiles, arrived_lab = pl.pallas_call(
        functools.partial(move_kernel, n, per_peer, unit),
        out_shape=(
            jax.ShapeDtypeStruct((n, rows, WIDTH), BF16),
            jax.ShapeDtypeStruct((n, 1, HALF), jnp.int32),
        ),
        in_specs=[smem, smem, any_spec, any_spec] + [vmem] * 7,
        out_specs=(any_spec, any_spec),
        scratch_shapes=[
            pltpu.VMEM((slots, TILE, WIDTH), BF16),
            pltpu.VMEM((n, rows, WIDTH), BF16),
            pltpu.VMEM((n, rows, WIDTH), BF16),
            pltpu.VMEM((WIDTH, WIDTH), F32),
            pltpu.VMEM((8, WIDTH), F32),
            pltpu.VMEM((levels + 1, stat_rows, HALF), F32),
            pltpu.VMEM((levels, stat_rows, HALF), F32),
            pltpu.VMEM((WIDTH, WIDTH), BF16),
            pltpu.VMEM((WIDTH, WIDTH), BF16),
            pltpu.VMEM((WIDTH, HALF), BF16),
            pltpu.VMEM((HALF, WIDTH), BF16),
            pltpu.VMEM((WIDTH, WIDTH), BF16),
            pltpu.VMEM((HALF, HALF), F32),
            pltpu.VMEM((3, HALF, HALF), F32),
            dma, dma((n, pieces)), dma((n, pieces)), dma((n,)), dma((n,)), dma, dma((n, pieces)),
            dma((levels,)), dma((levels,)),
        ],
        compiler_params=pltpu.CompilerParams(
            collective_id=15, has_side_effects=True, vmem_limit_bytes=60 << 20
        ),
        name="move",
    )(
        source, label, points.reshape(slots, TILE, WIDTH), labels, wp, bp.reshape(1, WIDTH),
        slice_weight, softness.reshape(1, FEAT), qkv, wo, bo.reshape(1, WIDTH),
    )

    per_chunk = 8
    chunks = LAND // per_chunk
    placed = pl.pallas_call(
        functools.partial(place_kernel, n, per_peer, chunks, per_chunk),
        out_shape=jax.ShapeDtypeStruct((LAND, TILE, WIDTH), BF16),
        grid_spec=pltpu.PrefetchScalarGridSpec(
            num_scalar_prefetch=1, grid=(), in_specs=[any_spec], out_specs=any_spec,
            scratch_shapes=[pltpu.VMEM((LAND, TILE, WIDTH), BF16), dma((chunks,)), dma((chunks,))],
        ),
        compiler_params=pltpu.CompilerParams(vmem_limit_bytes=60 << 20),
        name="place",
    )(arrived_lab.reshape(n, HALF), tiles.reshape(slots, TILE, WIDTH))
    return placed.reshape(LAND * TILE, WIDTH)


def mirror(me, n):
    steps, bit = [], 1
    while bit < n:
        steps.append((bit, bit - 2 * bit * (me // bit % 2)))
        bit = bit * 2

    def peer(x):
        out = me
        for bit, step in steps:
            if isinstance(x, int):
                out = out + step if x & bit else out
            else:
                out = out + step * (x // bit % 2)
        return out

    return peer


def tell_kernel(n, groups, rows, got, send_sem, recv_sem, own_sem):
    me, group = lax.axis_index("dom"), lax.axis_index("groups")
    mine = me // PLANE * PLANE
    peer, other = mirror(me, n), mirror(group, groups)
    barrier = pltpu.get_barrier_semaphore()

    def device(x):
        return {"groups": other(x // n), "dom": peer(x % n)}

    for x in range(1, n * groups):
        pl.semaphore_signal(barrier, inc=1, device_id=device(x), device_id_type=MESH)
    own = pltpu.make_async_copy(rows.at[0], got.at[mine], own_sem)
    own.start()
    pl.semaphore_wait(barrier, n * groups - 1)

    def tell(x):
        w = x % PLANE
        return pltpu.make_async_remote_copy(
            src_ref=rows.at[w], dst_ref=got.at[x // n * n + mine + w], send_sem=send_sem.at[x],
            recv_sem=recv_sem.at[x], device_id=device(x), device_id_type=MESH,
        )

    copies = [tell(x) for x in range(1, n * groups)]
    for copy in copies:
        copy.start()
    for copy in copies:
        copy.wait()
    own.wait()


def encoded(i):
    return (2 * i + 1) // 3


def due(w, j):
    step = PLANE * j + ENCODE_ORDER.index(w)
    if w == 0:
        return ((2 * step + 1) * 171) >> 9
    if w == 1:
        return ((2 * step + 4) * 171) >> 9
    return 5 * j + (4 if ENCODE_ORDER.index(w) < ENCODE_ORDER.index(5 - w) else 7)


def table_kernel(n, groups, per_peer, got, sends, slots, branch, starts):
    z = lax.axis_index("dom") // PLANE
    flow = LINE * per_peer
    table = ROOM + per_peer

    def clear(i, _):
        sends[0, i] = 0
        sends[1, i] = 0
        return 0

    lax.fori_loop(0, table, clear, 0)

    def schedule(g, column, keep):
        longest = jnp.int32(0)
        sizes, firsts = {}, {}
        for zo in range(LINE):
            for w in range(PLANE):
                total = jnp.int32(0)
                row = g * n + zo * PLANE + (column ^ w)
                for zd in DEST_ORDER[zo]:
                    if zd != zo:
                        size = got[row, flow + w * LINE + zd]
                        sizes[zo, w, zd], firsts[zo, w, zd] = size, total
                        total = total + size
        for way in range(2):
            def plane(p):
                return LINE - 1 - p if way else p

            def real(cl):
                return plane(cl[0]), cl[1], plane(cl[2])

            before = {}
            for lane, order in enumerate(LANES):
                pos, now = jnp.int32(0), {}
                for at, cl in enumerate(order):
                    size = sizes[real(cl)]
                    if cl[0] == lane:
                        begin = firsts[real(cl)]
                        last = ((begin + size - 1) * 13) >> 6
                        slack = CHUNK * last - begin - (1 if cl[1] < 2 else 0)
                        ready = STEP * due(cl[1], last) - jnp.maximum(0, slack)
                    else:
                        ready = before[cl] + HOP * STEP
                    start = jnp.where(size > 0, jnp.maximum(pos, ready), pos)
                    now[cl] = start
                    if keep:
                        starts[way, lane, at] = start
                    pos = start + size
                before = now
                longest = jnp.maximum(longest, pos)
        return longest

    longest = schedule(0, 0, True)

    def others(i, most):
        return jnp.maximum(most, schedule(i // PLANE, i % PLANE, False))

    longest = lax.fori_loop(1, groups * PLANE, others, longest)
    choice = jnp.int32(0)
    for limit in LIMITS:
        choice = choice + jnp.where(longest > limit, 1, 0)
    branch[0] = choice

    def fill(me):
        def row(zo, w):
            return zo * PLANE + w

        def size_of(zo, w, zd):
            return got[row(zo, w), flow + w * LINE + zd]

        def first_of(zo, w, zd):
            total = jnp.int32(0)
            for real in DEST_ORDER[zo]:
                if real == zd:
                    return total
                total = total + size_of(zo, w, real)

        for way in range(2):
            def plane(p):
                return LINE - 1 - p if way else p

            lane = plane(me)
            if lane == LINE - 1:
                continue
            landed = PLANE * flow + way * ROOM
            for at, cl in enumerate(LANES[lane]):
                zo, w, zd = plane(cl[0]), cl[1], plane(cl[2])
                if zo == me:
                    source = w * flow + first_of(zo, w, zd)
                else:
                    source = landed + starts[way, lane - 1, LANES[lane - 1].index(cl)]
                size = size_of(zo, w, zd)
                start = jnp.minimum(starts[way, lane, at], ROOM)
                for k in range(per_peer):
                    sends[way, start + k] = jnp.where(k < size, source + k, 0)
        for zo in range(LINE):
            for w in range(PLANE):
                first = first_of(zo, w, me)
                size = size_of(zo, w, me)
                if zo == me:
                    source = w * flow + first
                else:
                    way = 0 if zo < me else 1
                    lane = me - 1 if zo < me else LINE - 2 - me
                    cl = (zo, w, me) if zo < me else (LINE - 1 - zo, w, LINE - 1 - me)
                    source = PLANE * flow + way * ROOM + starts[way, lane, LANES[lane].index(cl)]
                for k in range(per_peer):
                    label = got[row(zo, w), first + k]
                    slots[jnp.where(k < size, label + 1, 0)] = source + k

    for me in range(LINE):
        @pl.when(z == me)
        def _():
            fill(me)


def relay_kernel(
    n, per_peer, limit, source, label, sends, slots, points, wp, bp, slice_weight, softness, qkv_small,
    wo, bo, result,
    held, pool, sending, landed, stage, landing, numer, denom, sums, inbox, mixed,
    ws, wt, spread_ones, ones, head_ones, qkv,
    point_sem, plane_send, plane_recv, line_send, line_recv, red_send, red_recv, out_sem,
):
    me = lax.axis_index("dom")
    z = me // PLANE
    peer = mirror(me, n)
    flow = LINE * per_peer
    chunks = flow // CHUNK
    rounds = limit // STEP
    fetch = pltpu.make_async_copy(points, held, point_sem)
    fetch.start()
    barrier = pltpu.get_barrier_semaphore()
    for x in range(1, n):
        pl.semaphore_signal(barrier, inc=1, device_id={"dom": peer(x)}, device_id_type=MESH)
    numer[...] = jnp.zeros_like(numer)
    denom[...] = jnp.zeros_like(denom)
    build(slice_weight, softness, qkv_small, ws, wt, spread_ones, ones, head_ones, qkv)
    pl.semaphore_wait(barrier, n - 1)
    fetch.wait()

    def plane_copy(w, j):
        return pltpu.make_async_remote_copy(
            src_ref=sending.at[w - 1, j], dst_ref=landed.at[w - 1, j], send_sem=plane_send.at[w - 1, j],
            recv_sem=plane_recv.at[w - 1, j], device_id={"dom": peer(w)},
            device_id_type=MESH,
        )

    def line_copy(way, r):
        slot = r % RING
        near = me + PLANE if way == 0 else me - PLANE
        return pltpu.make_async_remote_copy(
            src_ref=stage.at[way, slot], dst_ref=landing.at[way, slot], send_sem=line_send.at[way, slot],
            recv_sem=line_recv.at[way, slot], device_id={"dom": near}, device_id_type=MESH,
        )

    can_send = (z < LINE - 1, z > 0)
    can_recv = (z > 0, z < LINE - 1)

    def encode(i, _):
        j, turn = i // PLANE, i % PLANE
        w = ENCODE_ORDER[0]
        for at in range(1, PLANE):
            w = jnp.where(turn == at, ENCODE_ORDER[at], w)
        first = w * flow + j * CHUNK
        tiles = jnp.concatenate([held[source[first + k]] for k in range(CHUNK)], axis=0)
        proj, weights = encode_rows(
            tiles, wp[...], bp[...], ws[...], wt[...], spread_ones[...], ones[...]
        )
        live = jnp.concatenate(
            [jnp.full((TILE, WIDTH), label[first + k], jnp.int32) for k in range(CHUNK)], axis=0
        ) >= 0
        kept = jnp.where(live, weights.astype(F32), 0.0)
        weights = kept.astype(BF16)
        numer[...] += lax.dot_general(
            weights, proj, (((0,), (0,)), ((), ())), preferred_element_type=F32
        )
        denom[...] += jnp.sum(kept.reshape(CHUNK * TILE // 8, 8, WIDTH), axis=0)
        weights = weights.reshape(CHUNK, TILE, WIDTH)

        @pl.when(turn == 0)
        def _():
            pool[pl.ds(j * CHUNK, CHUNK)] = weights

        @pl.when(turn > 0)
        def _():
            sending[w - 1, j] = weights

        @pl.when(turn == ENCODE_ORDER.index(1))
        def _():
            plane_copy(1, j).start()

        return 0

    def line_arrive(way, m):
        line_copy(way, m).wait_recv()
        pool[pl.ds(PLANE * flow + way * ROOM + m * STEP, STEP)] = landing[way, m % RING]

    def release(w, r):
        begin, first = due(w, 0) - 5, encoded(ENCODE_ORDER.index(w))
        since = r - begin
        j = since // 5
        now = (since % 5 == 0) & (j >= 0) & (j < chunks)
        if begin < first:
            now = (now & (j > 0)) | (r == first)
            j = jnp.where(r == first, 0, j)

        @pl.when(now)
        def _():
            plane_copy(w, j).start()

    def relay(r):
        for w in range(2, PLANE):
            release(w, r)
        for way in range(2):
            @pl.when(can_recv[way] & (r >= HOP))
            def _():
                line_arrive(way, r - HOP)
        for w in range(1, PLANE):
            if w == 1:
                late = 2 * ENCODE_ORDER.index(w) + 4
                j = (3 * r + 7 - late) // 8
                now = (3 * r + 7 >= late) & ((8 * j + late) // 3 == r)
            else:
                since = r - due(w, 0)
                j = since // 5
                now = (since >= 0) & (since % 5 == 0)

            @pl.when(now & (j < chunks))
            def _():
                plane_copy(w, j).wait_recv()
                pool[pl.ds(w * flow + j * CHUNK, CHUNK)] = landed[w - 1, j]

        for way in range(2):
            @pl.when(can_send[way])
            def _():
                @pl.when(r >= RING)
                def _():
                    line_copy(way, r - RING).wait_send()

                for k in range(STEP):
                    stage[way, r % RING, k] = pool[sends[way, r * STEP + k]]
                line_copy(way, r).start()

    steps = PLANE * chunks

    def first_rounds(r, _):
        lax.fori_loop(3 * r // 2, jnp.minimum(3 * (r + 1) // 2, steps), encode, 0)
        relay(r)
        return 0

    def more_rounds(r, _):
        relay(r)
        return 0

    reached = encoded(steps - 1) + 1
    lax.fori_loop(0, reached, first_rounds, 0)

    lane_head = lax.broadcasted_iota(jnp.int32, (FEAT, HALF), 1) // FEAT
    for a in range(2):
        acc = jnp.zeros((FEAT, HALF), F32)
        for j in range(4):
            part = numer[pl.ds((a * 4 + j) * FEAT, FEAT), pl.ds(a * HALF, HALF)]
            acc = acc + jnp.where(lane_head == j, part, 0.0)
        sums[0, pl.ds(a * FEAT, FEAT), :] = acc
        total = jnp.sum(denom[:, pl.ds(a * HALF, HALF)], axis=0, keepdims=True)
        sums[0, pl.ds(2 * FEAT + a * 8, 8), :] = jnp.broadcast_to(total, (8, HALF))
    level, bit = 0, n // 2
    while bit > 0:
        swap = pltpu.make_async_remote_copy(
            src_ref=sums.at[level], dst_ref=inbox.at[level], send_sem=red_send.at[level],
            recv_sem=red_recv.at[level], device_id={"dom": peer(bit)}, device_id_type=MESH,
        )
        swap.start()
        lax.fori_loop(reached, reached + 4, more_rounds, 0)
        reached = reached + 4
        swap.wait()
        sums[level + 1] = sums[level] + inbox[level]
        level, bit = level + 1, bit // 2
    mixed[...] = mix(sums[level], qkv, head_ones[...])

    def decode(rows):
        deslice = jnp.dot(rows, mixed[...], preferred_element_type=F32).astype(BF16)
        y = (jnp.dot(deslice, wo[...], preferred_element_type=F32) + bo[...]).astype(BF16)
        return y.reshape(rows.shape[0] // TILE, TILE, WIDTH)

    group = LAND // (2 * LAST)
    early = rounds - LAST
    lax.fori_loop(reached, early, more_rounds, 0)

    def last_rounds(r, _):
        relay(r)
        for half in range(2):
            i = (2 * (r - early) + half) * group
            rows = jnp.concatenate([pool[slots[i + k + 1]] for k in range(group)], axis=0)
            held[pl.ds(i, group)] = decode(rows)
        return 0

    lax.fori_loop(early, rounds, last_rounds, 0)
    seen = (early - HOP + 1) * STEP
    rest = limit - seen
    for way in range(2):
        @pl.when(can_recv[way])
        def _():
            def arrive(m, _):
                line_arrive(way, m)
                return 0

            lax.fori_loop(rounds - HOP, rounds, arrive, 0)

        begin = PLANE * flow + way * ROOM + seen
        rows = pool[pl.ds(begin, rest)].reshape(rest * TILE, WIDTH)
        held[pl.ds(LAND + way * rest, rest)] = decode(rows)

    def out_copy(i):
        return pltpu.make_async_copy(
            landed.at[i // chunks, i % chunks], result.at[pl.ds(i * CHUNK, CHUNK)], out_sem.at[i]
        )

    def finish(i, _):
        for k in range(CHUNK):
            at = i * CHUNK + k
            where = slots[at + 1] - PLANE * flow
            way = jnp.where(where >= ROOM, 1, 0)
            pos = where - way * ROOM - seen
            late = (where >= 0) & (pos >= 0)
            landed[i // chunks, i % chunks, k] = held[jnp.where(late, LAND + way * rest + pos, at)]
        out_copy(i).start()
        return 0

    lax.fori_loop(0, LAND // CHUNK, finish, 0)

    for way in range(2):
        @pl.when(can_send[way])
        def _():
            def sent(r, _):
                line_copy(way, r).wait_send()
                return 0

            lax.fori_loop(rounds - RING, rounds, sent, 0)

    def plane_sent(i, _):
        plane_copy(1 + i % (PLANE - 1), i // (PLANE - 1)).wait_send()
        return 0

    lax.fori_loop(0, (PLANE - 1) * chunks, plane_sent, 0)

    def drain(i, _):
        out_copy(i).wait()
        return 0

    lax.fori_loop(0, LAND // CHUNK, drain, 0)


def arrange(destination, own_count, n, me):
    slots = destination.shape[0]
    flow = slots // PLANE
    index = jnp.arange(slots, dtype=jnp.int32)
    live = index < own_count
    target, slot = destination // LAND, destination % LAND
    w = (target % PLANE) ^ (me % PLANE)
    line, own = target // PLANE, me // PLANE
    upper = own >= LINE // 2
    far = jnp.where(upper, LINE - 1 - line, line)
    near = jnp.where(upper, LINE - 1 - own, own)
    rank = jnp.where(
        far > near, LINE - 1 - far, jnp.where(far < near, LINE - 1 - near + far, LINE - 1)
    )
    w = jnp.where(live, w, -1)
    key = rank * slots + index
    earlier = (w[:, None] == w[None, :]) & (key[None, :] < key[:, None])
    place = w * flow + jnp.sum(earlier.astype(jnp.int32), axis=1)
    matches = live[None, :] & (place[None, :] == index[:, None])
    source = jnp.sum(jnp.where(matches, index[None, :], 0), axis=1)
    label = jnp.sum(jnp.where(matches, slot[None, :] + 1, 0), axis=1) - 1
    kind = jnp.where(live, w * LINE + line, -1)
    kinds = jnp.arange(PLANE * LINE, dtype=jnp.int32)
    sizes = jnp.sum((kind[None, :] == kinds[:, None]).astype(jnp.int32), axis=1)
    return source, label, sizes


def relayed(n, groups, points, counts, destination, wp, bp, slice_weight, softness, qkv, wo, bo):
    slots = points.shape[0] // TILE
    per_peer = slots // n
    flow = slots // PLANE
    any_spec = pl.BlockSpec(memory_space=pl.ANY)
    vmem = pl.BlockSpec(memory_space=pltpu.VMEM)
    smem = pl.BlockSpec(memory_space=pltpu.SMEM)
    dma = pltpu.SemaphoreType.DMA
    source, label, sizes = arrange(destination, counts[0], n, lax.axis_index("dom"))
    rows = jnp.concatenate(
        [label.reshape(PLANE, flow), jnp.broadcast_to(sizes[None], (PLANE, PLANE * LINE))], axis=1
    )
    rows = jnp.pad(rows, ((0, 0), (0, HALF - rows.shape[1]))).reshape(PLANE, 1, HALF)
    got = pl.pallas_call(
        functools.partial(tell_kernel, n, groups),
        out_shape=jax.ShapeDtypeStruct((groups * n, 1, HALF), jnp.int32),
        in_specs=[any_spec], out_specs=any_spec,
        scratch_shapes=[dma((n * groups,)), dma((n * groups,)), dma],
        compiler_params=pltpu.CompilerParams(collective_id=0, has_side_effects=True),
        name="tell",
    )(rows)
    sends, places, branch = pl.pallas_call(
        functools.partial(table_kernel, n, groups, per_peer),
        out_shape=(
            jax.ShapeDtypeStruct((2, ROOM + per_peer), jnp.int32),
            jax.ShapeDtypeStruct((LAND + 1,), jnp.int32),
            jax.ShapeDtypeStruct((1,), jnp.int32),
        ),
        in_specs=[smem], out_specs=(smem, smem, smem),
        scratch_shapes=[pltpu.SMEM((2, LINE - 1, PLANE * LINE), jnp.int32)],
        name="table",
    )(got.reshape(groups * n, HALF))

    levels = (n - 1).bit_length()
    stat_rows = 2 * FEAT + 16
    tile = (TILE, WIDTH)

    def relay(limit, at, *_):
        placed = pl.pallas_call(
            functools.partial(relay_kernel, n, per_peer, limit),
            out_shape=jax.ShapeDtypeStruct((LAND,) + tile, BF16),
            in_specs=[smem] * 4 + [any_spec] + [vmem] * 7,
            out_specs=any_spec,
            scratch_shapes=[
                pltpu.VMEM((slots,) + tile, BF16),
                pltpu.VMEM((slots + 2 * ROOM,) + tile, BF16),
                pltpu.VMEM((PLANE - 1, flow // CHUNK, CHUNK) + tile, BF16),
                pltpu.VMEM((PLANE - 1, flow // CHUNK, CHUNK) + tile, BF16),
                pltpu.VMEM((2, RING, STEP) + tile, BF16),
                pltpu.VMEM((2, RING, STEP) + tile, BF16),
                pltpu.VMEM((WIDTH, WIDTH), F32),
                pltpu.VMEM((8, WIDTH), F32),
                pltpu.VMEM((levels + 1, stat_rows, HALF), F32),
                pltpu.VMEM((levels, stat_rows, HALF), F32),
                pltpu.VMEM((WIDTH, WIDTH), BF16),
                pltpu.VMEM((WIDTH, WIDTH), BF16),
                pltpu.VMEM((WIDTH, HALF), BF16),
                pltpu.VMEM((HALF, WIDTH), BF16),
                pltpu.VMEM((WIDTH, WIDTH), BF16),
                pltpu.VMEM((HALF, HALF), F32),
                pltpu.VMEM((3, HALF, HALF), F32),
                dma, dma((PLANE - 1, flow // CHUNK)), dma((PLANE - 1, flow // CHUNK)),
                dma((2, RING)), dma((2, RING)), dma((levels,)), dma((levels,)), dma((LAND // CHUNK,)),
            ],
            compiler_params=pltpu.CompilerParams(
                collective_id=1 + at, has_side_effects=True, vmem_limit_bytes=62 << 20
            ),
            name="relay" + str(limit),
        )(
            source, label, sends, places, points.reshape((slots,) + tile), wp, bp.reshape(1, WIDTH),
            slice_weight, softness.reshape(1, FEAT), qkv, wo, bo.reshape(1, WIDTH),
        )
        return placed.reshape(LAND * TILE, WIDTH)

    def fallback():
        return direct(n, points, counts, destination, wp, bp, slice_weight, softness, qkv, wo, bo)

    branches = [functools.partial(relay, limit, at) for at, limit in enumerate(LIMITS)]
    return lax.switch(branch[0], branches + [fallback])


def solution(mesh):
    spec = P(("groups", "dom"))
    wide = P(("groups", "dom"), None)
    n, groups = mesh.shape["dom"], mesh.shape["groups"]
    if n == PLANE * LINE and groups == 2:
        body = functools.partial(relayed, n, groups)
    else:
        body = functools.partial(direct, n)
    return jax.shard_map(
        body, mesh=mesh, in_specs=(wide, spec, spec) + (P(),) * 7, out_specs=wide, check_vma=False,
    )
```

```python
import functools

import jax
import jax.numpy as jnp
from jax import lax
from jax.experimental import pallas as pl
from jax.experimental.pallas import tpu as pltpu
from jax.sharding import PartitionSpec as P

WIDTH = 256
HEADS = 8
FEAT = 32
TILE = 128
LAND = 80
HALF = 128
PLANE = 4
LINE = 4
CHUNK = 5
STEP = 2
HOP = 2
RING = 4
LIMITS = (94, 102, 104, 124)
ROOM = LIMITS[-1]
ENCODE_ORDER = (0, 1, 2, 3)
LAST = 5
DEST_ORDER = ((3, 2, 1, 0), (3, 2, 0, 1), (0, 1, 3, 2), (0, 1, 2, 3))
LANES = (
    ((0, 0, 3), (0, 0, 2), (0, 1, 3), (0, 2, 3), (0, 3, 3), (0, 1, 2), (0, 2, 2), (0, 3, 2), (0, 2, 1), (0, 0, 1), (0, 1, 1), (0, 3, 1)),
    ((1, 0, 3), (1, 0, 2), (1, 1, 3), (0, 0, 3), (0, 0, 2), (0, 1, 3), (1, 2, 3), (1, 3, 3), (1, 1, 2), (0, 2, 3), (0, 3, 3), (1, 3, 2), (1, 2, 2), (0, 2, 2), (0, 3, 2), (0, 1, 2)),
    ((1, 0, 3), (1, 1, 3), (2, 0, 3), (2, 1, 3), (0, 0, 3), (0, 1, 3), (1, 2, 3), (1, 3, 3), (0, 2, 3), (2, 3, 3), (0, 3, 3), (2, 2, 3)),
)
MESH = pl.DeviceIdType.MESH
HIGHEST = lax.Precision.HIGHEST
F32 = jnp.float32
BF16 = jnp.bfloat16


def split(x):
    high = x.astype(BF16)
    return high, x - high.astype(F32)


def encode_rows(x, wp, bp, ws, wt, spread_ones, ones):
    x = x.astype(F32)
    centred = x - jnp.sum(x, axis=-1, keepdims=True) * (1.0 / WIDTH)
    spread = jnp.sum(centred * centred, axis=-1, keepdims=True) * (1.0 / WIDTH)
    normed = (centred * lax.rsqrt(spread + 1e-05)).astype(BF16)
    dot = functools.partial(jnp.dot, preferred_element_type=F32)
    proj = (dot(normed, wp) + bp).astype(BF16)
    logits = dot(proj, ws)
    soft = dot(proj, wt)
    temper = 0.5 + (jnp.maximum(soft, 0.0) + jnp.log1p(jnp.exp(-jnp.abs(soft))))
    first, rest = split(1.0 / temper)
    second, rest = split(rest)
    lane = lax.broadcasted_iota(jnp.int32, soft.shape, 1)
    parts = jnp.where(lane < HEADS, first.astype(F32), jnp.where(lane < 2 * HEADS, second.astype(F32), rest))
    scale = dot(parts.astype(BF16), spread_ones)
    raised = jnp.exp(logits * scale)
    first, rest = split(raised)
    total = dot(first, ones) + dot(rest.astype(BF16), ones)
    return proj, (raised / total).astype(BF16)


def diagonal(block, times):
    wide = jnp.concatenate([block] * times, axis=1)
    full = jnp.concatenate([wide] * times, axis=0)
    size = times * FEAT
    row = lax.broadcasted_iota(jnp.int32, (size, size), 0) // FEAT
    lane = lax.broadcasted_iota(jnp.int32, (size, size), 1) // FEAT
    return jnp.where(row == lane, full, 0.0)


def build(slice_weight, softness, qkv_small, ws, wt, spread_ones, ones, head_ones, qkv):
    ws[...] = diagonal(slice_weight[...].astype(F32), HEADS).astype(BF16)
    for i in range(3):
        qkv[i] = diagonal(qkv_small[i], 4)
    unity = jnp.ones((FEAT, FEAT), F32)
    ones[...] = diagonal(unity, HEADS).astype(BF16)
    head_ones[...] = diagonal(unity, 4)
    row = lax.broadcasted_iota(jnp.int32, (HALF, WIDTH), 0)
    lane = lax.broadcasted_iota(jnp.int32, (HALF, WIDTH), 1) // FEAT
    spread_ones[...] = jnp.where((row % HEADS == lane) & (row < 3 * HEADS), 1.0, 0.0).astype(BF16)
    flat = jnp.concatenate([softness[...].astype(F32)] * 4, axis=1)
    tall = jnp.transpose(jnp.broadcast_to(flat, (HALF, HALF)))
    tall = jnp.concatenate([tall, tall], axis=0)
    row = lax.broadcasted_iota(jnp.int32, (WIDTH, HALF), 0) // FEAT
    lane = lax.broadcasted_iota(jnp.int32, (WIDTH, HALF), 1)
    wt[...] = jnp.where((row == lane % HEADS) & (lane < 3 * HEADS), tall, 0.0).astype(BF16)


def move_kernel(
    n, per_peer, unit, source, label, points, labels, wp, bp, slice_weight, softness, qkv_small,
    wo, bo, result, labels_out,
    held_points, sending, arrived, numer, denom, sums, inbox, mixed,
    ws, wt, spread_ones, ones, head_ones, qkv,
    point_sem, send_sem, recv_sem, lab_send, lab_recv, own_sem, out_sem, red_send, red_recv,
):
    me = lax.axis_index("dom")
    pieces = per_peer // unit
    rows = unit * TILE
    fetch = pltpu.make_async_copy(points, held_points, point_sem)
    fetch.start()

    def partner(x):
        peer, bit = 0, 1
        while bit < n:
            mine, flip = me // bit % 2, x // bit % 2
            peer = peer + bit * (mine + flip - 2 * mine * flip)
            bit = bit * 2
        return peer

    barrier = pltpu.get_barrier_semaphore()
    for x in range(1, n):
        pl.semaphore_signal(barrier, inc=1, device_id={"dom": partner(x)}, device_id_type=MESH)
    numer[...] = jnp.zeros_like(numer)
    denom[...] = jnp.zeros_like(denom)
    build(slice_weight, softness, qkv_small, ws, wt, spread_ones, ones, head_ones, qkv)
    pl.semaphore_wait(barrier, n - 1)

    def order(i):
        quarter = n // 4
        near = lax.rem(i, 2) * 2 * quarter
        early = 3 * quarter + i // 2 - near
        late = jnp.where(i < 3 * quarter, i, n - 1 - i)
        return jnp.where(i < 2 * quarter, early, late)

    def lab_copy(x):
        peer = partner(x)
        return pltpu.make_async_remote_copy(
            src_ref=labels.at[peer], dst_ref=labels_out.at[me], send_sem=lab_send.at[x],
            recv_sem=lab_recv.at[x], device_id={"dom": peer}, device_id_type=MESH,
        )

    def piece_copy(x, s):
        at = pl.ds(pl.multiple_of(s * rows, rows), rows)
        return pltpu.make_async_remote_copy(
            src_ref=sending.at[x, at], dst_ref=arrived.at[x, at], send_sem=send_sem.at[x, s],
            recv_sem=recv_sem.at[x, s], device_id={"dom": partner(x)}, device_id_type=MESH,
        )

    def lab_start(x, _):
        lab_copy(x).start()
        return 0

    lax.fori_loop(1, n, lab_start, 0)
    own_lab = pltpu.make_async_copy(labels.at[me], labels_out.at[me], own_sem)
    own_lab.start()
    fetch.wait()

    def compute(x, peer, s):
        first = peer * per_peer + s * unit
        tiles = jnp.concatenate([held_points[source[first + j]] for j in range(unit)], axis=0)
        proj, weights = encode_rows(
            tiles, wp[...], bp[...], ws[...], wt[...], spread_ones[...], ones[...]
        )
        live = jnp.concatenate(
            [jnp.full((TILE, WIDTH), label[first + j], jnp.int32) for j in range(unit)], axis=0
        ) >= 0
        kept = jnp.where(live, weights.astype(F32), 0.0)
        weights = kept.astype(BF16)
        sending[x, pl.ds(pl.multiple_of(s * rows, rows), rows), :] = weights
        numer[...] += lax.dot_general(
            weights, proj, (((0,), (0,)), ((), ())), preferred_element_type=F32
        )
        denom[...] += jnp.sum(kept.reshape(rows // 8, 8, WIDTH), axis=0)

    steps = (n - 1) * pieces
    held_from = (n - 1) * (pieces - 1)

    def encode_step(i, _):
        x = order(i % (n - 1))
        compute(x, partner(x), i // (n - 1))

        @pl.when((i > 0) & (i <= held_from))
        def _():
            piece_copy(order((i - 1) % (n - 1)), (i - 1) // (n - 1)).start()

        return 0

    lax.fori_loop(0, steps, encode_step, 0)

    def own_step(s, _):
        compute(0, me, s)
        return 0

    lax.fori_loop(0, pieces, own_step, 0)

    lane_head = lax.broadcasted_iota(jnp.int32, (FEAT, HALF), 1) // FEAT
    for a in range(2):
        acc = jnp.zeros((FEAT, HALF), F32)
        for j in range(4):
            part = numer[pl.ds((a * 4 + j) * FEAT, FEAT), pl.ds(a * HALF, HALF)]
            acc = acc + jnp.where(lane_head == j, part, 0.0)
        sums[0, pl.ds(a * FEAT, FEAT), :] = acc
        total = jnp.sum(denom[:, pl.ds(a * HALF, HALF)], axis=0, keepdims=True)
        sums[0, pl.ds(2 * FEAT + a * 8, 8), :] = jnp.broadcast_to(total, (8, HALF))

    def release(i, _):
        piece_copy(order(i - held_from), pieces - 1).start()
        return 0

    level, bit = 0, n // 2
    while bit > 0:
        swap = pltpu.make_async_remote_copy(
            src_ref=sums.at[level], dst_ref=inbox.at[level], send_sem=red_send.at[level],
            recv_sem=red_recv.at[level], device_id={"dom": partner(bit)}, device_id_type=MESH,
        )
        swap.start()
        swap.wait()
        sums[level + 1] = sums[level] + inbox[level]
        level, bit = level + 1, bit // 2
        if level == max(1, (n - 1).bit_length() - 2):
            lax.fori_loop(held_from, steps, release, 0)
    mixed[...] = mix(sums[level], qkv, head_ones[...])

    def out_copy(x, s):
        at = pl.ds(pl.multiple_of(s * rows, rows), rows)
        return pltpu.make_async_copy(arrived.at[x, at], result.at[partner(x), at], out_sem.at[x, s])

    def decode(read, x, s):
        at = pl.ds(pl.multiple_of(s * rows, rows), rows)
        deslice = jnp.dot(read[x, at, :], mixed[...], preferred_element_type=F32).astype(BF16)
        y = (jnp.dot(deslice, wo[...], preferred_element_type=F32) + bo[...]).astype(BF16)
        arrived[x, at, :] = y
        out_copy(x, s).start()

    def decode_own(s, _):
        decode(sending, 0, s)
        return 0

    lax.fori_loop(0, pieces, decode_own, 0)

    def from_peer(i, _):
        x, s = order(i % (n - 1)), i // (n - 1)
        piece_copy(x, s).wait_recv()
        decode(arrived, x, s)
        return 0

    lax.fori_loop(0, steps, from_peer, 0)

    def finish(x, _):
        def one(s, _):
            piece_copy(x, s).wait_send()
            return 0

        lax.fori_loop(0, pieces, one, 0)
        lab_copy(x).wait()
        return 0

    lax.fori_loop(1, n, finish, 0)
    own_lab.wait()

    def drain(i, _):
        out_copy(i // pieces, i % pieces).wait()
        return 0

    lax.fori_loop(0, n * pieces, drain, 0)


def mix(stats, qkv, ones):
    row_head = lax.broadcasted_iota(jnp.int32, (HALF, HALF), 0) // FEAT
    lane_head = lax.broadcasted_iota(jnp.int32, (HALF, HALF), 1) // FEAT
    same = row_head == lane_head
    blocks = []
    for a in range(2):
        numer = stats[a * FEAT:(a + 1) * FEAT, :]
        row = stats[2 * FEAT + a * 8:2 * FEAT + (a + 1) * 8, :]
        col = jnp.transpose(jnp.broadcast_to(row[:1], (HALF, HALF)))
        spread = jnp.zeros((FEAT, HALF), F32)
        for j in range(4):
            spread = spread + jnp.where(
                lane_head[:FEAT] == j, col[j * FEAT:(j + 1) * FEAT, :], 0.0
            )
        tokens = numer / (spread + 1e-05)
        dot = functools.partial(jnp.dot, preferred_element_type=F32, precision=HIGHEST)
        query, keys, values = (dot(tokens, qkv[i]) for i in range(3))
        spread_keys = jnp.where(same, jnp.concatenate([keys] * 4, axis=0), 0.0)
        scores = lax.dot_general(
            query, spread_keys, (((1,), (1,)), ((), ())), preferred_element_type=F32, precision=HIGHEST
        ) * FEAT ** (-0.5)
        raised = jnp.exp(scores)
        attend = raised / dot(raised, ones)
        spread_values = jnp.where(same, jnp.concatenate([values] * 4, axis=0), 0.0)
        mixed = dot(attend, spread_values)
        blocks.append(jnp.where(same, jnp.concatenate([mixed] * 4, axis=0), 0.0))
    nil = jnp.zeros((HALF, HALF), F32)
    return jnp.concatenate(
        [jnp.concatenate([blocks[0], nil], axis=1), jnp.concatenate([nil, blocks[1]], axis=1)], axis=0
    ).astype(BF16)


def place_kernel(n, per_peer, chunks, per_chunk, labels, tiles, out, held, in_sem, out_sem):
    def load(k, _):
        def one(t, _):
            slot = labels[k, t]

            @pl.when(slot >= 0)
            def _():
                pltpu.make_async_copy(
                    tiles.at[k * per_peer + t], held.at[slot], in_sem.at[slot // per_chunk]
                ).start()

            return 0

        return lax.fori_loop(0, per_peer, one, 0)

    lax.fori_loop(0, n, load, 0)

    def step(c, _):
        part = pl.ds(c * per_chunk, per_chunk)
        pltpu.make_async_copy(tiles.at[pl.ds(0, per_chunk)], held.at[part], in_sem.at[c]).wait()
        pltpu.make_async_copy(held.at[part], out.at[part], out_sem.at[c]).start()
        return 0

    lax.fori_loop(0, chunks, step, 0)

    def finish(c, _):
        part = pl.ds(c * per_chunk, per_chunk)
        pltpu.make_async_copy(held.at[part], out.at[part], out_sem.at[c]).wait()
        return 0

    lax.fori_loop(0, chunks, finish, 0)


def plan(destination, own_count, n):
    slots = destination.shape[0]
    per_peer = slots // n
    index = jnp.arange(slots, dtype=jnp.int32)
    live = index < own_count
    target = jnp.where(live, destination // LAND, -1)
    slot = jnp.where(live, destination % LAND, -1)
    earlier = (target[:, None] == target[None, :]) & live[None, :] & (index[None, :] < index[:, None])
    rank = jnp.sum(earlier.astype(jnp.int32), axis=1)
    place = target * per_peer + rank
    matches = live[None, :] & (place[None, :] == index[:, None])
    source = jnp.sum(jnp.where(matches, index[None, :], 0), axis=1)
    label = jnp.sum(jnp.where(matches, slot[None, :] + 1, 0), axis=1) - 1
    return source, label


def direct(n, points, counts, destination, wp, bp, slice_weight, softness, qkv, wo, bo):
    slots = points.shape[0] // TILE
    per_peer = slots // n
    any_spec = pl.BlockSpec(memory_space=pl.ANY)
    vmem = pl.BlockSpec(memory_space=pltpu.VMEM)
    smem = pl.BlockSpec(memory_space=pltpu.SMEM)
    source, label = plan(destination, counts[0], n)
    rows = per_peer * TILE
    labels = jnp.pad(label.reshape(n, 1, per_peer), ((0, 0), (0, 0), (0, HALF - per_peer)))
    unit = 2 if per_peer % 2 == 0 else 1
    pieces = per_peer // unit
    levels = (n - 1).bit_length()
    stat_rows = 2 * FEAT + 16
    dma = pltpu.SemaphoreType.DMA
    tiles, arrived_lab = pl.pallas_call(
        functools.partial(move_kernel, n, per_peer, unit),
        out_shape=(
            jax.ShapeDtypeStruct((n, rows, WIDTH), BF16),
            jax.ShapeDtypeStruct((n, 1, HALF), jnp.int32),
        ),
        in_specs=[smem, smem, any_spec, any_spec] + [vmem] * 7,
        out_specs=(any_spec, any_spec),
        scratch_shapes=[
            pltpu.VMEM((slots, TILE, WIDTH), BF16),
            pltpu.VMEM((n, rows, WIDTH), BF16),
            pltpu.VMEM((n, rows, WIDTH), BF16),
            pltpu.VMEM((WIDTH, WIDTH), F32),
            pltpu.VMEM((8, WIDTH), F32),
            pltpu.VMEM((levels + 1, stat_rows, HALF), F32),
            pltpu.VMEM((levels, stat_rows, HALF), F32),
            pltpu.VMEM((WIDTH, WIDTH), BF16),
            pltpu.VMEM((WIDTH, WIDTH), BF16),
            pltpu.VMEM((WIDTH, HALF), BF16),
            pltpu.VMEM((HALF, WIDTH), BF16),
            pltpu.VMEM((WIDTH, WIDTH), BF16),
            pltpu.VMEM((HALF, HALF), F32),
            pltpu.VMEM((3, HALF, HALF), F32),
            dma, dma((n, pieces)), dma((n, pieces)), dma((n,)), dma((n,)), dma, dma((n, pieces)),
            dma((levels,)), dma((levels,)),
        ],
        compiler_params=pltpu.CompilerParams(
            collective_id=15, has_side_effects=True, vmem_limit_bytes=60 << 20
        ),
        name="move",
    )(
        source, label, points.reshape(slots, TILE, WIDTH), labels, wp, bp.reshape(1, WIDTH),
        slice_weight, softness.reshape(1, FEAT), qkv, wo, bo.reshape(1, WIDTH),
    )

    per_chunk = 8
    chunks = LAND // per_chunk
    placed = pl.pallas_call(
        functools.partial(place_kernel, n, per_peer, chunks, per_chunk),
        out_shape=jax.ShapeDtypeStruct((LAND, TILE, WIDTH), BF16),
        grid_spec=pltpu.PrefetchScalarGridSpec(
            num_scalar_prefetch=1, grid=(), in_specs=[any_spec], out_specs=any_spec,
            scratch_shapes=[pltpu.VMEM((LAND, TILE, WIDTH), BF16), dma((chunks,)), dma((chunks,))],
        ),
        compiler_params=pltpu.CompilerParams(vmem_limit_bytes=60 << 20),
        name="place",
    )(arrived_lab.reshape(n, HALF), tiles.reshape(slots, TILE, WIDTH))
    return placed.reshape(LAND * TILE, WIDTH)


def mirror(me, n):
    steps, bit = [], 1
    while bit < n:
        steps.append((bit, bit - 2 * bit * (me // bit % 2)))
        bit = bit * 2

    def peer(x):
        out = me
        for bit, step in steps:
            if isinstance(x, int):
                out = out + step if x & bit else out
            else:
                out = out + step * (x // bit % 2)
        return out

    return peer


def tell_kernel(n, groups, rows, got, send_sem, recv_sem, own_sem):
    me, group = lax.axis_index("dom"), lax.axis_index("groups")
    near = groups * PLANE
    mine = me // PLANE * near
    peer, other = mirror(me, n), mirror(group, groups)
    barrier = pltpu.get_barrier_semaphore()

    def device(x):
        return {"groups": other(x // n), "dom": peer(x % n)}

    for x in range(1, n * groups):
        pl.semaphore_signal(barrier, inc=1, device_id=device(x), device_id_type=MESH)
    own = pltpu.make_async_copy(rows.at[0], got.at[mine], own_sem)
    own.start()
    pl.semaphore_wait(barrier, n * groups - 1)

    def tell(x):
        w = x % PLANE
        return pltpu.make_async_remote_copy(
            src_ref=rows.at[w], dst_ref=got.at[mine + x // n * PLANE + w], send_sem=send_sem.at[x],
            recv_sem=recv_sem.at[x], device_id=device(x), device_id_type=MESH,
        )

    copies = [tell(x) for x in range(1, n * groups)]
    for copy in copies:
        copy.start()
    for copy in copies:
        copy.wait()
    own.wait()


def encoded(i):
    return (2 * i + 1) // 3


def due(w, j):
    step = PLANE * j + ENCODE_ORDER.index(w)
    if w == 0:
        return ((2 * step + 1) * 171) >> 9
    if w == 1:
        return ((2 * step + 4) * 171) >> 9
    return 5 * j + (4 if ENCODE_ORDER.index(w) < ENCODE_ORDER.index(5 - w) else 7)


def timetable(sizes):
    starts, longest = {}, 0
    firsts = {}
    for zo in range(LINE):
        for w in range(PLANE):
            total = 0
            for zd in DEST_ORDER[zo]:
                if zd != zo:
                    firsts[zo, w, zd] = total
                    total = total + sizes[zo, w, zd]
    for way in range(2):
        def real(cl):
            return (LINE - 1 - cl[0], cl[1], LINE - 1 - cl[2]) if way else cl

        for lane, order in enumerate(LANES):
            pos = 0
            for cl in order:
                size = sizes[real(cl)]
                if cl[0] == lane:
                    begin = firsts[real(cl)]
                    last = ((begin + size - 1) * 13) >> 6
                    slack = CHUNK * last - begin - (1 if cl[1] < 2 else 0)
                    ready = STEP * due(cl[1], last) - jnp.maximum(0, slack)
                else:
                    ready = starts[way, lane - 1, cl] + HOP * STEP
                start = jnp.maximum(pos, jnp.where(size > 0, ready, 0))
                starts[way, lane, cl] = start
                pos = start + size
            longest = jnp.maximum(longest, pos)
    return starts, longest


def table_kernel(n, groups, per_peer, got, wide, sends, slots, branch, starts):
    z = lax.axis_index("dom") // PLANE
    flow = LINE * per_peer
    near = groups * PLANE
    table = HALF

    def clear(i, _):
        for k in range(8):
            sends[0, i * 8 + k] = 0
            sends[1, i * 8 + k] = 0
        return 0

    lax.fori_loop(0, table // 8, clear, 0)

    sizes = {
        (zo, w, zd): got[zo * near + w, flow + w * LINE + zd]
        for zo in range(LINE) for w in range(PLANE) for zd in range(LINE)
    }
    mine, _ = timetable(sizes)
    for way in range(2):
        for lane, order in enumerate(LANES):
            for at, cl in enumerate(order):
                starts[way, lane, at] = mine[way, lane, cl]

    full = jnp.concatenate([wide[...], jnp.zeros((HALF - wide.shape[0], HALF), jnp.int32)], axis=0)
    turned = jnp.transpose(full)
    lanes = lax.broadcasted_iota(jnp.int32, (LINE, HALF), 1)
    every = {}
    for w in range(PLANE):
        block = turned[flow + w * LINE:flow + (w + 1) * LINE]
        for bit in (1, 2):
            if w & bit:
                block = jnp.where(
                    lanes // bit % 2 == 0, pltpu.roll(block, HALF - bit, 1), pltpu.roll(block, bit, 1)
                )
        for zo in range(LINE):
            moved = pltpu.roll(block, HALF - zo * near, 1) if zo else block
            for zd in range(LINE):
                every[zo, w, zd] = jnp.broadcast_to(moved[zd:zd + 1], (8, HALF))
    _, longest = timetable(every)
    lanes = lax.broadcasted_iota(jnp.int32, (8, HALF), 1)
    longest = jnp.max(jnp.where(lanes < near, longest, 0))
    choice = jnp.int32(0)
    for limit in LIMITS:
        choice = choice + jnp.where(longest > limit, 1, 0)
    branch[0] = choice

    def fill(me):
        def row(zo, w):
            return zo * near + w

        def size_of(zo, w, zd):
            return got[row(zo, w), flow + w * LINE + zd]

        def first_of(zo, w, zd):
            total = jnp.int32(0)
            for real in DEST_ORDER[zo]:
                if real == zd:
                    return total
                total = total + size_of(zo, w, real)

        for way in range(2):
            def plane(p):
                return LINE - 1 - p if way else p

            lane = plane(me)
            if lane == LINE - 1:
                continue
            landed = PLANE * flow + way * ROOM
            for at, cl in enumerate(LANES[lane]):
                zo, w, zd = plane(cl[0]), cl[1], plane(cl[2])
                if zo == me:
                    source = w * flow + first_of(zo, w, zd)
                else:
                    source = landed + starts[way, lane - 1, LANES[lane - 1].index(cl)]
                size = size_of(zo, w, zd)
                start = jnp.minimum(starts[way, lane, at], ROOM)
                for k in range(per_peer):
                    sends[way, start + k] = jnp.where(k < size, source + k, 0)
        for zo in range(LINE):
            for w in range(PLANE):
                first = first_of(zo, w, me)
                size = size_of(zo, w, me)
                if zo == me:
                    source = w * flow + first
                else:
                    way = 0 if zo < me else 1
                    lane = me - 1 if zo < me else LINE - 2 - me
                    cl = (zo, w, me) if zo < me else (LINE - 1 - zo, w, LINE - 1 - me)
                    source = PLANE * flow + way * ROOM + starts[way, lane, LANES[lane].index(cl)]
                for k in range(per_peer):
                    label = got[row(zo, w), first + k]
                    slots[jnp.where(k < size, label + 1, 0)] = source + k

    for me in range(LINE):
        @pl.when(z == me)
        def _():
            fill(me)


def relay_kernel(
    n, per_peer, limit, source, label, sends, slots, points, wp, bp, slice_weight, softness, qkv_small,
    wo, bo, result,
    held, pool, sending, landed, stage, landing, numer, denom, sums, inbox, mixed,
    ws, wt, spread_ones, ones, head_ones, qkv,
    point_sem, plane_send, plane_recv, line_send, line_recv, red_send, red_recv, out_sem,
):
    me = lax.axis_index("dom")
    z = me // PLANE
    peer = mirror(me, n)
    flow = LINE * per_peer
    chunks = flow // CHUNK
    rounds = limit // STEP
    fetch = pltpu.make_async_copy(points, held, point_sem)
    fetch.start()
    barrier = pltpu.get_barrier_semaphore()
    for x in range(1, n):
        pl.semaphore_signal(barrier, inc=1, device_id={"dom": peer(x)}, device_id_type=MESH)
    numer[...] = jnp.zeros_like(numer)
    denom[...] = jnp.zeros_like(denom)
    build(slice_weight, softness, qkv_small, ws, wt, spread_ones, ones, head_ones, qkv)
    pl.semaphore_wait(barrier, n - 1)
    fetch.wait()

    def plane_copy(w, j):
        return pltpu.make_async_remote_copy(
            src_ref=sending.at[w - 1, j], dst_ref=landed.at[w - 1, j], send_sem=plane_send.at[w - 1, j],
            recv_sem=plane_recv.at[w - 1, j], device_id={"dom": peer(w)},
            device_id_type=MESH,
        )

    def line_copy(way, r):
        slot = r % RING
        near = me + PLANE if way == 0 else me - PLANE
        return pltpu.make_async_remote_copy(
            src_ref=stage.at[way, slot], dst_ref=landing.at[way, slot], send_sem=line_send.at[way, slot],
            recv_sem=line_recv.at[way, slot], device_id={"dom": near}, device_id_type=MESH,
        )

    can_send = (z < LINE - 1, z > 0)
    can_recv = (z > 0, z < LINE - 1)

    def encode(i, _):
        j, turn = i // PLANE, i % PLANE
        w = ENCODE_ORDER[0]
        for at in range(1, PLANE):
            w = jnp.where(turn == at, ENCODE_ORDER[at], w)
        first = w * flow + j * CHUNK
        tiles = jnp.concatenate([held[source[first + k]] for k in range(CHUNK)], axis=0)
        proj, weights = encode_rows(
            tiles, wp[...], bp[...], ws[...], wt[...], spread_ones[...], ones[...]
        )
        live = jnp.concatenate(
            [jnp.full((TILE, WIDTH), label[first + k], jnp.int32) for k in range(CHUNK)], axis=0
        ) >= 0
        kept = jnp.where(live, weights.astype(F32), 0.0)
        weights = kept.astype(BF16)
        numer[...] += lax.dot_general(
            weights, proj, (((0,), (0,)), ((), ())), preferred_element_type=F32
        )
        denom[...] += jnp.sum(kept.reshape(CHUNK * TILE // 8, 8, WIDTH), axis=0)
        weights = weights.reshape(CHUNK, TILE, WIDTH)

        @pl.when(turn == 0)
        def _():
            pool[pl.ds(j * CHUNK, CHUNK)] = weights

        @pl.when(turn > 0)
        def _():
            sending[w - 1, j] = weights

        @pl.when(turn == ENCODE_ORDER.index(1))
        def _():
            plane_copy(1, j).start()

        return 0

    def line_arrive(way, m):
        line_copy(way, m).wait_recv()
        pool[pl.ds(PLANE * flow + way * ROOM + m * STEP, STEP)] = landing[way, m % RING]

    def release(w, r):
        begin, first = due(w, 0) - 5, encoded(ENCODE_ORDER.index(w))
        since = r - begin
        j = since // 5
        now = (since % 5 == 0) & (j >= 0) & (j < chunks)
        if begin < first:
            now = (now & (j > 0)) | (r == first)
            j = jnp.where(r == first, 0, j)

        @pl.when(now)
        def _():
            plane_copy(w, j).start()

    def relay(r):
        for w in range(2, PLANE):
            release(w, r)
        for way in range(2):
            @pl.when(can_recv[way] & (r >= HOP))
            def _():
                line_arrive(way, r - HOP)
        for w in range(1, PLANE):
            if w == 1:
                late = 2 * ENCODE_ORDER.index(w) + 4
                j = (3 * r + 7 - late) // 8
                now = (3 * r + 7 >= late) & ((8 * j + late) // 3 == r)
            else:
                since = r - due(w, 0)
                j = since // 5
                now = (since >= 0) & (since % 5 == 0)

            @pl.when(now & (j < chunks))
            def _():
                plane_copy(w, j).wait_recv()
                pool[pl.ds(w * flow + j * CHUNK, CHUNK)] = landed[w - 1, j]

        for way in range(2):
            @pl.when(can_send[way])
            def _():
                @pl.when(r >= RING)
                def _():
                    line_copy(way, r - RING).wait_send()

                for k in range(STEP):
                    stage[way, r % RING, k] = pool[sends[way, r * STEP + k]]
                line_copy(way, r).start()

    steps = PLANE * chunks

    reached = encoded(steps - 1) + 1
    levels = sums.shape[0] - 1
    group = LAND // (2 * LAST)
    early = rounds - LAST
    seen = (early - HOP + 1) * STEP
    rest = limit - seen

    def swap(level):
        return pltpu.make_async_remote_copy(
            src_ref=sums.at[level], dst_ref=inbox.at[level], send_sem=red_send.at[level],
            recv_sem=red_recv.at[level], device_id={"dom": peer(n >> (level + 1))}, device_id_type=MESH,
        )

    def own_sums():
        lane_head = lax.broadcasted_iota(jnp.int32, (FEAT, HALF), 1) // FEAT
        for a in range(2):
            acc = jnp.zeros((FEAT, HALF), F32)
            for j in range(4):
                part = numer[pl.ds((a * 4 + j) * FEAT, FEAT), pl.ds(a * HALF, HALF)]
                acc = acc + jnp.where(lane_head == j, part, 0.0)
            sums[0, pl.ds(a * FEAT, FEAT), :] = acc
            total = jnp.sum(denom[:, pl.ds(a * HALF, HALF)], axis=0, keepdims=True)
            sums[0, pl.ds(2 * FEAT + a * 8, 8), :] = jnp.broadcast_to(total, (8, HALF))

    def decode(rows):
        deslice = jnp.dot(rows, mixed[...], preferred_element_type=F32).astype(BF16)
        y = (jnp.dot(deslice, wo[...], preferred_element_type=F32) + bo[...]).astype(BF16)
        return y.reshape(rows.shape[0] // TILE, TILE, WIDTH)

    def decode_slots(i, _):
        rows = jnp.concatenate([pool[slots[i * group + k + 1]] for k in range(group)], axis=0)
        held[pl.ds(i * group, group)] = decode(rows)
        return 0

    def one_round(r, _):
        @pl.when(r < reached)
        def _():
            lax.fori_loop(3 * r // 2, jnp.minimum(3 * (r + 1) // 2, steps), encode, 0)

        @pl.when(r == reached)
        def _():
            own_sums()
            swap(0).start()

        for level in range(levels):
            @pl.when(r == reached + 4 * (level + 1))
            def _():
                swap(level).wait()
                sums[level + 1] = sums[level] + inbox[level]
                if level + 1 < levels:
                    swap(level + 1).start()
                else:
                    mixed[...] = mix(sums[levels], qkv, head_ones[...])

        relay(r)

        @pl.when(r >= early)
        def _():
            lax.fori_loop(2 * (r - early), 2 * (r - early) + 2, decode_slots, 0)

        return 0

    lax.fori_loop(0, rounds, one_round, 0)
    for way in range(2):
        @pl.when(can_recv[way])
        def _():
            def arrive(m, _):
                line_arrive(way, m)
                return 0

            lax.fori_loop(rounds - HOP, rounds, arrive, 0)

    half = rest // 2

    def decode_rest(i, _):
        begin = PLANE * flow + i // 2 * ROOM + seen + i % 2 * half
        rows = pool[pl.ds(begin, half)].reshape(half * TILE, WIDTH)
        held[pl.ds(LAND + i * half, half)] = decode(rows)
        return 0

    lax.fori_loop(0, 4, decode_rest, 0)

    def out_copy(i):
        return pltpu.make_async_copy(
            landed.at[i // chunks, i % chunks], result.at[pl.ds(i * CHUNK, CHUNK)], out_sem.at[i]
        )

    def finish(i, _):
        for k in range(CHUNK):
            at = i * CHUNK + k
            where = slots[at + 1] - PLANE * flow
            way = jnp.where(where >= ROOM, 1, 0)
            pos = where - way * ROOM - seen
            late = (where >= 0) & (pos >= 0)
            landed[i // chunks, i % chunks, k] = held[jnp.where(late, LAND + way * rest + pos, at)]
        out_copy(i).start()
        return 0

    lax.fori_loop(0, LAND // CHUNK, finish, 0)

    for way in range(2):
        @pl.when(can_send[way])
        def _():
            def sent(r, _):
                line_copy(way, r).wait_send()
                return 0

            lax.fori_loop(rounds - RING, rounds, sent, 0)

    def plane_sent(i, _):
        plane_copy(1 + i % (PLANE - 1), i // (PLANE - 1)).wait_send()
        return 0

    lax.fori_loop(0, (PLANE - 1) * chunks, plane_sent, 0)

    def drain(i, _):
        out_copy(i).wait()
        return 0

    lax.fori_loop(0, LAND // CHUNK, drain, 0)


def arrange(destination, own_count, n, me):
    slots = destination.shape[0]
    flow = slots // PLANE
    index = jnp.arange(slots, dtype=jnp.int32)
    live = index < own_count
    target, slot = destination // LAND, destination % LAND
    w = (target % PLANE) ^ (me % PLANE)
    line, own = target // PLANE, me // PLANE
    upper = own >= LINE // 2
    far = jnp.where(upper, LINE - 1 - line, line)
    near = jnp.where(upper, LINE - 1 - own, own)
    rank = jnp.where(
        far > near, LINE - 1 - far, jnp.where(far < near, LINE - 1 - near + far, LINE - 1)
    )
    w = jnp.where(live, w, -1)
    key = rank * slots + index
    earlier = (w[:, None] == w[None, :]) & (key[None, :] < key[:, None])
    place = w * flow + jnp.sum(earlier.astype(jnp.int32), axis=1)
    matches = live[None, :] & (place[None, :] == index[:, None])
    source = jnp.sum(jnp.where(matches, index[None, :], 0), axis=1)
    label = jnp.sum(jnp.where(matches, slot[None, :] + 1, 0), axis=1) - 1
    kind = jnp.where(live, w * LINE + line, -1)
    kinds = jnp.arange(PLANE * LINE, dtype=jnp.int32)
    sizes = jnp.sum((kind[None, :] == kinds[:, None]).astype(jnp.int32), axis=1)
    return source, label, sizes


def relayed(n, groups, points, counts, destination, wp, bp, slice_weight, softness, qkv, wo, bo):
    slots = points.shape[0] // TILE
    per_peer = slots // n
    flow = slots // PLANE
    any_spec = pl.BlockSpec(memory_space=pl.ANY)
    vmem = pl.BlockSpec(memory_space=pltpu.VMEM)
    smem = pl.BlockSpec(memory_space=pltpu.SMEM)
    dma = pltpu.SemaphoreType.DMA
    source, label, sizes = arrange(destination, counts[0], n, lax.axis_index("dom"))
    rows = jnp.concatenate(
        [label.reshape(PLANE, flow), jnp.broadcast_to(sizes[None], (PLANE, PLANE * LINE))], axis=1
    )
    rows = jnp.pad(rows, ((0, 0), (0, HALF - rows.shape[1]))).reshape(PLANE, 1, HALF)
    got = pl.pallas_call(
        functools.partial(tell_kernel, n, groups),
        out_shape=jax.ShapeDtypeStruct((groups * n, 1, HALF), jnp.int32),
        in_specs=[any_spec], out_specs=any_spec,
        scratch_shapes=[dma((n * groups,)), dma((n * groups,)), dma],
        compiler_params=pltpu.CompilerParams(collective_id=0, has_side_effects=True),
        name="tell",
    )(rows)
    sends, places, branch = pl.pallas_call(
        functools.partial(table_kernel, n, groups, per_peer),
        out_shape=(
            jax.ShapeDtypeStruct((2, HALF), jnp.int32),
            jax.ShapeDtypeStruct((LAND + 1,), jnp.int32),
            jax.ShapeDtypeStruct((1,), jnp.int32),
        ),
        in_specs=[smem, vmem], out_specs=(smem, smem, smem),
        scratch_shapes=[pltpu.SMEM((2, LINE - 1, PLANE * LINE), jnp.int32)],
        name="table",
    )(got.reshape(groups * n, HALF), got.reshape(groups * n, HALF))

    levels = (n - 1).bit_length()
    stat_rows = 2 * FEAT + 16
    tile = (TILE, WIDTH)

    def relay(limit, at, *_):
        placed = pl.pallas_call(
            functools.partial(relay_kernel, n, per_peer, limit),
            out_shape=jax.ShapeDtypeStruct((LAND,) + tile, BF16),
            in_specs=[smem] * 4 + [any_spec] + [vmem] * 7,
            out_specs=any_spec,
            scratch_shapes=[
                pltpu.VMEM((slots,) + tile, BF16),
                pltpu.VMEM((slots + 2 * ROOM,) + tile, BF16),
                pltpu.VMEM((PLANE - 1, flow // CHUNK, CHUNK) + tile, BF16),
                pltpu.VMEM((PLANE - 1, flow // CHUNK, CHUNK) + tile, BF16),
                pltpu.VMEM((2, RING, STEP) + tile, BF16),
                pltpu.VMEM((2, RING, STEP) + tile, BF16),
                pltpu.VMEM((WIDTH, WIDTH), F32),
                pltpu.VMEM((8, WIDTH), F32),
                pltpu.VMEM((levels + 1, stat_rows, HALF), F32),
                pltpu.VMEM((levels, stat_rows, HALF), F32),
                pltpu.VMEM((WIDTH, WIDTH), BF16),
                pltpu.VMEM((WIDTH, WIDTH), BF16),
                pltpu.VMEM((WIDTH, HALF), BF16),
                pltpu.VMEM((HALF, WIDTH), BF16),
                pltpu.VMEM((WIDTH, WIDTH), BF16),
                pltpu.VMEM((HALF, HALF), F32),
                pltpu.VMEM((3, HALF, HALF), F32),
                dma, dma((PLANE - 1, flow // CHUNK)), dma((PLANE - 1, flow // CHUNK)),
                dma((2, RING)), dma((2, RING)), dma((levels,)), dma((levels,)), dma((LAND // CHUNK,)),
            ],
            compiler_params=pltpu.CompilerParams(
                collective_id=1 + at, has_side_effects=True, vmem_limit_bytes=62 << 20
            ),
            name="relay" + str(limit),
        )(
            source, label, sends, places, points.reshape((slots,) + tile), wp, bp.reshape(1, WIDTH),
            slice_weight, softness.reshape(1, FEAT), qkv, wo, bo.reshape(1, WIDTH),
        )
        return placed.reshape(LAND * TILE, WIDTH)

    def fallback():
        return direct(n, points, counts, destination, wp, bp, slice_weight, softness, qkv, wo, bo)

    branches = [functools.partial(relay, limit, at) for at, limit in enumerate(LIMITS)]
    return lax.switch(branch[0], branches + [fallback])


def solution(mesh):
    spec = P(("groups", "dom"))
    wide = P(("groups", "dom"), None)
    n, groups = mesh.shape["dom"], mesh.shape["groups"]
    if n == PLANE * LINE and groups == 2:
        body = functools.partial(relayed, n, groups)
    else:
        body = functools.partial(direct, n)
    return jax.shard_map(
        body, mesh=mesh, in_specs=(wide, spec, spec) + (P(),) * 7, out_specs=wide, check_vma=False,
    )
```

```python
import functools

import jax
import jax.numpy as jnp
from jax import lax
from jax.experimental import pallas as pl
from jax.experimental.pallas import tpu as pltpu
from jax.sharding import PartitionSpec as P

WIDTH = 256
HEADS = 8
FEAT = 32
TILE = 128
LAND = 80
HALF = 128
PLANE = 4
LINE = 4
CHUNK = 5
STEP = 2
HOP = 2
RING = 4
LIMITS = (94, 102, 104, 124)
ROOM = LIMITS[-1]
ENCODE_ORDER = (0, 1, 2, 3)
LAST = 5
DEST_ORDER = ((3, 2, 1, 0), (3, 2, 0, 1), (0, 1, 3, 2), (0, 1, 2, 3))
LANES = (
    ((0, 0, 3), (0, 0, 2), (0, 1, 3), (0, 2, 3), (0, 3, 3), (0, 1, 2), (0, 2, 2), (0, 3, 2), (0, 2, 1), (0, 0, 1), (0, 1, 1), (0, 3, 1)),
    ((1, 0, 3), (1, 0, 2), (1, 1, 3), (0, 0, 3), (0, 0, 2), (0, 1, 3), (1, 2, 3), (1, 3, 3), (1, 1, 2), (0, 2, 3), (0, 3, 3), (1, 3, 2), (1, 2, 2), (0, 2, 2), (0, 3, 2), (0, 1, 2)),
    ((1, 0, 3), (1, 1, 3), (2, 0, 3), (2, 1, 3), (0, 0, 3), (0, 1, 3), (1, 2, 3), (1, 3, 3), (0, 2, 3), (2, 3, 3), (0, 3, 3), (2, 2, 3)),
)
MESH = pl.DeviceIdType.MESH
HIGHEST = lax.Precision.HIGHEST
F32 = jnp.float32
BF16 = jnp.bfloat16


def split(x):
    high = x.astype(BF16)
    return high, x - high.astype(F32)


def encode_rows(x, wp, bp, ws, wt, spread_ones, ones):
    x = x.astype(F32)
    centred = x - jnp.sum(x, axis=-1, keepdims=True) * (1.0 / WIDTH)
    spread = jnp.sum(centred * centred, axis=-1, keepdims=True) * (1.0 / WIDTH)
    normed = (centred * lax.rsqrt(spread + 1e-05)).astype(BF16)
    dot = functools.partial(jnp.dot, preferred_element_type=F32)
    proj = (dot(normed, wp) + bp).astype(BF16)
    logits = dot(proj, ws)
    soft = dot(proj, wt)
    temper = 0.5 + (jnp.maximum(soft, 0.0) + jnp.log1p(jnp.exp(-jnp.abs(soft))))
    first, rest = split(1.0 / temper)
    second, rest = split(rest)
    lane = lax.broadcasted_iota(jnp.int32, soft.shape, 1)
    parts = jnp.where(lane < HEADS, first.astype(F32), jnp.where(lane < 2 * HEADS, second.astype(F32), rest))
    scale = dot(parts.astype(BF16), spread_ones)
    raised = jnp.exp(logits * scale)
    first, rest = split(raised)
    total = dot(first, ones) + dot(rest.astype(BF16), ones)
    return proj, (raised / total).astype(BF16)


def diagonal(block, times):
    wide = jnp.concatenate([block] * times, axis=1)
    full = jnp.concatenate([wide] * times, axis=0)
    size = times * FEAT
    row = lax.broadcasted_iota(jnp.int32, (size, size), 0) // FEAT
    lane = lax.broadcasted_iota(jnp.int32, (size, size), 1) // FEAT
    return jnp.where(row == lane, full, 0.0)


def build(slice_weight, softness, qkv_small, ws, wt, spread_ones, ones, head_ones, qkv):
    ws[...] = diagonal(slice_weight[...].astype(F32), HEADS).astype(BF16)
    for i in range(3):
        qkv[i] = diagonal(qkv_small[i], 4)
    unity = jnp.ones((FEAT, FEAT), F32)
    ones[...] = diagonal(unity, HEADS).astype(BF16)
    head_ones[...] = diagonal(unity, 4)
    row = lax.broadcasted_iota(jnp.int32, (HALF, WIDTH), 0)
    lane = lax.broadcasted_iota(jnp.int32, (HALF, WIDTH), 1) // FEAT
    spread_ones[...] = jnp.where((row % HEADS == lane) & (row < 3 * HEADS), 1.0, 0.0).astype(BF16)
    flat = jnp.concatenate([softness[...].astype(F32)] * 4, axis=1)
    tall = jnp.transpose(jnp.broadcast_to(flat, (HALF, HALF)))
    tall = jnp.concatenate([tall, tall], axis=0)
    row = lax.broadcasted_iota(jnp.int32, (WIDTH, HALF), 0) // FEAT
    lane = lax.broadcasted_iota(jnp.int32, (WIDTH, HALF), 1)
    wt[...] = jnp.where((row == lane % HEADS) & (lane < 3 * HEADS), tall, 0.0).astype(BF16)


def move_kernel(
    n, per_peer, unit, source, label, points, labels, wp, bp, slice_weight, softness, qkv_small,
    wo, bo, result, labels_out,
    held_points, sending, arrived, numer, denom, sums, inbox, mixed,
    ws, wt, spread_ones, ones, head_ones, qkv,
    point_sem, send_sem, recv_sem, lab_send, lab_recv, own_sem, out_sem, red_send, red_recv,
):
    me = lax.axis_index("dom")
    pieces = per_peer // unit
    rows = unit * TILE
    fetch = pltpu.make_async_copy(points, held_points, point_sem)
    fetch.start()

    def partner(x):
        peer, bit = 0, 1
        while bit < n:
            mine, flip = me // bit % 2, x // bit % 2
            peer = peer + bit * (mine + flip - 2 * mine * flip)
            bit = bit * 2
        return peer

    barrier = pltpu.get_barrier_semaphore()
    for x in range(1, n):
        pl.semaphore_signal(barrier, inc=1, device_id={"dom": partner(x)}, device_id_type=MESH)
    numer[...] = jnp.zeros_like(numer)
    denom[...] = jnp.zeros_like(denom)
    build(slice_weight, softness, qkv_small, ws, wt, spread_ones, ones, head_ones, qkv)
    pl.semaphore_wait(barrier, n - 1)

    def order(i):
        quarter = n // 4
        near = lax.rem(i, 2) * 2 * quarter
        early = 3 * quarter + i // 2 - near
        late = jnp.where(i < 3 * quarter, i, n - 1 - i)
        return jnp.where(i < 2 * quarter, early, late)

    def lab_copy(x):
        peer = partner(x)
        return pltpu.make_async_remote_copy(
            src_ref=labels.at[peer], dst_ref=labels_out.at[me], send_sem=lab_send.at[x],
            recv_sem=lab_recv.at[x], device_id={"dom": peer}, device_id_type=MESH,
        )

    def piece_copy(x, s):
        at = pl.ds(pl.multiple_of(s * rows, rows), rows)
        return pltpu.make_async_remote_copy(
            src_ref=sending.at[x, at], dst_ref=arrived.at[x, at], send_sem=send_sem.at[x, s],
            recv_sem=recv_sem.at[x, s], device_id={"dom": partner(x)}, device_id_type=MESH,
        )

    def lab_start(x, _):
        lab_copy(x).start()
        return 0

    lax.fori_loop(1, n, lab_start, 0)
    own_lab = pltpu.make_async_copy(labels.at[me], labels_out.at[me], own_sem)
    own_lab.start()
    fetch.wait()

    def compute(x, peer, s):
        first = peer * per_peer + s * unit
        tiles = jnp.concatenate([held_points[source[first + j]] for j in range(unit)], axis=0)
        proj, weights = encode_rows(
            tiles, wp[...], bp[...], ws[...], wt[...], spread_ones[...], ones[...]
        )
        live = jnp.concatenate(
            [jnp.full((TILE, WIDTH), label[first + j], jnp.int32) for j in range(unit)], axis=0
        ) >= 0
        kept = jnp.where(live, weights.astype(F32), 0.0)
        weights = kept.astype(BF16)
        sending[x, pl.ds(pl.multiple_of(s * rows, rows), rows), :] = weights
        numer[...] += lax.dot_general(
            weights, proj, (((0,), (0,)), ((), ())), preferred_element_type=F32
        )
        denom[...] += jnp.sum(kept.reshape(rows // 8, 8, WIDTH), axis=0)

    steps = (n - 1) * pieces
    held_from = (n - 1) * (pieces - 1)

    def encode_step(i, _):
        x = order(i % (n - 1))
        compute(x, partner(x), i // (n - 1))

        @pl.when((i > 0) & (i <= held_from))
        def _():
            piece_copy(order((i - 1) % (n - 1)), (i - 1) // (n - 1)).start()

        return 0

    lax.fori_loop(0, steps, encode_step, 0)

    def own_step(s, _):
        compute(0, me, s)
        return 0

    lax.fori_loop(0, pieces, own_step, 0)

    lane_head = lax.broadcasted_iota(jnp.int32, (FEAT, HALF), 1) // FEAT
    for a in range(2):
        acc = jnp.zeros((FEAT, HALF), F32)
        for j in range(4):
            part = numer[pl.ds((a * 4 + j) * FEAT, FEAT), pl.ds(a * HALF, HALF)]
            acc = acc + jnp.where(lane_head == j, part, 0.0)
        sums[0, pl.ds(a * FEAT, FEAT), :] = acc
        total = jnp.sum(denom[:, pl.ds(a * HALF, HALF)], axis=0, keepdims=True)
        sums[0, pl.ds(2 * FEAT + a * 8, 8), :] = jnp.broadcast_to(total, (8, HALF))

    def release(i, _):
        piece_copy(order(i - held_from), pieces - 1).start()
        return 0

    level, bit = 0, n // 2
    while bit > 0:
        swap = pltpu.make_async_remote_copy(
            src_ref=sums.at[level], dst_ref=inbox.at[level], send_sem=red_send.at[level],
            recv_sem=red_recv.at[level], device_id={"dom": partner(bit)}, device_id_type=MESH,
        )
        swap.start()
        swap.wait()
        sums[level + 1] = sums[level] + inbox[level]
        level, bit = level + 1, bit // 2
        if level == max(1, (n - 1).bit_length() - 2):
            lax.fori_loop(held_from, steps, release, 0)
    mixed[...] = mix(sums[level], qkv, head_ones[...])

    def out_copy(x, s):
        at = pl.ds(pl.multiple_of(s * rows, rows), rows)
        return pltpu.make_async_copy(arrived.at[x, at], result.at[partner(x), at], out_sem.at[x, s])

    def decode(read, x, s):
        at = pl.ds(pl.multiple_of(s * rows, rows), rows)
        deslice = jnp.dot(read[x, at, :], mixed[...], preferred_element_type=F32).astype(BF16)
        y = (jnp.dot(deslice, wo[...], preferred_element_type=F32) + bo[...]).astype(BF16)
        arrived[x, at, :] = y
        out_copy(x, s).start()

    def decode_own(s, _):
        decode(sending, 0, s)
        return 0

    lax.fori_loop(0, pieces, decode_own, 0)

    def from_peer(i, _):
        x, s = order(i % (n - 1)), i // (n - 1)
        piece_copy(x, s).wait_recv()
        decode(arrived, x, s)
        return 0

    lax.fori_loop(0, steps, from_peer, 0)

    def finish(x, _):
        def one(s, _):
            piece_copy(x, s).wait_send()
            return 0

        lax.fori_loop(0, pieces, one, 0)
        lab_copy(x).wait()
        return 0

    lax.fori_loop(1, n, finish, 0)
    own_lab.wait()

    def drain(i, _):
        out_copy(i // pieces, i % pieces).wait()
        return 0

    lax.fori_loop(0, n * pieces, drain, 0)


def mix(stats, qkv, ones):
    row_head = lax.broadcasted_iota(jnp.int32, (HALF, HALF), 0) // FEAT
    lane_head = lax.broadcasted_iota(jnp.int32, (HALF, HALF), 1) // FEAT
    same = row_head == lane_head
    blocks = []
    for a in range(2):
        numer = stats[a * FEAT:(a + 1) * FEAT, :]
        row = stats[2 * FEAT + a * 8:2 * FEAT + (a + 1) * 8, :]
        col = jnp.transpose(jnp.broadcast_to(row[:1], (HALF, HALF)))
        spread = jnp.zeros((FEAT, HALF), F32)
        for j in range(4):
            spread = spread + jnp.where(
                lane_head[:FEAT] == j, col[j * FEAT:(j + 1) * FEAT, :], 0.0
            )
        tokens = numer / (spread + 1e-05)
        dot = functools.partial(jnp.dot, preferred_element_type=F32, precision=HIGHEST)
        query, keys, values = (dot(tokens, qkv[i]) for i in range(3))
        spread_keys = jnp.where(same, jnp.concatenate([keys] * 4, axis=0), 0.0)
        scores = lax.dot_general(
            query, spread_keys, (((1,), (1,)), ((), ())), preferred_element_type=F32, precision=HIGHEST
        ) * FEAT ** (-0.5)
        raised = jnp.exp(scores)
        attend = raised / dot(raised, ones)
        spread_values = jnp.where(same, jnp.concatenate([values] * 4, axis=0), 0.0)
        mixed = dot(attend, spread_values)
        blocks.append(jnp.where(same, jnp.concatenate([mixed] * 4, axis=0), 0.0))
    nil = jnp.zeros((HALF, HALF), F32)
    return jnp.concatenate(
        [jnp.concatenate([blocks[0], nil], axis=1), jnp.concatenate([nil, blocks[1]], axis=1)], axis=0
    ).astype(BF16)


def place_kernel(n, per_peer, chunks, per_chunk, labels, tiles, out, held, in_sem, out_sem):
    def load(k, _):
        def one(t, _):
            slot = labels[k, t]

            @pl.when(slot >= 0)
            def _():
                pltpu.make_async_copy(
                    tiles.at[k * per_peer + t], held.at[slot], in_sem.at[slot // per_chunk]
                ).start()

            return 0

        return lax.fori_loop(0, per_peer, one, 0)

    lax.fori_loop(0, n, load, 0)

    def step(c, _):
        part = pl.ds(c * per_chunk, per_chunk)
        pltpu.make_async_copy(tiles.at[pl.ds(0, per_chunk)], held.at[part], in_sem.at[c]).wait()
        pltpu.make_async_copy(held.at[part], out.at[part], out_sem.at[c]).start()
        return 0

    lax.fori_loop(0, chunks, step, 0)

    def finish(c, _):
        part = pl.ds(c * per_chunk, per_chunk)
        pltpu.make_async_copy(held.at[part], out.at[part], out_sem.at[c]).wait()
        return 0

    lax.fori_loop(0, chunks, finish, 0)


def plan(destination, own_count, n):
    slots = destination.shape[0]
    per_peer = slots // n
    index = jnp.arange(slots, dtype=jnp.int32)
    live = index < own_count
    target = jnp.where(live, destination // LAND, -1)
    slot = jnp.where(live, destination % LAND, -1)
    earlier = (target[:, None] == target[None, :]) & live[None, :] & (index[None, :] < index[:, None])
    rank = jnp.sum(earlier.astype(jnp.int32), axis=1)
    place = target * per_peer + rank
    matches = live[None, :] & (place[None, :] == index[:, None])
    source = jnp.sum(jnp.where(matches, index[None, :], 0), axis=1)
    label = jnp.sum(jnp.where(matches, slot[None, :] + 1, 0), axis=1) - 1
    return source, label


def direct(n, points, counts, destination, wp, bp, slice_weight, softness, qkv, wo, bo):
    slots = points.shape[0] // TILE
    per_peer = slots // n
    any_spec = pl.BlockSpec(memory_space=pl.ANY)
    vmem = pl.BlockSpec(memory_space=pltpu.VMEM)
    smem = pl.BlockSpec(memory_space=pltpu.SMEM)
    source, label = plan(destination, counts[0], n)
    rows = per_peer * TILE
    labels = jnp.pad(label.reshape(n, 1, per_peer), ((0, 0), (0, 0), (0, HALF - per_peer)))
    unit = 2 if per_peer % 2 == 0 else 1
    pieces = per_peer // unit
    levels = (n - 1).bit_length()
    stat_rows = 2 * FEAT + 16
    dma = pltpu.SemaphoreType.DMA
    tiles, arrived_lab = pl.pallas_call(
        functools.partial(move_kernel, n, per_peer, unit),
        out_shape=(
            jax.ShapeDtypeStruct((n, rows, WIDTH), BF16),
            jax.ShapeDtypeStruct((n, 1, HALF), jnp.int32),
        ),
        in_specs=[smem, smem, any_spec, any_spec] + [vmem] * 7,
        out_specs=(any_spec, any_spec),
        scratch_shapes=[
            pltpu.VMEM((slots, TILE, WIDTH), BF16),
            pltpu.VMEM((n, rows, WIDTH), BF16),
            pltpu.VMEM((n, rows, WIDTH), BF16),
            pltpu.VMEM((WIDTH, WIDTH), F32),
            pltpu.VMEM((8, WIDTH), F32),
            pltpu.VMEM((levels + 1, stat_rows, HALF), F32),
            pltpu.VMEM((levels, stat_rows, HALF), F32),
            pltpu.VMEM((WIDTH, WIDTH), BF16),
            pltpu.VMEM((WIDTH, WIDTH), BF16),
            pltpu.VMEM((WIDTH, HALF), BF16),
            pltpu.VMEM((HALF, WIDTH), BF16),
            pltpu.VMEM((WIDTH, WIDTH), BF16),
            pltpu.VMEM((HALF, HALF), F32),
            pltpu.VMEM((3, HALF, HALF), F32),
            dma, dma((n, pieces)), dma((n, pieces)), dma((n,)), dma((n,)), dma, dma((n, pieces)),
            dma((levels,)), dma((levels,)),
        ],
        compiler_params=pltpu.CompilerParams(
            collective_id=15, has_side_effects=True, vmem_limit_bytes=60 << 20
        ),
        name="move",
    )(
        source, label, points.reshape(slots, TILE, WIDTH), labels, wp, bp.reshape(1, WIDTH),
        slice_weight, softness.reshape(1, FEAT), qkv, wo, bo.reshape(1, WIDTH),
    )

    per_chunk = 8
    chunks = LAND // per_chunk
    placed = pl.pallas_call(
        functools.partial(place_kernel, n, per_peer, chunks, per_chunk),
        out_shape=jax.ShapeDtypeStruct((LAND, TILE, WIDTH), BF16),
        grid_spec=pltpu.PrefetchScalarGridSpec(
            num_scalar_prefetch=1, grid=(), in_specs=[any_spec], out_specs=any_spec,
            scratch_shapes=[pltpu.VMEM((LAND, TILE, WIDTH), BF16), dma((chunks,)), dma((chunks,))],
        ),
        compiler_params=pltpu.CompilerParams(vmem_limit_bytes=60 << 20),
        name="place",
    )(arrived_lab.reshape(n, HALF), tiles.reshape(slots, TILE, WIDTH))
    return placed.reshape(LAND * TILE, WIDTH)


def mirror(me, n):
    steps, bit = [], 1
    while bit < n:
        steps.append((bit, bit - 2 * bit * (me // bit % 2)))
        bit = bit * 2

    def peer(x):
        out = me
        for bit, step in steps:
            if isinstance(x, int):
                out = out + step if x & bit else out
            else:
                out = out + step * (x // bit % 2)
        return out

    return peer


def tell_kernel(n, groups, rows, got, send_sem, recv_sem, own_sem):
    me, group = lax.axis_index("dom"), lax.axis_index("groups")
    near = groups * PLANE
    mine = me // PLANE * near
    peer, other = mirror(me, n), mirror(group, groups)
    barrier = pltpu.get_barrier_semaphore()

    def device(x):
        return {"groups": other(x // n), "dom": peer(x % n)}

    for x in range(1, n * groups):
        pl.semaphore_signal(barrier, inc=1, device_id=device(x), device_id_type=MESH)
    own = pltpu.make_async_copy(rows.at[0], got.at[mine], own_sem)
    own.start()
    pl.semaphore_wait(barrier, n * groups - 1)

    def tell(x):
        w = x % PLANE
        return pltpu.make_async_remote_copy(
            src_ref=rows.at[w], dst_ref=got.at[mine + x // n * PLANE + w], send_sem=send_sem.at[x],
            recv_sem=recv_sem.at[x], device_id=device(x), device_id_type=MESH,
        )

    copies = [tell(x) for x in range(1, n * groups)]
    for copy in copies:
        copy.start()
    for copy in copies:
        copy.wait()
    own.wait()


def encoded(i):
    return (2 * i + 1) // 3


def due(w, j):
    step = PLANE * j + ENCODE_ORDER.index(w)
    if w == 0:
        return ((2 * step + 1) * 171) >> 9
    if w == 1:
        return ((2 * step + 4) * 171) >> 9
    return 5 * j + (4 if ENCODE_ORDER.index(w) < ENCODE_ORDER.index(5 - w) else 7)


def timetable(sizes):
    starts, longest = {}, 0
    firsts = {}
    for zo in range(LINE):
        for w in range(PLANE):
            total = 0
            for zd in DEST_ORDER[zo]:
                if zd != zo:
                    firsts[zo, w, zd] = total
                    total = total + sizes[zo, w, zd]
    for way in range(2):
        def real(cl):
            return (LINE - 1 - cl[0], cl[1], LINE - 1 - cl[2]) if way else cl

        for lane, order in enumerate(LANES):
            pos = 0
            for cl in order:
                size = sizes[real(cl)]
                if cl[0] == lane:
                    begin = firsts[real(cl)]
                    last = ((begin + size - 1) * 13) >> 6
                    slack = CHUNK * last - begin - (1 if cl[1] < 2 else 0)
                    ready = STEP * due(cl[1], last) - jnp.maximum(0, slack)
                else:
                    ready = starts[way, lane - 1, cl] + HOP * STEP
                start = jnp.maximum(pos, jnp.where(size > 0, ready, 0))
                starts[way, lane, cl] = start
                pos = start + size
            longest = jnp.maximum(longest, pos)
    return starts, longest


def table_kernel(n, groups, per_peer, got, wide, sends, slots, branch, starts):
    z = lax.axis_index("dom") // PLANE
    flow = LINE * per_peer
    near = groups * PLANE
    table = HALF

    def clear(i, _):
        for k in range(8):
            sends[0, i * 8 + k] = 0
            sends[1, i * 8 + k] = 0
        return 0

    lax.fori_loop(0, table // 8, clear, 0)

    sizes = {
        (zo, w, zd): got[zo * near + w, flow + w * LINE + zd]
        for zo in range(LINE) for w in range(PLANE) for zd in range(LINE)
    }
    mine, _ = timetable(sizes)
    for way in range(2):
        for lane, order in enumerate(LANES):
            for at, cl in enumerate(order):
                starts[way, lane, at] = mine[way, lane, cl]

    full = jnp.concatenate([wide[...], jnp.zeros((HALF - wide.shape[0], HALF), jnp.int32)], axis=0)
    turned = jnp.transpose(full)
    lanes = lax.broadcasted_iota(jnp.int32, (LINE, HALF), 1)
    every = {}
    for w in range(PLANE):
        block = turned[flow + w * LINE:flow + (w + 1) * LINE]
        for bit in (1, 2):
            if w & bit:
                block = jnp.where(
                    lanes // bit % 2 == 0, pltpu.roll(block, HALF - bit, 1), pltpu.roll(block, bit, 1)
                )
        for zo in range(LINE):
            moved = pltpu.roll(block, HALF - zo * near, 1) if zo else block
            for zd in range(LINE):
                every[zo, w, zd] = jnp.broadcast_to(moved[zd:zd + 1], (8, HALF))
    _, longest = timetable(every)
    lanes = lax.broadcasted_iota(jnp.int32, (8, HALF), 1)
    longest = jnp.max(jnp.where(lanes < near, longest, 0))
    choice = jnp.int32(0)
    for limit in LIMITS:
        choice = choice + jnp.where(longest > limit, 1, 0)
    branch[0] = choice

    def fill(me):
        def row(zo, w):
            return zo * near + w

        def size_of(zo, w, zd):
            return got[row(zo, w), flow + w * LINE + zd]

        def first_of(zo, w, zd):
            total = jnp.int32(0)
            for real in DEST_ORDER[zo]:
                if real == zd:
                    return total
                total = total + size_of(zo, w, real)

        for way in range(2):
            def plane(p):
                return LINE - 1 - p if way else p

            lane = plane(me)
            if lane == LINE - 1:
                continue
            landed = PLANE * flow + way * ROOM
            for at, cl in enumerate(LANES[lane]):
                zo, w, zd = plane(cl[0]), cl[1], plane(cl[2])
                if zo == me:
                    source = w * flow + first_of(zo, w, zd)
                else:
                    source = landed + starts[way, lane - 1, LANES[lane - 1].index(cl)]
                size = size_of(zo, w, zd)
                start = jnp.minimum(starts[way, lane, at], ROOM)
                for k in range(per_peer):
                    sends[way, start + k] = jnp.where(k < size, source + k, 0)
        for zo in range(LINE):
            for w in range(PLANE):
                first = first_of(zo, w, me)
                size = size_of(zo, w, me)
                if zo == me:
                    source = w * flow + first
                else:
                    way = 0 if zo < me else 1
                    lane = me - 1 if zo < me else LINE - 2 - me
                    cl = (zo, w, me) if zo < me else (LINE - 1 - zo, w, LINE - 1 - me)
                    source = PLANE * flow + way * ROOM + starts[way, lane, LANES[lane].index(cl)]
                for k in range(per_peer):
                    label = got[row(zo, w), first + k]
                    slots[jnp.where(k < size, label + 1, 0)] = source + k

    for me in range(LINE):
        @pl.when(z == me)
        def _():
            fill(me)


def relay_kernel(
    n, per_peer, limit, source, label, sends, slots, points, wp, bp, slice_weight, softness, qkv_small,
    wo, bo, result,
    held, pool, sending, landed, stage, landing, numer, denom, sums, inbox, mixed,
    ws, wt, spread_ones, ones, head_ones, qkv,
    point_sem, plane_send, plane_recv, line_send, line_recv, red_send, red_recv, out_sem,
):
    me = lax.axis_index("dom")
    z = me // PLANE
    peer = mirror(me, n)
    flow = LINE * per_peer
    chunks = flow // CHUNK
    rounds = limit // STEP
    fetch = pltpu.make_async_copy(points, held, point_sem)
    fetch.start()
    barrier = pltpu.get_barrier_semaphore()
    for x in range(1, n):
        pl.semaphore_signal(barrier, inc=1, device_id={"dom": peer(x)}, device_id_type=MESH)
    numer[...] = jnp.zeros_like(numer)
    denom[...] = jnp.zeros_like(denom)
    build(slice_weight, softness, qkv_small, ws, wt, spread_ones, ones, head_ones, qkv)
    pl.semaphore_wait(barrier, n - 1)
    fetch.wait()

    def plane_copy(w, j):
        return pltpu.make_async_remote_copy(
            src_ref=sending.at[w - 1, j], dst_ref=landed.at[w - 1, j], send_sem=plane_send.at[w - 1, j],
            recv_sem=plane_recv.at[w - 1, j], device_id={"dom": peer(w)},
            device_id_type=MESH,
        )

    def line_copy(way, r):
        slot = r % RING
        near = me + PLANE if way == 0 else me - PLANE
        return pltpu.make_async_remote_copy(
            src_ref=stage.at[way, slot], dst_ref=landing.at[way, slot], send_sem=line_send.at[way, slot],
            recv_sem=line_recv.at[way, slot], device_id={"dom": near}, device_id_type=MESH,
        )

    can_send = (z < LINE - 1, z > 0)
    can_recv = (z > 0, z < LINE - 1)

    def encode(i, _):
        j, turn = i // PLANE, i % PLANE
        w = ENCODE_ORDER[0]
        for at in range(1, PLANE):
            w = jnp.where(turn == at, ENCODE_ORDER[at], w)
        tiles = jnp.concatenate([held[source[w, 0, j * CHUNK + k]] for k in range(CHUNK)], axis=0)
        proj, weights = encode_rows(
            tiles, wp[...], bp[...], ws[...], wt[...], spread_ones[...], ones[...]
        )
        live = jnp.concatenate(
            [jnp.full((TILE, WIDTH), label[w, 0, j * CHUNK + k], jnp.int32) for k in range(CHUNK)], axis=0
        ) >= 0
        kept = jnp.where(live, weights.astype(F32), 0.0)
        weights = kept.astype(BF16)
        numer[...] += lax.dot_general(
            weights, proj, (((0,), (0,)), ((), ())), preferred_element_type=F32
        )
        denom[...] += jnp.sum(kept.reshape(CHUNK * TILE // 8, 8, WIDTH), axis=0)
        weights = weights.reshape(CHUNK, TILE, WIDTH)

        @pl.when(turn == 0)
        def _():
            pool[pl.ds(j * CHUNK, CHUNK)] = weights

        @pl.when(turn > 0)
        def _():
            sending[w - 1, j] = weights

        @pl.when(turn == ENCODE_ORDER.index(1))
        def _():
            plane_copy(1, j).start()

        return 0

    def line_arrive(way, m):
        line_copy(way, m).wait_recv()
        pool[pl.ds(PLANE * flow + way * ROOM + m * STEP, STEP)] = landing[way, m % RING]

    def release(w, r):
        begin, first = due(w, 0) - 5, encoded(ENCODE_ORDER.index(w))
        since = r - begin
        j = since // 5
        now = (since % 5 == 0) & (j >= 0) & (j < chunks)
        if begin < first:
            now = (now & (j > 0)) | (r == first)
            j = jnp.where(r == first, 0, j)

        @pl.when(now)
        def _():
            plane_copy(w, j).start()

    def relay(r):
        for w in range(2, PLANE):
            release(w, r)
        for way in range(2):
            @pl.when(can_recv[way] & (r >= HOP))
            def _():
                line_arrive(way, r - HOP)
        for w in range(1, PLANE):
            if w == 1:
                late = 2 * ENCODE_ORDER.index(w) + 4
                j = (3 * r + 7 - late) // 8
                now = (3 * r + 7 >= late) & ((8 * j + late) // 3 == r)
            else:
                since = r - due(w, 0)
                j = since // 5
                now = (since >= 0) & (since % 5 == 0)

            @pl.when(now & (j < chunks))
            def _():
                plane_copy(w, j).wait_recv()
                pool[pl.ds(w * flow + j * CHUNK, CHUNK)] = landed[w - 1, j]

        for way in range(2):
            @pl.when(can_send[way])
            def _():
                @pl.when(r >= RING)
                def _():
                    line_copy(way, r - RING).wait_send()

                for k in range(STEP):
                    stage[way, r % RING, k] = pool[sends[way, r * STEP + k]]
                line_copy(way, r).start()

    steps = PLANE * chunks

    reached = encoded(steps - 1) + 1
    levels = sums.shape[0] - 1
    group = LAND // (2 * LAST)
    early = rounds - LAST
    seen = (early - HOP + 1) * STEP
    rest = limit - seen

    def swap(level):
        return pltpu.make_async_remote_copy(
            src_ref=sums.at[level], dst_ref=inbox.at[level], send_sem=red_send.at[level],
            recv_sem=red_recv.at[level], device_id={"dom": peer(n >> (level + 1))}, device_id_type=MESH,
        )

    def own_sums():
        lane_head = lax.broadcasted_iota(jnp.int32, (FEAT, HALF), 1) // FEAT
        for a in range(2):
            acc = jnp.zeros((FEAT, HALF), F32)
            for j in range(4):
                part = numer[pl.ds((a * 4 + j) * FEAT, FEAT), pl.ds(a * HALF, HALF)]
                acc = acc + jnp.where(lane_head == j, part, 0.0)
            sums[0, pl.ds(a * FEAT, FEAT), :] = acc
            total = jnp.sum(denom[:, pl.ds(a * HALF, HALF)], axis=0, keepdims=True)
            sums[0, pl.ds(2 * FEAT + a * 8, 8), :] = jnp.broadcast_to(total, (8, HALF))

    def decode(rows):
        deslice = jnp.dot(rows, mixed[...], preferred_element_type=F32).astype(BF16)
        y = (jnp.dot(deslice, wo[...], preferred_element_type=F32) + bo[...]).astype(BF16)
        return y.reshape(rows.shape[0] // TILE, TILE, WIDTH)

    def decode_slots(i, _):
        rows = jnp.concatenate([pool[slots[i * group + k + 1]] for k in range(group)], axis=0)
        held[pl.ds(i * group, group)] = decode(rows)
        return 0

    def one_round(r, _):
        @pl.when(r < reached)
        def _():
            lax.fori_loop(3 * r // 2, jnp.minimum(3 * (r + 1) // 2, steps), encode, 0)

        @pl.when(r == reached)
        def _():
            own_sums()
            swap(0).start()

        for level in range(levels):
            @pl.when(r == reached + 4 * (level + 1))
            def _():
                swap(level).wait()
                sums[level + 1] = sums[level] + inbox[level]
                if level + 1 < levels:
                    swap(level + 1).start()
                else:
                    mixed[...] = mix(sums[levels], qkv, head_ones[...])

        relay(r)

        @pl.when(r >= early)
        def _():
            lax.fori_loop(2 * (r - early), 2 * (r - early) + 2, decode_slots, 0)

        return 0

    lax.fori_loop(0, rounds, one_round, 0)
    final = HOP * STEP
    blocks = rest // final

    def decode_rest(i, _):
        way, part = i % 2, i // 2
        begin = PLANE * flow + way * ROOM + seen + part * final
        rows = pool[pl.ds(begin, final)].reshape(final * TILE, WIDTH)
        held[pl.ds(LAND + way * rest + part * final, final)] = decode(rows)
        return 0

    lax.fori_loop(0, 2 * (blocks - 1), decode_rest, 0)
    for m in range(rounds - HOP, rounds):
        for way in range(2):
            @pl.when(can_recv[way])
            def _():
                line_arrive(way, m)
    lax.fori_loop(2 * (blocks - 1), 2 * blocks, decode_rest, 0)

    def out_copy(i):
        return pltpu.make_async_copy(
            landed.at[i // chunks, i % chunks], result.at[pl.ds(i * CHUNK, CHUNK)], out_sem.at[i]
        )

    def finish(i, _):
        for k in range(CHUNK):
            at = i * CHUNK + k
            where = slots[at + 1] - PLANE * flow
            way = jnp.where(where >= ROOM, 1, 0)
            pos = where - way * ROOM - seen
            late = (where >= 0) & (pos >= 0)
            landed[i // chunks, i % chunks, k] = held[jnp.where(late, LAND + way * rest + pos, at)]
        out_copy(i).start()
        return 0

    lax.fori_loop(0, LAND // CHUNK, finish, 0)

    for way in range(2):
        @pl.when(can_send[way])
        def _():
            def sent(r, _):
                line_copy(way, r).wait_send()
                return 0

            lax.fori_loop(rounds - RING, rounds, sent, 0)

    def plane_sent(i, _):
        plane_copy(1 + i % (PLANE - 1), i // (PLANE - 1)).wait_send()
        return 0

    lax.fori_loop(0, (PLANE - 1) * chunks, plane_sent, 0)

    def drain(i, _):
        out_copy(i).wait()
        return 0

    lax.fori_loop(0, LAND // CHUNK, drain, 0)


def arrange(destination, own_count, n, me):
    slots = destination.shape[0]
    flow = slots // PLANE
    index = jnp.arange(slots, dtype=jnp.int32)
    live = index < own_count
    target, slot = destination // LAND, destination % LAND
    w = (target % PLANE) ^ (me % PLANE)
    line, own = target // PLANE, me // PLANE
    upper = own >= LINE // 2
    far = jnp.where(upper, LINE - 1 - line, line)
    near = jnp.where(upper, LINE - 1 - own, own)
    rank = jnp.where(
        far > near, LINE - 1 - far, jnp.where(far < near, LINE - 1 - near + far, LINE - 1)
    )
    w = jnp.where(live, w, -1)
    key = rank * slots + index
    earlier = (w[:, None] == w[None, :]) & (key[None, :] < key[:, None])
    place = w * flow + jnp.sum(earlier.astype(jnp.int32), axis=1)
    kind = jnp.where(live, w * LINE + line, -HALF)
    grid = jnp.arange(PLANE * HALF, dtype=jnp.int32)
    row, lane = grid // HALF, grid % HALF
    at = jnp.where(lane < flow, row * flow + lane, -2)
    placed = jnp.where(live, place, -1)
    matches = placed[None, :] == at[:, None]
    source = jnp.sum(jnp.where(matches, index[None, :], 0), axis=1)
    told = jnp.where(
        matches, slot[None, :] + 1, (kind[None, :] == (lane - flow)[:, None]).astype(jnp.int32)
    )
    rows = jnp.sum(told, axis=1) - jnp.where(lane < flow, 1, 0)
    shape = (PLANE, 1, HALF)
    return lax.optimization_barrier((source.reshape(shape), rows.reshape(shape)))


def relayed(n, groups, points, counts, destination, wp, bp, slice_weight, softness, qkv, wo, bo):
    slots = points.shape[0] // TILE
    per_peer = slots // n
    flow = slots // PLANE
    any_spec = pl.BlockSpec(memory_space=pl.ANY)
    vmem = pl.BlockSpec(memory_space=pltpu.VMEM)
    smem = pl.BlockSpec(memory_space=pltpu.SMEM)
    dma = pltpu.SemaphoreType.DMA
    source, rows = arrange(destination, counts[0], n, lax.axis_index("dom"))
    got = pl.pallas_call(
        functools.partial(tell_kernel, n, groups),
        out_shape=jax.ShapeDtypeStruct((groups * n, 1, HALF), jnp.int32),
        in_specs=[any_spec], out_specs=any_spec,
        scratch_shapes=[dma((n * groups,)), dma((n * groups,)), dma],
        compiler_params=pltpu.CompilerParams(collective_id=0, has_side_effects=True),
        name="tell",
    )(rows)
    sends, places, branch = pl.pallas_call(
        functools.partial(table_kernel, n, groups, per_peer),
        out_shape=(
            jax.ShapeDtypeStruct((2, HALF), jnp.int32),
            jax.ShapeDtypeStruct((LAND + 1,), jnp.int32),
            jax.ShapeDtypeStruct((1,), jnp.int32),
        ),
        in_specs=[smem, vmem], out_specs=(smem, smem, smem),
        scratch_shapes=[pltpu.SMEM((2, LINE - 1, PLANE * LINE), jnp.int32)],
        name="table",
    )(got.reshape(groups * n, HALF), got.reshape(groups * n, HALF))

    levels = (n - 1).bit_length()
    stat_rows = 2 * FEAT + 16
    tile = (TILE, WIDTH)

    def relay(limit, at, *_):
        placed = pl.pallas_call(
            functools.partial(relay_kernel, n, per_peer, limit),
            out_shape=jax.ShapeDtypeStruct((LAND,) + tile, BF16),
            in_specs=[smem] * 4 + [any_spec] + [vmem] * 7,
            out_specs=any_spec,
            scratch_shapes=[
                pltpu.VMEM((slots,) + tile, BF16),
                pltpu.VMEM((slots + 2 * ROOM,) + tile, BF16),
                pltpu.VMEM((PLANE - 1, flow // CHUNK, CHUNK) + tile, BF16),
                pltpu.VMEM((PLANE - 1, flow // CHUNK, CHUNK) + tile, BF16),
                pltpu.VMEM((2, RING, STEP) + tile, BF16),
                pltpu.VMEM((2, RING, STEP) + tile, BF16),
                pltpu.VMEM((WIDTH, WIDTH), F32),
                pltpu.VMEM((8, WIDTH), F32),
                pltpu.VMEM((levels + 1, stat_rows, HALF), F32),
                pltpu.VMEM((levels, stat_rows, HALF), F32),
                pltpu.VMEM((WIDTH, WIDTH), BF16),
                pltpu.VMEM((WIDTH, WIDTH), BF16),
                pltpu.VMEM((WIDTH, HALF), BF16),
                pltpu.VMEM((HALF, WIDTH), BF16),
                pltpu.VMEM((WIDTH, WIDTH), BF16),
                pltpu.VMEM((HALF, HALF), F32),
                pltpu.VMEM((3, HALF, HALF), F32),
                dma, dma((PLANE - 1, flow // CHUNK)), dma((PLANE - 1, flow // CHUNK)),
                dma((2, RING)), dma((2, RING)), dma((levels,)), dma((levels,)), dma((LAND // CHUNK,)),
            ],
            compiler_params=pltpu.CompilerParams(
                collective_id=1 + at, has_side_effects=True, vmem_limit_bytes=62 << 20
            ),
            name="relay" + str(limit),
        )(
            source, rows, sends, places, points.reshape((slots,) + tile), wp, bp.reshape(1, WIDTH),
            slice_weight, softness.reshape(1, FEAT), qkv, wo, bo.reshape(1, WIDTH),
        )
        return placed.reshape(LAND * TILE, WIDTH)

    def fallback():
        return direct(n, points, counts, destination, wp, bp, slice_weight, softness, qkv, wo, bo)

    branches = [functools.partial(relay, limit, at) for at, limit in enumerate(LIMITS)]
    return lax.switch(branch[0], branches + [fallback])


def solution(mesh):
    spec = P(("groups", "dom"))
    wide = P(("groups", "dom"), None)
    n, groups = mesh.shape["dom"], mesh.shape["groups"]
    if n == PLANE * LINE and groups == 2:
        body = functools.partial(relayed, n, groups)
    else:
        body = functools.partial(direct, n)
    return jax.shard_map(
        body, mesh=mesh, in_specs=(wide, spec, spec) + (P(),) * 7, out_specs=wide, check_vma=False,
    )
```

```python
import functools

import jax
import jax.numpy as jnp
from jax import lax
from jax.experimental import pallas as pl
from jax.experimental.pallas import tpu as pltpu
from jax.sharding import PartitionSpec as P

WIDTH = 256
HEADS = 8
FEAT = 32
TILE = 128
LAND = 80
HALF = 128
PLANE = 4
LINE = 4
CHUNK = 5
STEP = 2
HOP = 2
RING = 4
LIMITS = (94, 102, 104, 124)
ROOM = LIMITS[-1]
ENCODE_ORDER = (0, 1, 2, 3)
LAST = 5
DEST_ORDER = ((3, 2, 1, 0), (3, 2, 0, 1), (0, 1, 3, 2), (0, 1, 2, 3))
LANES = (
    ((0, 0, 3), (0, 0, 2), (0, 1, 3), (0, 2, 3), (0, 3, 3), (0, 1, 2), (0, 2, 2), (0, 3, 2), (0, 2, 1), (0, 0, 1), (0, 1, 1), (0, 3, 1)),
    ((1, 0, 3), (1, 0, 2), (1, 1, 3), (0, 0, 3), (0, 0, 2), (0, 1, 3), (1, 2, 3), (1, 3, 3), (1, 1, 2), (0, 2, 3), (0, 3, 3), (1, 3, 2), (1, 2, 2), (0, 2, 2), (0, 3, 2), (0, 1, 2)),
    ((1, 0, 3), (1, 1, 3), (2, 0, 3), (2, 1, 3), (0, 0, 3), (0, 1, 3), (1, 2, 3), (1, 3, 3), (0, 2, 3), (2, 3, 3), (0, 3, 3), (2, 2, 3)),
)
MESH = pl.DeviceIdType.MESH
HIGHEST = lax.Precision.HIGHEST
F32 = jnp.float32
BF16 = jnp.bfloat16


def split(x):
    high = x.astype(BF16)
    return high, x - high.astype(F32)


def encode_rows(x, wp, bp, ws, wt, spread_ones, ones):
    x = x.astype(F32)
    centred = x - jnp.sum(x, axis=-1, keepdims=True) * (1.0 / WIDTH)
    spread = jnp.sum(centred * centred, axis=-1, keepdims=True) * (1.0 / WIDTH)
    normed = (centred * lax.rsqrt(spread + 1e-05)).astype(BF16)
    dot = functools.partial(jnp.dot, preferred_element_type=F32)
    proj = (dot(normed, wp) + bp).astype(BF16)
    logits = dot(proj, ws)
    soft = dot(proj, wt)
    temper = 0.5 + (jnp.maximum(soft, 0.0) + jnp.log1p(jnp.exp(-jnp.abs(soft))))
    first, rest = split(1.0 / temper)
    second, rest = split(rest)
    lane = lax.broadcasted_iota(jnp.int32, soft.shape, 1)
    parts = jnp.where(lane < HEADS, first.astype(F32), jnp.where(lane < 2 * HEADS, second.astype(F32), rest))
    scale = dot(parts.astype(BF16), spread_ones)
    raised = jnp.exp(logits * scale)
    first, rest = split(raised)
    total = dot(first, ones) + dot(rest.astype(BF16), ones)
    return proj, (raised / total).astype(BF16)


def diagonal(block, times):
    wide = jnp.concatenate([block] * times, axis=1)
    full = jnp.concatenate([wide] * times, axis=0)
    size = times * FEAT
    row = lax.broadcasted_iota(jnp.int32, (size, size), 0) // FEAT
    lane = lax.broadcasted_iota(jnp.int32, (size, size), 1) // FEAT
    return jnp.where(row == lane, full, 0.0)


def build(slice_weight, softness, qkv_small, ws, wt, spread_ones, ones, head_ones, qkv):
    ws[...] = diagonal(slice_weight[...].astype(F32), HEADS).astype(BF16)
    for i in range(3):
        qkv[i] = diagonal(qkv_small[i], 4)
    unity = jnp.ones((FEAT, FEAT), F32)
    ones[...] = diagonal(unity, HEADS).astype(BF16)
    head_ones[...] = diagonal(unity, 4)
    row = lax.broadcasted_iota(jnp.int32, (HALF, WIDTH), 0)
    lane = lax.broadcasted_iota(jnp.int32, (HALF, WIDTH), 1) // FEAT
    spread_ones[...] = jnp.where((row % HEADS == lane) & (row < 3 * HEADS), 1.0, 0.0).astype(BF16)
    flat = jnp.concatenate([softness[...].astype(F32)] * 4, axis=1)
    tall = jnp.transpose(jnp.broadcast_to(flat, (HALF, HALF)))
    tall = jnp.concatenate([tall, tall], axis=0)
    row = lax.broadcasted_iota(jnp.int32, (WIDTH, HALF), 0) // FEAT
    lane = lax.broadcasted_iota(jnp.int32, (WIDTH, HALF), 1)
    wt[...] = jnp.where((row == lane % HEADS) & (lane < 3 * HEADS), tall, 0.0).astype(BF16)


def move_kernel(
    n, per_peer, unit, source, label, points, labels, wp, bp, slice_weight, softness, qkv_small,
    wo, bo, result, labels_out,
    held_points, sending, arrived, numer, denom, sums, inbox, mixed,
    ws, wt, spread_ones, ones, head_ones, qkv,
    point_sem, send_sem, recv_sem, lab_send, lab_recv, own_sem, out_sem, red_send, red_recv,
):
    me = lax.axis_index("dom")
    pieces = per_peer // unit
    rows = unit * TILE
    fetch = pltpu.make_async_copy(points, held_points, point_sem)
    fetch.start()

    def partner(x):
        peer, bit = 0, 1
        while bit < n:
            mine, flip = me // bit % 2, x // bit % 2
            peer = peer + bit * (mine + flip - 2 * mine * flip)
            bit = bit * 2
        return peer

    barrier = pltpu.get_barrier_semaphore()
    for x in range(1, n):
        pl.semaphore_signal(barrier, inc=1, device_id={"dom": partner(x)}, device_id_type=MESH)
    numer[...] = jnp.zeros_like(numer)
    denom[...] = jnp.zeros_like(denom)
    build(slice_weight, softness, qkv_small, ws, wt, spread_ones, ones, head_ones, qkv)
    pl.semaphore_wait(barrier, n - 1)

    def order(i):
        quarter = n // 4
        near = lax.rem(i, 2) * 2 * quarter
        early = 3 * quarter + i // 2 - near
        late = jnp.where(i < 3 * quarter, i, n - 1 - i)
        return jnp.where(i < 2 * quarter, early, late)

    def lab_copy(x):
        peer = partner(x)
        return pltpu.make_async_remote_copy(
            src_ref=labels.at[peer], dst_ref=labels_out.at[me], send_sem=lab_send.at[x],
            recv_sem=lab_recv.at[x], device_id={"dom": peer}, device_id_type=MESH,
        )

    def piece_copy(x, s):
        at = pl.ds(pl.multiple_of(s * rows, rows), rows)
        return pltpu.make_async_remote_copy(
            src_ref=sending.at[x, at], dst_ref=arrived.at[x, at], send_sem=send_sem.at[x, s],
            recv_sem=recv_sem.at[x, s], device_id={"dom": partner(x)}, device_id_type=MESH,
        )

    def lab_start(x, _):
        lab_copy(x).start()
        return 0

    lax.fori_loop(1, n, lab_start, 0)
    own_lab = pltpu.make_async_copy(labels.at[me], labels_out.at[me], own_sem)
    own_lab.start()
    fetch.wait()

    def compute(x, peer, s):
        first = peer * per_peer + s * unit
        tiles = jnp.concatenate([held_points[source[first + j]] for j in range(unit)], axis=0)
        proj, weights = encode_rows(
            tiles, wp[...], bp[...], ws[...], wt[...], spread_ones[...], ones[...]
        )
        live = jnp.concatenate(
            [jnp.full((TILE, WIDTH), label[first + j], jnp.int32) for j in range(unit)], axis=0
        ) >= 0
        kept = jnp.where(live, weights.astype(F32), 0.0)
        weights = kept.astype(BF16)
        sending[x, pl.ds(pl.multiple_of(s * rows, rows), rows), :] = weights
        numer[...] += lax.dot_general(
            weights, proj, (((0,), (0,)), ((), ())), preferred_element_type=F32
        )
        denom[...] += jnp.sum(kept.reshape(rows // 8, 8, WIDTH), axis=0)

    steps = (n - 1) * pieces
    held_from = (n - 1) * (pieces - 1)

    def encode_step(i, _):
        x = order(i % (n - 1))
        compute(x, partner(x), i // (n - 1))

        @pl.when((i > 0) & (i <= held_from))
        def _():
            piece_copy(order((i - 1) % (n - 1)), (i - 1) // (n - 1)).start()

        return 0

    lax.fori_loop(0, steps, encode_step, 0)

    def own_step(s, _):
        compute(0, me, s)
        return 0

    lax.fori_loop(0, pieces, own_step, 0)

    lane_head = lax.broadcasted_iota(jnp.int32, (FEAT, HALF), 1) // FEAT
    for a in range(2):
        acc = jnp.zeros((FEAT, HALF), F32)
        for j in range(4):
            part = numer[pl.ds((a * 4 + j) * FEAT, FEAT), pl.ds(a * HALF, HALF)]
            acc = acc + jnp.where(lane_head == j, part, 0.0)
        sums[0, pl.ds(a * FEAT, FEAT), :] = acc
        total = jnp.sum(denom[:, pl.ds(a * HALF, HALF)], axis=0, keepdims=True)
        sums[0, pl.ds(2 * FEAT + a * 8, 8), :] = jnp.broadcast_to(total, (8, HALF))

    def release(i, _):
        piece_copy(order(i - held_from), pieces - 1).start()
        return 0

    level, bit = 0, n // 2
    while bit > 0:
        swap = pltpu.make_async_remote_copy(
            src_ref=sums.at[level], dst_ref=inbox.at[level], send_sem=red_send.at[level],
            recv_sem=red_recv.at[level], device_id={"dom": partner(bit)}, device_id_type=MESH,
        )
        swap.start()
        swap.wait()
        sums[level + 1] = sums[level] + inbox[level]
        level, bit = level + 1, bit // 2
        if level == max(1, (n - 1).bit_length() - 2):
            lax.fori_loop(held_from, steps, release, 0)
    mixed[...] = mix(sums[level], qkv, head_ones[...])

    def out_copy(x, s):
        at = pl.ds(pl.multiple_of(s * rows, rows), rows)
        return pltpu.make_async_copy(arrived.at[x, at], result.at[partner(x), at], out_sem.at[x, s])

    def decode(read, x, s):
        at = pl.ds(pl.multiple_of(s * rows, rows), rows)
        deslice = jnp.dot(read[x, at, :], mixed[...], preferred_element_type=F32).astype(BF16)
        y = (jnp.dot(deslice, wo[...], preferred_element_type=F32) + bo[...]).astype(BF16)
        arrived[x, at, :] = y
        out_copy(x, s).start()

    def decode_own(s, _):
        decode(sending, 0, s)
        return 0

    lax.fori_loop(0, pieces, decode_own, 0)

    def from_peer(i, _):
        x, s = order(i % (n - 1)), i // (n - 1)
        piece_copy(x, s).wait_recv()
        decode(arrived, x, s)
        return 0

    lax.fori_loop(0, steps, from_peer, 0)

    def finish(x, _):
        def one(s, _):
            piece_copy(x, s).wait_send()
            return 0

        lax.fori_loop(0, pieces, one, 0)
        lab_copy(x).wait()
        return 0

    lax.fori_loop(1, n, finish, 0)
    own_lab.wait()

    def drain(i, _):
        out_copy(i // pieces, i % pieces).wait()
        return 0

    lax.fori_loop(0, n * pieces, drain, 0)


def mix(stats, qkv, ones):
    row_head = lax.broadcasted_iota(jnp.int32, (HALF, HALF), 0) // FEAT
    lane_head = lax.broadcasted_iota(jnp.int32, (HALF, HALF), 1) // FEAT
    same = row_head == lane_head
    blocks = []
    for a in range(2):
        numer = stats[a * FEAT:(a + 1) * FEAT, :]
        row = stats[2 * FEAT + a * 8:2 * FEAT + (a + 1) * 8, :]
        col = jnp.transpose(jnp.broadcast_to(row[:1], (HALF, HALF)))
        spread = jnp.zeros((FEAT, HALF), F32)
        for j in range(4):
            spread = spread + jnp.where(
                lane_head[:FEAT] == j, col[j * FEAT:(j + 1) * FEAT, :], 0.0
            )
        tokens = numer / (spread + 1e-05)
        dot = functools.partial(jnp.dot, preferred_element_type=F32, precision=HIGHEST)
        query, keys, values = (dot(tokens, qkv[i]) for i in range(3))
        spread_keys = jnp.where(same, jnp.concatenate([keys] * 4, axis=0), 0.0)
        scores = lax.dot_general(
            query, spread_keys, (((1,), (1,)), ((), ())), preferred_element_type=F32, precision=HIGHEST
        ) * FEAT ** (-0.5)
        raised = jnp.exp(scores)
        attend = raised / dot(raised, ones)
        spread_values = jnp.where(same, jnp.concatenate([values] * 4, axis=0), 0.0)
        mixed = dot(attend, spread_values)
        blocks.append(jnp.where(same, jnp.concatenate([mixed] * 4, axis=0), 0.0))
    nil = jnp.zeros((HALF, HALF), F32)
    return jnp.concatenate(
        [jnp.concatenate([blocks[0], nil], axis=1), jnp.concatenate([nil, blocks[1]], axis=1)], axis=0
    ).astype(BF16)


def place_kernel(n, per_peer, chunks, per_chunk, labels, tiles, out, held, in_sem, out_sem):
    def load(k, _):
        def one(t, _):
            slot = labels[k, t]

            @pl.when(slot >= 0)
            def _():
                pltpu.make_async_copy(
                    tiles.at[k * per_peer + t], held.at[slot], in_sem.at[slot // per_chunk]
                ).start()

            return 0

        return lax.fori_loop(0, per_peer, one, 0)

    lax.fori_loop(0, n, load, 0)

    def step(c, _):
        part = pl.ds(c * per_chunk, per_chunk)
        pltpu.make_async_copy(tiles.at[pl.ds(0, per_chunk)], held.at[part], in_sem.at[c]).wait()
        pltpu.make_async_copy(held.at[part], out.at[part], out_sem.at[c]).start()
        return 0

    lax.fori_loop(0, chunks, step, 0)

    def finish(c, _):
        part = pl.ds(c * per_chunk, per_chunk)
        pltpu.make_async_copy(held.at[part], out.at[part], out_sem.at[c]).wait()
        return 0

    lax.fori_loop(0, chunks, finish, 0)


def plan(destination, own_count, n):
    slots = destination.shape[0]
    per_peer = slots // n
    index = jnp.arange(slots, dtype=jnp.int32)
    live = index < own_count
    target = jnp.where(live, destination // LAND, -1)
    slot = jnp.where(live, destination % LAND, -1)
    earlier = (target[:, None] == target[None, :]) & live[None, :] & (index[None, :] < index[:, None])
    rank = jnp.sum(earlier.astype(jnp.int32), axis=1)
    place = target * per_peer + rank
    matches = live[None, :] & (place[None, :] == index[:, None])
    source = jnp.sum(jnp.where(matches, index[None, :], 0), axis=1)
    label = jnp.sum(jnp.where(matches, slot[None, :] + 1, 0), axis=1) - 1
    return source, label


def direct(n, points, counts, destination, wp, bp, slice_weight, softness, qkv, wo, bo):
    slots = points.shape[0] // TILE
    per_peer = slots // n
    any_spec = pl.BlockSpec(memory_space=pl.ANY)
    vmem = pl.BlockSpec(memory_space=pltpu.VMEM)
    smem = pl.BlockSpec(memory_space=pltpu.SMEM)
    source, label = plan(destination, counts[0], n)
    rows = per_peer * TILE
    labels = jnp.pad(label.reshape(n, 1, per_peer), ((0, 0), (0, 0), (0, HALF - per_peer)))
    unit = 2 if per_peer % 2 == 0 else 1
    pieces = per_peer // unit
    levels = (n - 1).bit_length()
    stat_rows = 2 * FEAT + 16
    dma = pltpu.SemaphoreType.DMA
    tiles, arrived_lab = pl.pallas_call(
        functools.partial(move_kernel, n, per_peer, unit),
        out_shape=(
            jax.ShapeDtypeStruct((n, rows, WIDTH), BF16),
            jax.ShapeDtypeStruct((n, 1, HALF), jnp.int32),
        ),
        in_specs=[smem, smem, any_spec, any_spec] + [vmem] * 7,
        out_specs=(any_spec, any_spec),
        scratch_shapes=[
            pltpu.VMEM((slots, TILE, WIDTH), BF16),
            pltpu.VMEM((n, rows, WIDTH), BF16),
            pltpu.VMEM((n, rows, WIDTH), BF16),
            pltpu.VMEM((WIDTH, WIDTH), F32),
            pltpu.VMEM((8, WIDTH), F32),
            pltpu.VMEM((levels + 1, stat_rows, HALF), F32),
            pltpu.VMEM((levels, stat_rows, HALF), F32),
            pltpu.VMEM((WIDTH, WIDTH), BF16),
            pltpu.VMEM((WIDTH, WIDTH), BF16),
            pltpu.VMEM((WIDTH, HALF), BF16),
            pltpu.VMEM((HALF, WIDTH), BF16),
            pltpu.VMEM((WIDTH, WIDTH), BF16),
            pltpu.VMEM((HALF, HALF), F32),
            pltpu.VMEM((3, HALF, HALF), F32),
            dma, dma((n, pieces)), dma((n, pieces)), dma((n,)), dma((n,)), dma, dma((n, pieces)),
            dma((levels,)), dma((levels,)),
        ],
        compiler_params=pltpu.CompilerParams(
            collective_id=15, has_side_effects=True, vmem_limit_bytes=60 << 20
        ),
        name="move",
    )(
        source, label, points.reshape(slots, TILE, WIDTH), labels, wp, bp.reshape(1, WIDTH),
        slice_weight, softness.reshape(1, FEAT), qkv, wo, bo.reshape(1, WIDTH),
    )

    per_chunk = 8
    chunks = LAND // per_chunk
    placed = pl.pallas_call(
        functools.partial(place_kernel, n, per_peer, chunks, per_chunk),
        out_shape=jax.ShapeDtypeStruct((LAND, TILE, WIDTH), BF16),
        grid_spec=pltpu.PrefetchScalarGridSpec(
            num_scalar_prefetch=1, grid=(), in_specs=[any_spec], out_specs=any_spec,
            scratch_shapes=[pltpu.VMEM((LAND, TILE, WIDTH), BF16), dma((chunks,)), dma((chunks,))],
        ),
        compiler_params=pltpu.CompilerParams(vmem_limit_bytes=60 << 20),
        name="place",
    )(arrived_lab.reshape(n, HALF), tiles.reshape(slots, TILE, WIDTH))
    return placed.reshape(LAND * TILE, WIDTH)


def mirror(me, n):
    steps, bit = [], 1
    while bit < n:
        steps.append((bit, bit - 2 * bit * (me // bit % 2)))
        bit = bit * 2

    def peer(x):
        out = me
        for bit, step in steps:
            if isinstance(x, int):
                out = out + step if x & bit else out
            else:
                out = out + step * (x // bit % 2)
        return out

    return peer


def tell_kernel(n, groups, rows, got, send_sem, recv_sem, own_sem):
    me, group = lax.axis_index("dom"), lax.axis_index("groups")
    near = groups * PLANE
    mine = me // PLANE * near
    peer, other = mirror(me, n), mirror(group, groups)
    barrier = pltpu.get_barrier_semaphore()

    def device(x):
        return {"groups": other(x // n), "dom": peer(x % n)}

    for x in range(1, n * groups):
        pl.semaphore_signal(barrier, inc=1, device_id=device(x), device_id_type=MESH)
    own = pltpu.make_async_copy(rows.at[0], got.at[mine], own_sem)
    own.start()
    pl.semaphore_wait(barrier, n * groups - 1)

    def tell(x):
        w = x % PLANE
        return pltpu.make_async_remote_copy(
            src_ref=rows.at[w], dst_ref=got.at[mine + x // n * PLANE + w], send_sem=send_sem.at[x],
            recv_sem=recv_sem.at[x], device_id=device(x), device_id_type=MESH,
        )

    copies = [tell(x) for x in range(1, n * groups)]
    for copy in copies:
        copy.start()
    for copy in copies:
        copy.wait()
    own.wait()


def encoded(i):
    return (2 * i + 1) // 3


def due(w, j):
    step = PLANE * j + ENCODE_ORDER.index(w)
    if w == 0:
        return ((2 * step + 1) * 171) >> 9
    if w == 1:
        return ((2 * step + 4) * 171) >> 9
    return 5 * j + (4 if ENCODE_ORDER.index(w) < ENCODE_ORDER.index(5 - w) else 7)


def timetable(sizes):
    starts, longest = {}, 0
    firsts = {}
    for zo in range(LINE):
        for w in range(PLANE):
            total = 0
            for zd in DEST_ORDER[zo]:
                if zd != zo:
                    firsts[zo, w, zd] = total
                    total = total + sizes[zo, w, zd]
    for way in range(2):
        def real(cl):
            return (LINE - 1 - cl[0], cl[1], LINE - 1 - cl[2]) if way else cl

        for lane, order in enumerate(LANES):
            pos = 0
            for cl in order:
                size = sizes[real(cl)]
                if cl[0] == lane:
                    begin = firsts[real(cl)]
                    last = ((begin + size - 1) * 13) >> 6
                    slack = CHUNK * last - begin - (1 if cl[1] < 2 else 0)
                    ready = STEP * due(cl[1], last) - jnp.maximum(0, slack)
                else:
                    ready = starts[way, lane - 1, cl] + HOP * STEP
                start = jnp.maximum(pos, jnp.where(size > 0, ready, 0))
                starts[way, lane, cl] = start
                pos = start + size
            longest = jnp.maximum(longest, pos)
    return starts, longest


def table_kernel(n, groups, per_peer, got, wide, sends, slots, branch, starts):
    z = lax.axis_index("dom") // PLANE
    flow = LINE * per_peer
    near = groups * PLANE
    table = sends.shape[1]

    def clear(i, _):
        for k in range(8):
            sends[0, i * 8 + k] = 0
            sends[1, i * 8 + k] = 0
        return 0

    lax.fori_loop(0, table // 8, clear, 0)

    sizes = {
        (zo, w, zd): got[zo * near + w, flow + w * LINE + zd]
        for zo in range(LINE) for w in range(PLANE) for zd in range(LINE)
    }
    mine, _ = timetable(sizes)
    for way in range(2):
        for lane, order in enumerate(LANES):
            for at, cl in enumerate(order):
                starts[way, lane, at] = mine[way, lane, cl]

    full = jnp.concatenate([wide[...], jnp.zeros((HALF - wide.shape[0], HALF), jnp.int32)], axis=0)
    turned = jnp.transpose(full)
    lanes = lax.broadcasted_iota(jnp.int32, (LINE, HALF), 1)
    every = {}
    for w in range(PLANE):
        block = turned[flow + w * LINE:flow + (w + 1) * LINE]
        for bit in (1, 2):
            if w & bit:
                block = jnp.where(
                    lanes // bit % 2 == 0, pltpu.roll(block, HALF - bit, 1), pltpu.roll(block, bit, 1)
                )
        for zo in range(LINE):
            moved = pltpu.roll(block, HALF - zo * near, 1) if zo else block
            for zd in range(LINE):
                every[zo, w, zd] = jnp.broadcast_to(moved[zd:zd + 1], (8, HALF))
    _, longest = timetable(every)
    lanes = lax.broadcasted_iota(jnp.int32, (8, HALF), 1)
    longest = jnp.max(jnp.where(lanes < near, longest, 0))
    choice = jnp.int32(0)
    for limit in LIMITS:
        choice = choice + jnp.where(longest > limit, 1, 0)
    branch[0] = choice

    def fill(me):
        def row(zo, w):
            return zo * near + w

        def size_of(zo, w, zd):
            return got[row(zo, w), flow + w * LINE + zd]

        def first_of(zo, w, zd):
            total = jnp.int32(0)
            for real in DEST_ORDER[zo]:
                if real == zd:
                    return total
                total = total + size_of(zo, w, real)

        for way in range(2):
            def plane(p):
                return LINE - 1 - p if way else p

            lane = plane(me)
            if lane == LINE - 1:
                continue
            landed = PLANE * flow + way * ROOM
            for at, cl in enumerate(LANES[lane]):
                zo, w, zd = plane(cl[0]), cl[1], plane(cl[2])
                if zo == me:
                    source = w * flow + first_of(zo, w, zd)
                else:
                    source = landed + starts[way, lane - 1, LANES[lane - 1].index(cl)]
                size = size_of(zo, w, zd)
                start = jnp.minimum(starts[way, lane, at], ROOM)
                for k in range(per_peer):
                    sends[way, start + k] = jnp.where(k < size, source + k, 0)
        for zo in range(LINE):
            for w in range(PLANE):
                first = first_of(zo, w, me)
                size = size_of(zo, w, me)
                if zo == me:
                    source = w * flow + first
                else:
                    way = 0 if zo < me else 1
                    lane = me - 1 if zo < me else LINE - 2 - me
                    cl = (zo, w, me) if zo < me else (LINE - 1 - zo, w, LINE - 1 - me)
                    source = PLANE * flow + way * ROOM + starts[way, lane, LANES[lane].index(cl)]
                for k in range(per_peer):
                    label = got[row(zo, w), first + k]
                    slots[jnp.where(k < size, label + 1, 0)] = source + k

    for me in range(LINE):
        @pl.when(z == me)
        def _():
            fill(me)


def relay_kernel(
    n, per_peer, limit, source, label, sends, slots, points, wp, bp, slice_weight, softness, qkv_small,
    wo, bo, result,
    held, pool, sending, landed, stage, landing, numer, denom, sums, inbox, mixed,
    ws, wt, spread_ones, ones, head_ones, qkv,
    point_sem, plane_send, plane_recv, line_send, line_recv, red_send, red_recv, out_sem,
):
    me = lax.axis_index("dom")
    z = me // PLANE
    peer = mirror(me, n)
    flow = LINE * per_peer
    chunks = flow // CHUNK
    rounds = limit // STEP
    share = points.shape[0] // LINE

    def fetch(i):
        at = pl.ds(i * share, share)
        return pltpu.make_async_copy(points.at[at], held.at[at], point_sem.at[i])

    for i in range(LINE):
        fetch(i).start()
    barrier = pltpu.get_barrier_semaphore()
    for x in range(1, n):
        pl.semaphore_signal(barrier, inc=1, device_id={"dom": peer(x)}, device_id_type=MESH)
    numer[...] = jnp.zeros_like(numer)
    denom[...] = jnp.zeros_like(denom)
    build(slice_weight, softness, qkv_small, ws, wt, spread_ones, ones, head_ones, qkv)
    pl.semaphore_wait(barrier, n - 1)
    for i in range(LINE):
        fetch(i).wait()

    def plane_copy(w, j):
        return pltpu.make_async_remote_copy(
            src_ref=sending.at[w - 1, j], dst_ref=landed.at[w - 1, j], send_sem=plane_send.at[w - 1, j],
            recv_sem=plane_recv.at[w - 1, j], device_id={"dom": peer(w)},
            device_id_type=MESH,
        )

    def line_copy(way, r):
        slot = r % RING
        near = me + PLANE if way == 0 else me - PLANE
        return pltpu.make_async_remote_copy(
            src_ref=stage.at[way, slot], dst_ref=landing.at[way, slot], send_sem=line_send.at[way, slot],
            recv_sem=line_recv.at[way, slot], device_id={"dom": near}, device_id_type=MESH,
        )

    can_send = (z < LINE - 1, z > 0)
    can_recv = (z > 0, z < LINE - 1)

    def encode(i, _):
        j, turn = i // PLANE, i % PLANE
        w = ENCODE_ORDER[0]
        for at in range(1, PLANE):
            w = jnp.where(turn == at, ENCODE_ORDER[at], w)
        tiles = jnp.concatenate([held[source[w, 0, j * CHUNK + k]] for k in range(CHUNK)], axis=0)
        proj, weights = encode_rows(
            tiles, wp[...], bp[...], ws[...], wt[...], spread_ones[...], ones[...]
        )
        live = jnp.concatenate(
            [jnp.full((TILE, WIDTH), label[w, 0, j * CHUNK + k], jnp.int32) for k in range(CHUNK)], axis=0
        ) >= 0
        kept = jnp.where(live, weights.astype(F32), 0.0)
        weights = kept.astype(BF16)
        numer[...] += lax.dot_general(
            weights, proj, (((0,), (0,)), ((), ())), preferred_element_type=F32
        )
        denom[...] += jnp.sum(kept.reshape(CHUNK * TILE // 8, 8, WIDTH), axis=0)
        weights = weights.reshape(CHUNK, TILE, WIDTH)

        @pl.when(turn == 0)
        def _():
            pool[pl.ds(j * CHUNK, CHUNK)] = weights

        @pl.when(turn > 0)
        def _():
            sending[w - 1, j] = weights

        @pl.when(turn == ENCODE_ORDER.index(1))
        def _():
            plane_copy(1, j).start()

        return 0

    def line_arrive(way, m):
        line_copy(way, m).wait_recv()
        pool[pl.ds(PLANE * flow + way * ROOM + m * STEP, STEP)] = landing[way, m % RING]

    def release(w, r):
        begin, first = due(w, 0) - 5, encoded(ENCODE_ORDER.index(w))
        since = r - begin
        j = since // 5
        now = (since % 5 == 0) & (j >= 0) & (j < chunks)
        if begin < first:
            now = (now & (j > 0)) | (r == first)
            j = jnp.where(r == first, 0, j)

        @pl.when(now)
        def _():
            plane_copy(w, j).start()

    def relay(r):
        for w in range(2, PLANE):
            release(w, r)
        for way in range(2):
            @pl.when(can_recv[way] & (r >= HOP))
            def _():
                line_arrive(way, r - HOP)
        for w in range(1, PLANE):
            if w == 1:
                late = 2 * ENCODE_ORDER.index(w) + 4
                j = (3 * r + 7 - late) // 8
                now = (3 * r + 7 >= late) & ((8 * j + late) // 3 == r)
            else:
                since = r - due(w, 0)
                j = since // 5
                now = (since >= 0) & (since % 5 == 0)

            @pl.when(now & (j < chunks))
            def _():
                plane_copy(w, j).wait_recv()
                pool[pl.ds(w * flow + j * CHUNK, CHUNK)] = landed[w - 1, j]

        for way in range(2):
            @pl.when(can_send[way])
            def _():
                @pl.when(r >= RING)
                def _():
                    line_copy(way, r - RING).wait_send()

                for k in range(STEP):
                    stage[way, r % RING, k] = pool[sends[way, r * STEP + k]]
                line_copy(way, r).start()

    steps = PLANE * chunks

    reached = encoded(steps - 1) + 1
    levels = sums.shape[0] - 1
    group = LAND // (2 * LAST)
    early = rounds - LAST
    seen = (early - HOP + 1) * STEP
    rest = limit - seen

    def swap(level):
        return pltpu.make_async_remote_copy(
            src_ref=sums.at[level], dst_ref=inbox.at[level], send_sem=red_send.at[level],
            recv_sem=red_recv.at[level], device_id={"dom": peer(n >> (level + 1))}, device_id_type=MESH,
        )

    def own_sums():
        lane_head = lax.broadcasted_iota(jnp.int32, (FEAT, HALF), 1) // FEAT
        for a in range(2):
            acc = jnp.zeros((FEAT, HALF), F32)
            for j in range(4):
                part = numer[pl.ds((a * 4 + j) * FEAT, FEAT), pl.ds(a * HALF, HALF)]
                acc = acc + jnp.where(lane_head == j, part, 0.0)
            sums[0, pl.ds(a * FEAT, FEAT), :] = acc
            total = jnp.sum(denom[:, pl.ds(a * HALF, HALF)], axis=0, keepdims=True)
            sums[0, pl.ds(2 * FEAT + a * 8, 8), :] = jnp.broadcast_to(total, (8, HALF))

    def decode(rows):
        deslice = jnp.dot(rows, mixed[...], preferred_element_type=F32).astype(BF16)
        y = (jnp.dot(deslice, wo[...], preferred_element_type=F32) + bo[...]).astype(BF16)
        return y.reshape(rows.shape[0] // TILE, TILE, WIDTH)

    def decode_slots(i, _):
        rows = jnp.concatenate([pool[slots[i * group + k + 1]] for k in range(group)], axis=0)
        held[pl.ds(i * group, group)] = decode(rows)
        return 0

    def one_round(r, _):
        @pl.when(r < reached)
        def _():
            lax.fori_loop(3 * r // 2, jnp.minimum(3 * (r + 1) // 2, steps), encode, 0)

        @pl.when(r == reached)
        def _():
            own_sums()
            swap(0).start()

        for level in range(levels):
            @pl.when(r == reached + 4 * (level + 1))
            def _():
                swap(level).wait()
                sums[level + 1] = sums[level] + inbox[level]
                if level + 1 < levels:
                    swap(level + 1).start()
                else:
                    mixed[...] = mix(sums[levels], qkv, head_ones[...])

        relay(r)

        @pl.when(r >= early)
        def _():
            lax.fori_loop(2 * (r - early), 2 * (r - early) + 2, decode_slots, 0)

        return 0

    lax.fori_loop(0, rounds, one_round, 0)
    final = HOP * STEP
    blocks = rest // final

    def decode_rest(i, _):
        way, part = i % 2, i // 2
        begin = PLANE * flow + way * ROOM + seen + part * final
        rows = pool[pl.ds(begin, final)].reshape(final * TILE, WIDTH)
        held[pl.ds(LAND + way * rest + part * final, final)] = decode(rows)
        return 0

    lax.fori_loop(0, 2 * (blocks - 1), decode_rest, 0)
    for m in range(rounds - HOP, rounds):
        for way in range(2):
            @pl.when(can_recv[way])
            def _():
                line_arrive(way, m)
    lax.fori_loop(2 * (blocks - 1), 2 * blocks, decode_rest, 0)

    def out_copy(i):
        return pltpu.make_async_copy(
            landed.at[i // chunks, i % chunks], result.at[pl.ds(i * CHUNK, CHUNK)], out_sem.at[i]
        )

    def finish(i, _):
        for k in range(CHUNK):
            at = i * CHUNK + k
            where = slots[at + 1] - PLANE * flow
            way = jnp.where(where >= ROOM, 1, 0)
            pos = where - way * ROOM - seen
            late = (where >= 0) & (pos >= 0)
            landed[i // chunks, i % chunks, k] = held[jnp.where(late, LAND + way * rest + pos, at)]
        out_copy(i).start()
        return 0

    lax.fori_loop(0, LAND // CHUNK, finish, 0)

    for way in range(2):
        @pl.when(can_send[way])
        def _():
            def sent(r, _):
                line_copy(way, r).wait_send()
                return 0

            lax.fori_loop(rounds - RING, rounds, sent, 0)

    def plane_sent(i, _):
        plane_copy(1 + i % (PLANE - 1), i // (PLANE - 1)).wait_send()
        return 0

    lax.fori_loop(0, (PLANE - 1) * chunks, plane_sent, 0)

    def drain(i, _):
        out_copy(i).wait()
        return 0

    lax.fori_loop(0, LAND // CHUNK, drain, 0)


def arrange(destination, own_count, n, me):
    slots = destination.shape[0]
    flow = slots // PLANE
    index = jnp.arange(slots, dtype=jnp.int32)
    live = index < own_count
    target, slot = destination // LAND, destination % LAND
    w = (target % PLANE) ^ (me % PLANE)
    line, own = target // PLANE, me // PLANE
    upper = own >= LINE // 2
    far = jnp.where(upper, LINE - 1 - line, line)
    near = jnp.where(upper, LINE - 1 - own, own)
    rank = jnp.where(
        far > near, LINE - 1 - far, jnp.where(far < near, LINE - 1 - near + far, LINE - 1)
    )
    w = jnp.where(live, w, -1)
    key = rank * slots + index
    earlier = (w[:, None] == w[None, :]) & (key[None, :] < key[:, None])
    place = w * flow + jnp.sum(earlier.astype(jnp.int32), axis=1)
    kind = jnp.where(live, w * LINE + line, -HALF)
    grid = jnp.arange(PLANE * HALF, dtype=jnp.int32)
    row, lane = grid // HALF, grid % HALF
    at = jnp.where(lane < flow, row * flow + lane, -2)
    placed = jnp.where(live, place, -1)
    matches = placed[None, :] == at[:, None]
    source = jnp.sum(jnp.where(matches, index[None, :], 0), axis=1)
    told = jnp.where(
        matches, slot[None, :] + 1, (kind[None, :] == (lane - flow)[:, None]).astype(jnp.int32)
    )
    rows = jnp.sum(told, axis=1) - jnp.where(lane < flow, 1, 0)
    shape = (PLANE, 1, HALF)
    return lax.optimization_barrier((source.reshape(shape), rows.reshape(shape)))


def relayed(n, groups, points, counts, destination, wp, bp, slice_weight, softness, qkv, wo, bo):
    slots = points.shape[0] // TILE
    per_peer = slots // n
    flow = slots // PLANE
    any_spec = pl.BlockSpec(memory_space=pl.ANY)
    vmem = pl.BlockSpec(memory_space=pltpu.VMEM)
    smem = pl.BlockSpec(memory_space=pltpu.SMEM)
    dma = pltpu.SemaphoreType.DMA
    source, rows = arrange(destination, counts[0], n, lax.axis_index("dom"))
    got = pl.pallas_call(
        functools.partial(tell_kernel, n, groups),
        out_shape=jax.ShapeDtypeStruct((groups * n, 1, HALF), jnp.int32),
        in_specs=[any_spec], out_specs=any_spec,
        scratch_shapes=[dma((n * groups,)), dma((n * groups,)), dma],
        compiler_params=pltpu.CompilerParams(collective_id=0, has_side_effects=True),
        name="tell",
    )(rows)
    sends, places, branch = pl.pallas_call(
        functools.partial(table_kernel, n, groups, per_peer),
        out_shape=(
            jax.ShapeDtypeStruct((2, -(-(ROOM + per_peer) // 8) * 8), jnp.int32),
            jax.ShapeDtypeStruct((LAND + 1,), jnp.int32),
            jax.ShapeDtypeStruct((1,), jnp.int32),
        ),
        in_specs=[smem, vmem], out_specs=(smem, smem, smem),
        scratch_shapes=[pltpu.SMEM((2, LINE - 1, PLANE * LINE), jnp.int32)],
        name="table",
    )(got.reshape(groups * n, HALF), got.reshape(groups * n, HALF))

    levels = (n - 1).bit_length()
    stat_rows = 2 * FEAT + 16
    tile = (TILE, WIDTH)

    def relay(limit, at, *_):
        placed = pl.pallas_call(
            functools.partial(relay_kernel, n, per_peer, limit),
            out_shape=jax.ShapeDtypeStruct((LAND,) + tile, BF16),
            in_specs=[smem] * 4 + [any_spec] + [vmem] * 7,
            out_specs=any_spec,
            scratch_shapes=[
                pltpu.VMEM((slots,) + tile, BF16),
                pltpu.VMEM((slots + 2 * ROOM,) + tile, BF16),
                pltpu.VMEM((PLANE - 1, flow // CHUNK, CHUNK) + tile, BF16),
                pltpu.VMEM((PLANE - 1, flow // CHUNK, CHUNK) + tile, BF16),
                pltpu.VMEM((2, RING, STEP) + tile, BF16),
                pltpu.VMEM((2, RING, STEP) + tile, BF16),
                pltpu.VMEM((WIDTH, WIDTH), F32),
                pltpu.VMEM((8, WIDTH), F32),
                pltpu.VMEM((levels + 1, stat_rows, HALF), F32),
                pltpu.VMEM((levels, stat_rows, HALF), F32),
                pltpu.VMEM((WIDTH, WIDTH), BF16),
                pltpu.VMEM((WIDTH, WIDTH), BF16),
                pltpu.VMEM((WIDTH, HALF), BF16),
                pltpu.VMEM((HALF, WIDTH), BF16),
                pltpu.VMEM((WIDTH, WIDTH), BF16),
                pltpu.VMEM((HALF, HALF), F32),
                pltpu.VMEM((3, HALF, HALF), F32),
                dma((LINE,)), dma((PLANE - 1, flow // CHUNK)), dma((PLANE - 1, flow // CHUNK)),
                dma((2, RING)), dma((2, RING)), dma((levels,)), dma((levels,)), dma((LAND // CHUNK,)),
            ],
            compiler_params=pltpu.CompilerParams(
                collective_id=1 + at, has_side_effects=True, vmem_limit_bytes=62 << 20
            ),
            name="relay" + str(limit),
        )(
            source, rows, sends, places, points.reshape((slots,) + tile), wp, bp.reshape(1, WIDTH),
            slice_weight, softness.reshape(1, FEAT), qkv, wo, bo.reshape(1, WIDTH),
        )
        return placed.reshape(LAND * TILE, WIDTH)

    def fallback():
        return direct(n, points, counts, destination, wp, bp, slice_weight, softness, qkv, wo, bo)

    branches = [functools.partial(relay, limit, at) for at, limit in enumerate(LIMITS)]
    return lax.switch(branch[0], branches + [fallback])


def solution(mesh):
    spec = P(("groups", "dom"))
    wide = P(("groups", "dom"), None)
    n, groups = mesh.shape["dom"], mesh.shape["groups"]
    if n == PLANE * LINE and groups == 2:
        body = functools.partial(relayed, n, groups)
    else:
        body = functools.partial(direct, n)
    return jax.shard_map(
        body, mesh=mesh, in_specs=(wide, spec, spec) + (P(),) * 7, out_specs=wide, check_vma=False,
    )
```

```python
import functools

import jax
import jax.numpy as jnp
from jax import lax
from jax.experimental import pallas as pl
from jax.experimental.pallas import tpu as pltpu
from jax.sharding import PartitionSpec as P

WIDTH = 256
HEADS = 8
FEAT = 32
TILE = 128
LAND = 80
HALF = 128
PLANE = 4
LINE = 4
CHUNK = 5
STEP = 2
HOP = 2
RING = 4
LIMITS = (94, 102, 104, 124)
ROOM = LIMITS[-1]
ENCODE_ORDER = (0, 1, 2, 3)
LAST = 4
DEST_ORDER = ((3, 2, 1, 0), (3, 2, 0, 1), (0, 1, 3, 2), (0, 1, 2, 3))
LANES = (
    ((0, 0, 3), (0, 0, 2), (0, 1, 3), (0, 2, 3), (0, 3, 3), (0, 1, 2), (0, 2, 2), (0, 3, 2), (0, 2, 1), (0, 0, 1), (0, 1, 1), (0, 3, 1)),
    ((1, 0, 3), (1, 0, 2), (1, 1, 3), (0, 0, 3), (0, 0, 2), (0, 1, 3), (1, 2, 3), (1, 3, 3), (1, 1, 2), (0, 2, 3), (0, 3, 3), (1, 3, 2), (1, 2, 2), (0, 2, 2), (0, 3, 2), (0, 1, 2)),
    ((1, 0, 3), (1, 1, 3), (2, 0, 3), (2, 1, 3), (0, 0, 3), (0, 1, 3), (1, 2, 3), (1, 3, 3), (0, 2, 3), (2, 3, 3), (0, 3, 3), (2, 2, 3)),
)
MESH = pl.DeviceIdType.MESH
HIGHEST = lax.Precision.HIGHEST
F32 = jnp.float32
BF16 = jnp.bfloat16


def split(x):
    high = x.astype(BF16)
    return high, x - high.astype(F32)


def encode_rows(x, wp, bp, ws, wt, spread_ones, ones):
    x = x.astype(F32)
    centred = x - jnp.sum(x, axis=-1, keepdims=True) * (1.0 / WIDTH)
    spread = jnp.sum(centred * centred, axis=-1, keepdims=True) * (1.0 / WIDTH)
    normed = (centred * lax.rsqrt(spread + 1e-05)).astype(BF16)
    dot = functools.partial(jnp.dot, preferred_element_type=F32)
    proj = (dot(normed, wp) + bp).astype(BF16)
    logits = dot(proj, ws)
    soft = dot(proj, wt)
    temper = 0.5 + (jnp.maximum(soft, 0.0) + jnp.log1p(jnp.exp(-jnp.abs(soft))))
    first, rest = split(1.0 / temper)
    second, rest = split(rest)
    lane = lax.broadcasted_iota(jnp.int32, soft.shape, 1)
    parts = jnp.where(lane < HEADS, first.astype(F32), jnp.where(lane < 2 * HEADS, second.astype(F32), rest))
    scale = dot(parts.astype(BF16), spread_ones)
    raised = jnp.exp(logits * scale)
    first, rest = split(raised)
    total = dot(first, ones) + dot(rest.astype(BF16), ones)
    return proj, (raised / total).astype(BF16)


def diagonal(block, times):
    wide = jnp.concatenate([block] * times, axis=1)
    full = jnp.concatenate([wide] * times, axis=0)
    size = times * FEAT
    row = lax.broadcasted_iota(jnp.int32, (size, size), 0) // FEAT
    lane = lax.broadcasted_iota(jnp.int32, (size, size), 1) // FEAT
    return jnp.where(row == lane, full, 0.0)


def build(slice_weight, softness, qkv_small, ws, wt, spread_ones, ones, head_ones, qkv):
    ws[...] = diagonal(slice_weight[...].astype(F32), HEADS).astype(BF16)
    for i in range(3):
        qkv[i] = diagonal(qkv_small[i], 4)
    unity = jnp.ones((FEAT, FEAT), F32)
    ones[...] = diagonal(unity, HEADS).astype(BF16)
    head_ones[...] = diagonal(unity, 4)
    row = lax.broadcasted_iota(jnp.int32, (HALF, WIDTH), 0)
    lane = lax.broadcasted_iota(jnp.int32, (HALF, WIDTH), 1) // FEAT
    spread_ones[...] = jnp.where((row % HEADS == lane) & (row < 3 * HEADS), 1.0, 0.0).astype(BF16)
    flat = jnp.concatenate([softness[...].astype(F32)] * 4, axis=1)
    tall = jnp.transpose(jnp.broadcast_to(flat, (HALF, HALF)))
    tall = jnp.concatenate([tall, tall], axis=0)
    row = lax.broadcasted_iota(jnp.int32, (WIDTH, HALF), 0) // FEAT
    lane = lax.broadcasted_iota(jnp.int32, (WIDTH, HALF), 1)
    wt[...] = jnp.where((row == lane % HEADS) & (lane < 3 * HEADS), tall, 0.0).astype(BF16)


def move_kernel(
    n, per_peer, unit, source, label, points, labels, wp, bp, slice_weight, softness, qkv_small,
    wo, bo, result, labels_out,
    held_points, sending, arrived, numer, denom, sums, inbox, mixed,
    ws, wt, spread_ones, ones, head_ones, qkv,
    point_sem, send_sem, recv_sem, lab_send, lab_recv, own_sem, out_sem, red_send, red_recv,
):
    me = lax.axis_index("dom")
    pieces = per_peer // unit
    rows = unit * TILE
    fetch = pltpu.make_async_copy(points, held_points, point_sem)
    fetch.start()

    def partner(x):
        peer, bit = 0, 1
        while bit < n:
            mine, flip = me // bit % 2, x // bit % 2
            peer = peer + bit * (mine + flip - 2 * mine * flip)
            bit = bit * 2
        return peer

    barrier = pltpu.get_barrier_semaphore()
    for x in range(1, n):
        pl.semaphore_signal(barrier, inc=1, device_id={"dom": partner(x)}, device_id_type=MESH)
    numer[...] = jnp.zeros_like(numer)
    denom[...] = jnp.zeros_like(denom)
    build(slice_weight, softness, qkv_small, ws, wt, spread_ones, ones, head_ones, qkv)
    pl.semaphore_wait(barrier, n - 1)

    def order(i):
        quarter = n // 4
        near = lax.rem(i, 2) * 2 * quarter
        early = 3 * quarter + i // 2 - near
        late = jnp.where(i < 3 * quarter, i, n - 1 - i)
        return jnp.where(i < 2 * quarter, early, late)

    def lab_copy(x):
        peer = partner(x)
        return pltpu.make_async_remote_copy(
            src_ref=labels.at[peer], dst_ref=labels_out.at[me], send_sem=lab_send.at[x],
            recv_sem=lab_recv.at[x], device_id={"dom": peer}, device_id_type=MESH,
        )

    def piece_copy(x, s):
        at = pl.ds(pl.multiple_of(s * rows, rows), rows)
        return pltpu.make_async_remote_copy(
            src_ref=sending.at[x, at], dst_ref=arrived.at[x, at], send_sem=send_sem.at[x, s],
            recv_sem=recv_sem.at[x, s], device_id={"dom": partner(x)}, device_id_type=MESH,
        )

    def lab_start(x, _):
        lab_copy(x).start()
        return 0

    lax.fori_loop(1, n, lab_start, 0)
    own_lab = pltpu.make_async_copy(labels.at[me], labels_out.at[me], own_sem)
    own_lab.start()
    fetch.wait()

    def compute(x, peer, s):
        first = peer * per_peer + s * unit
        tiles = jnp.concatenate([held_points[source[first + j]] for j in range(unit)], axis=0)
        proj, weights = encode_rows(
            tiles, wp[...], bp[...], ws[...], wt[...], spread_ones[...], ones[...]
        )
        live = jnp.concatenate(
            [jnp.full((TILE, WIDTH), label[first + j], jnp.int32) for j in range(unit)], axis=0
        ) >= 0
        kept = jnp.where(live, weights.astype(F32), 0.0)
        weights = kept.astype(BF16)
        sending[x, pl.ds(pl.multiple_of(s * rows, rows), rows), :] = weights
        numer[...] += lax.dot_general(
            weights, proj, (((0,), (0,)), ((), ())), preferred_element_type=F32
        )
        denom[...] += jnp.sum(kept.reshape(rows // 8, 8, WIDTH), axis=0)

    steps = (n - 1) * pieces
    held_from = (n - 1) * (pieces - 1)

    def encode_step(i, _):
        x = order(i % (n - 1))
        compute(x, partner(x), i // (n - 1))

        @pl.when((i > 0) & (i <= held_from))
        def _():
            piece_copy(order((i - 1) % (n - 1)), (i - 1) // (n - 1)).start()

        return 0

    lax.fori_loop(0, steps, encode_step, 0)

    def own_step(s, _):
        compute(0, me, s)
        return 0

    lax.fori_loop(0, pieces, own_step, 0)

    lane_head = lax.broadcasted_iota(jnp.int32, (FEAT, HALF), 1) // FEAT
    for a in range(2):
        acc = jnp.zeros((FEAT, HALF), F32)
        for j in range(4):
            part = numer[pl.ds((a * 4 + j) * FEAT, FEAT), pl.ds(a * HALF, HALF)]
            acc = acc + jnp.where(lane_head == j, part, 0.0)
        sums[0, pl.ds(a * FEAT, FEAT), :] = acc
        total = jnp.sum(denom[:, pl.ds(a * HALF, HALF)], axis=0, keepdims=True)
        sums[0, pl.ds(2 * FEAT + a * 8, 8), :] = jnp.broadcast_to(total, (8, HALF))

    def release(i, _):
        piece_copy(order(i - held_from), pieces - 1).start()
        return 0

    level, bit = 0, n // 2
    while bit > 0:
        swap = pltpu.make_async_remote_copy(
            src_ref=sums.at[level], dst_ref=inbox.at[level], send_sem=red_send.at[level],
            recv_sem=red_recv.at[level], device_id={"dom": partner(bit)}, device_id_type=MESH,
        )
        swap.start()
        swap.wait()
        sums[level + 1] = sums[level] + inbox[level]
        level, bit = level + 1, bit // 2
        if level == max(1, (n - 1).bit_length() - 2):
            lax.fori_loop(held_from, steps, release, 0)
    mixed[...] = mix(sums[level], qkv, head_ones[...])

    def out_copy(x, s):
        at = pl.ds(pl.multiple_of(s * rows, rows), rows)
        return pltpu.make_async_copy(arrived.at[x, at], result.at[partner(x), at], out_sem.at[x, s])

    def decode(read, x, s):
        at = pl.ds(pl.multiple_of(s * rows, rows), rows)
        deslice = jnp.dot(read[x, at, :], mixed[...], preferred_element_type=F32).astype(BF16)
        y = (jnp.dot(deslice, wo[...], preferred_element_type=F32) + bo[...]).astype(BF16)
        arrived[x, at, :] = y
        out_copy(x, s).start()

    def decode_own(s, _):
        decode(sending, 0, s)
        return 0

    lax.fori_loop(0, pieces, decode_own, 0)

    def from_peer(i, _):
        x, s = order(i % (n - 1)), i // (n - 1)
        piece_copy(x, s).wait_recv()
        decode(arrived, x, s)
        return 0

    lax.fori_loop(0, steps, from_peer, 0)

    def finish(x, _):
        def one(s, _):
            piece_copy(x, s).wait_send()
            return 0

        lax.fori_loop(0, pieces, one, 0)
        lab_copy(x).wait()
        return 0

    lax.fori_loop(1, n, finish, 0)
    own_lab.wait()

    def drain(i, _):
        out_copy(i // pieces, i % pieces).wait()
        return 0

    lax.fori_loop(0, n * pieces, drain, 0)


def mix(stats, qkv, ones):
    row_head = lax.broadcasted_iota(jnp.int32, (HALF, HALF), 0) // FEAT
    lane_head = lax.broadcasted_iota(jnp.int32, (HALF, HALF), 1) // FEAT
    same = row_head == lane_head
    blocks = []
    for a in range(2):
        numer = stats[a * FEAT:(a + 1) * FEAT, :]
        row = stats[2 * FEAT + a * 8:2 * FEAT + (a + 1) * 8, :]
        col = jnp.transpose(jnp.broadcast_to(row[:1], (HALF, HALF)))
        spread = jnp.zeros((FEAT, HALF), F32)
        for j in range(4):
            spread = spread + jnp.where(
                lane_head[:FEAT] == j, col[j * FEAT:(j + 1) * FEAT, :], 0.0
            )
        tokens = numer / (spread + 1e-05)
        dot = functools.partial(jnp.dot, preferred_element_type=F32, precision=HIGHEST)
        query, keys, values = (dot(tokens, qkv[i]) for i in range(3))
        spread_keys = jnp.where(same, jnp.concatenate([keys] * 4, axis=0), 0.0)
        scores = lax.dot_general(
            query, spread_keys, (((1,), (1,)), ((), ())), preferred_element_type=F32, precision=HIGHEST
        ) * FEAT ** (-0.5)
        raised = jnp.exp(scores)
        attend = raised / dot(raised, ones)
        spread_values = jnp.where(same, jnp.concatenate([values] * 4, axis=0), 0.0)
        mixed = dot(attend, spread_values)
        blocks.append(jnp.where(same, jnp.concatenate([mixed] * 4, axis=0), 0.0))
    nil = jnp.zeros((HALF, HALF), F32)
    return jnp.concatenate(
        [jnp.concatenate([blocks[0], nil], axis=1), jnp.concatenate([nil, blocks[1]], axis=1)], axis=0
    ).astype(BF16)


def place_kernel(n, per_peer, chunks, per_chunk, labels, tiles, out, held, in_sem, out_sem):
    def load(k, _):
        def one(t, _):
            slot = labels[k, t]

            @pl.when(slot >= 0)
            def _():
                pltpu.make_async_copy(
                    tiles.at[k * per_peer + t], held.at[slot], in_sem.at[slot // per_chunk]
                ).start()

            return 0

        return lax.fori_loop(0, per_peer, one, 0)

    lax.fori_loop(0, n, load, 0)

    def step(c, _):
        part = pl.ds(c * per_chunk, per_chunk)
        pltpu.make_async_copy(tiles.at[pl.ds(0, per_chunk)], held.at[part], in_sem.at[c]).wait()
        pltpu.make_async_copy(held.at[part], out.at[part], out_sem.at[c]).start()
        return 0

    lax.fori_loop(0, chunks, step, 0)

    def finish(c, _):
        part = pl.ds(c * per_chunk, per_chunk)
        pltpu.make_async_copy(held.at[part], out.at[part], out_sem.at[c]).wait()
        return 0

    lax.fori_loop(0, chunks, finish, 0)


def plan(destination, own_count, n):
    slots = destination.shape[0]
    per_peer = slots // n
    index = jnp.arange(slots, dtype=jnp.int32)
    live = index < own_count
    target = jnp.where(live, destination // LAND, -1)
    slot = jnp.where(live, destination % LAND, -1)
    earlier = (target[:, None] == target[None, :]) & live[None, :] & (index[None, :] < index[:, None])
    rank = jnp.sum(earlier.astype(jnp.int32), axis=1)
    place = target * per_peer + rank
    matches = live[None, :] & (place[None, :] == index[:, None])
    source = jnp.sum(jnp.where(matches, index[None, :], 0), axis=1)
    label = jnp.sum(jnp.where(matches, slot[None, :] + 1, 0), axis=1) - 1
    return source, label


def direct(n, points, counts, destination, wp, bp, slice_weight, softness, qkv, wo, bo):
    slots = points.shape[0] // TILE
    per_peer = slots // n
    any_spec = pl.BlockSpec(memory_space=pl.ANY)
    vmem = pl.BlockSpec(memory_space=pltpu.VMEM)
    smem = pl.BlockSpec(memory_space=pltpu.SMEM)
    source, label = plan(destination, counts[0], n)
    rows = per_peer * TILE
    labels = jnp.pad(label.reshape(n, 1, per_peer), ((0, 0), (0, 0), (0, HALF - per_peer)))
    unit = 2 if per_peer % 2 == 0 else 1
    pieces = per_peer // unit
    levels = (n - 1).bit_length()
    stat_rows = 2 * FEAT + 16
    dma = pltpu.SemaphoreType.DMA
    tiles, arrived_lab = pl.pallas_call(
        functools.partial(move_kernel, n, per_peer, unit),
        out_shape=(
            jax.ShapeDtypeStruct((n, rows, WIDTH), BF16),
            jax.ShapeDtypeStruct((n, 1, HALF), jnp.int32),
        ),
        in_specs=[smem, smem, any_spec, any_spec] + [vmem] * 7,
        out_specs=(any_spec, any_spec),
        scratch_shapes=[
            pltpu.VMEM((slots, TILE, WIDTH), BF16),
            pltpu.VMEM((n, rows, WIDTH), BF16),
            pltpu.VMEM((n, rows, WIDTH), BF16),
            pltpu.VMEM((WIDTH, WIDTH), F32),
            pltpu.VMEM((8, WIDTH), F32),
            pltpu.VMEM((levels + 1, stat_rows, HALF), F32),
            pltpu.VMEM((levels, stat_rows, HALF), F32),
            pltpu.VMEM((WIDTH, WIDTH), BF16),
            pltpu.VMEM((WIDTH, WIDTH), BF16),
            pltpu.VMEM((WIDTH, HALF), BF16),
            pltpu.VMEM((HALF, WIDTH), BF16),
            pltpu.VMEM((WIDTH, WIDTH), BF16),
            pltpu.VMEM((HALF, HALF), F32),
            pltpu.VMEM((3, HALF, HALF), F32),
            dma, dma((n, pieces)), dma((n, pieces)), dma((n,)), dma((n,)), dma, dma((n, pieces)),
            dma((levels,)), dma((levels,)),
        ],
        compiler_params=pltpu.CompilerParams(
            collective_id=15, has_side_effects=True, vmem_limit_bytes=60 << 20
        ),
        name="move",
    )(
        source, label, points.reshape(slots, TILE, WIDTH), labels, wp, bp.reshape(1, WIDTH),
        slice_weight, softness.reshape(1, FEAT), qkv, wo, bo.reshape(1, WIDTH),
    )

    per_chunk = 8
    chunks = LAND // per_chunk
    placed = pl.pallas_call(
        functools.partial(place_kernel, n, per_peer, chunks, per_chunk),
        out_shape=jax.ShapeDtypeStruct((LAND, TILE, WIDTH), BF16),
        grid_spec=pltpu.PrefetchScalarGridSpec(
            num_scalar_prefetch=1, grid=(), in_specs=[any_spec], out_specs=any_spec,
            scratch_shapes=[pltpu.VMEM((LAND, TILE, WIDTH), BF16), dma((chunks,)), dma((chunks,))],
        ),
        compiler_params=pltpu.CompilerParams(vmem_limit_bytes=60 << 20),
        name="place",
    )(arrived_lab.reshape(n, HALF), tiles.reshape(slots, TILE, WIDTH))
    return placed.reshape(LAND * TILE, WIDTH)


def mirror(me, n):
    steps, bit = [], 1
    while bit < n:
        steps.append((bit, bit - 2 * bit * (me // bit % 2)))
        bit = bit * 2

    def peer(x):
        out = me
        for bit, step in steps:
            if isinstance(x, int):
                out = out + step if x & bit else out
            else:
                out = out + step * (x // bit % 2)
        return out

    return peer


def tell_kernel(n, groups, rows, got, send_sem, recv_sem, own_sem):
    me, group = lax.axis_index("dom"), lax.axis_index("groups")
    near = groups * PLANE
    mine = me // PLANE * near
    peer, other = mirror(me, n), mirror(group, groups)
    barrier = pltpu.get_barrier_semaphore()

    def device(x):
        return {"groups": other(x // n), "dom": peer(x % n)}

    for x in range(1, n * groups):
        pl.semaphore_signal(barrier, inc=1, device_id=device(x), device_id_type=MESH)
    own = pltpu.make_async_copy(rows.at[0], got.at[mine], own_sem)
    own.start()
    pl.semaphore_wait(barrier, n * groups - 1)

    def tell(x):
        w = x % PLANE
        return pltpu.make_async_remote_copy(
            src_ref=rows.at[w], dst_ref=got.at[mine + x // n * PLANE + w], send_sem=send_sem.at[x],
            recv_sem=recv_sem.at[x], device_id=device(x), device_id_type=MESH,
        )

    copies = [tell(x) for x in range(1, n * groups)]
    for copy in copies:
        copy.start()
    for copy in copies:
        copy.wait()
    own.wait()


def encoded(i):
    return (2 * i + 1) // 3


def due(w, j):
    step = PLANE * j + ENCODE_ORDER.index(w)
    if w == 0:
        return ((2 * step + 1) * 171) >> 9
    if w == 1:
        return ((2 * step + 4) * 171) >> 9
    return 5 * j + (4 if ENCODE_ORDER.index(w) < ENCODE_ORDER.index(5 - w) else 7)


def timetable(sizes):
    starts, longest = {}, 0
    firsts = {}
    for zo in range(LINE):
        for w in range(PLANE):
            total = 0
            for zd in DEST_ORDER[zo]:
                if zd != zo:
                    firsts[zo, w, zd] = total
                    total = total + sizes[zo, w, zd]
    for way in range(2):
        def real(cl):
            return (LINE - 1 - cl[0], cl[1], LINE - 1 - cl[2]) if way else cl

        for lane, order in enumerate(LANES):
            pos = 0
            for cl in order:
                size = sizes[real(cl)]
                if cl[0] == lane:
                    begin = firsts[real(cl)]
                    last = ((begin + size - 1) * 13) >> 6
                    slack = CHUNK * last - begin - (1 if cl[1] < 2 else 0)
                    ready = STEP * due(cl[1], last) - jnp.maximum(0, slack)
                else:
                    ready = starts[way, lane - 1, cl] + HOP * STEP
                start = jnp.maximum(pos, jnp.where(size > 0, ready, 0))
                starts[way, lane, cl] = start
                pos = start + size
            longest = jnp.maximum(longest, pos)
    return starts, longest


def table_kernel(n, groups, per_peer, got, wide, sends, slots, branch, starts):
    z = lax.axis_index("dom") // PLANE
    flow = LINE * per_peer
    near = groups * PLANE
    table = sends.shape[1]

    def clear(i, _):
        for k in range(8):
            sends[0, i * 8 + k] = 0
            sends[1, i * 8 + k] = 0
        return 0

    lax.fori_loop(0, table // 8, clear, 0)

    sizes = {
        (zo, w, zd): got[zo * near + w, flow + w * LINE + zd]
        for zo in range(LINE) for w in range(PLANE) for zd in range(LINE)
    }
    mine, _ = timetable(sizes)
    for way in range(2):
        for lane, order in enumerate(LANES):
            for at, cl in enumerate(order):
                starts[way, lane, at] = mine[way, lane, cl]

    full = jnp.concatenate([wide[...], jnp.zeros((HALF - wide.shape[0], HALF), jnp.int32)], axis=0)
    turned = jnp.transpose(full)
    lanes = lax.broadcasted_iota(jnp.int32, (LINE, HALF), 1)
    every = {}
    for w in range(PLANE):
        block = turned[flow + w * LINE:flow + (w + 1) * LINE]
        for bit in (1, 2):
            if w & bit:
                block = jnp.where(
                    lanes // bit % 2 == 0, pltpu.roll(block, HALF - bit, 1), pltpu.roll(block, bit, 1)
                )
        for zo in range(LINE):
            moved = pltpu.roll(block, HALF - zo * near, 1) if zo else block
            for zd in range(LINE):
                every[zo, w, zd] = jnp.broadcast_to(moved[zd:zd + 1], (8, HALF))
    _, longest = timetable(every)
    lanes = lax.broadcasted_iota(jnp.int32, (8, HALF), 1)
    longest = jnp.max(jnp.where(lanes < near, longest, 0))
    choice = jnp.int32(0)
    for limit in LIMITS:
        choice = choice + jnp.where(longest > limit, 1, 0)
    branch[0] = choice

    def fill(me):
        def row(zo, w):
            return zo * near + w

        def size_of(zo, w, zd):
            return got[row(zo, w), flow + w * LINE + zd]

        def first_of(zo, w, zd):
            total = jnp.int32(0)
            for real in DEST_ORDER[zo]:
                if real == zd:
                    return total
                total = total + size_of(zo, w, real)

        for way in range(2):
            def plane(p):
                return LINE - 1 - p if way else p

            lane = plane(me)
            if lane == LINE - 1:
                continue
            landed = PLANE * flow + way * ROOM
            for at, cl in enumerate(LANES[lane]):
                zo, w, zd = plane(cl[0]), cl[1], plane(cl[2])
                if zo == me:
                    source = w * flow + first_of(zo, w, zd)
                else:
                    source = landed + starts[way, lane - 1, LANES[lane - 1].index(cl)]
                size = size_of(zo, w, zd)
                start = jnp.minimum(starts[way, lane, at], ROOM)
                for k in range(per_peer):
                    sends[way, start + k] = jnp.where(k < size, source + k, 0)
        for zo in range(LINE):
            for w in range(PLANE):
                first = first_of(zo, w, me)
                size = size_of(zo, w, me)
                if zo == me:
                    source = w * flow + first
                else:
                    way = 0 if zo < me else 1
                    lane = me - 1 if zo < me else LINE - 2 - me
                    cl = (zo, w, me) if zo < me else (LINE - 1 - zo, w, LINE - 1 - me)
                    source = PLANE * flow + way * ROOM + starts[way, lane, LANES[lane].index(cl)]
                for k in range(per_peer):
                    label = got[row(zo, w), first + k]
                    slots[jnp.where(k < size, label + 1, 0)] = source + k

    for me in range(LINE):
        @pl.when(z == me)
        def _():
            fill(me)


def relay_kernel(
    n, per_peer, limit, source, label, sends, slots, points, wp, bp, slice_weight, softness, qkv_small,
    wo, bo, result,
    held, pool, sending, landed, stage, landing, numer, denom, sums, inbox, mixed,
    ws, wt, spread_ones, ones, head_ones, qkv,
    point_sem, plane_send, plane_recv, line_send, line_recv, red_send, red_recv, out_sem,
):
    me = lax.axis_index("dom")
    z = me // PLANE
    peer = mirror(me, n)
    flow = LINE * per_peer
    chunks = flow // CHUNK
    rounds = limit // STEP
    share = points.shape[0] // LINE

    def fetch(i):
        at = pl.ds(i * share, share)
        return pltpu.make_async_copy(points.at[at], held.at[at], point_sem.at[i])

    for i in range(LINE):
        fetch(i).start()
    barrier = pltpu.get_barrier_semaphore()
    for x in range(1, n):
        pl.semaphore_signal(barrier, inc=1, device_id={"dom": peer(x)}, device_id_type=MESH)
    numer[...] = jnp.zeros_like(numer)
    denom[...] = jnp.zeros_like(denom)
    build(slice_weight, softness, qkv_small, ws, wt, spread_ones, ones, head_ones, qkv)
    pl.semaphore_wait(barrier, n - 1)
    for i in range(LINE):
        fetch(i).wait()

    def plane_copy(w, j):
        return pltpu.make_async_remote_copy(
            src_ref=sending.at[w - 1, j], dst_ref=landed.at[w - 1, j], send_sem=plane_send.at[w - 1, j],
            recv_sem=plane_recv.at[w - 1, j], device_id={"dom": peer(w)},
            device_id_type=MESH,
        )

    def line_copy(way, r):
        slot = r % RING
        near = me + PLANE if way == 0 else me - PLANE
        return pltpu.make_async_remote_copy(
            src_ref=stage.at[way, slot], dst_ref=landing.at[way, slot], send_sem=line_send.at[way, slot],
            recv_sem=line_recv.at[way, slot], device_id={"dom": near}, device_id_type=MESH,
        )

    can_send = (z < LINE - 1, z > 0)
    can_recv = (z > 0, z < LINE - 1)

    def encode(i, _):
        j, turn = i // PLANE, i % PLANE
        w = ENCODE_ORDER[0]
        for at in range(1, PLANE):
            w = jnp.where(turn == at, ENCODE_ORDER[at], w)
        tiles = jnp.concatenate([held[source[w, 0, j * CHUNK + k]] for k in range(CHUNK)], axis=0)
        proj, weights = encode_rows(
            tiles, wp[...], bp[...], ws[...], wt[...], spread_ones[...], ones[...]
        )
        live = jnp.concatenate(
            [jnp.full((TILE, WIDTH), label[w, 0, j * CHUNK + k], jnp.int32) for k in range(CHUNK)], axis=0
        ) >= 0
        kept = jnp.where(live, weights.astype(F32), 0.0)
        weights = kept.astype(BF16)
        numer[...] += lax.dot_general(
            weights, proj, (((0,), (0,)), ((), ())), preferred_element_type=F32
        )
        denom[...] += jnp.sum(kept.reshape(CHUNK * TILE // 8, 8, WIDTH), axis=0)
        weights = weights.reshape(CHUNK, TILE, WIDTH)

        @pl.when(turn == 0)
        def _():
            pool[pl.ds(j * CHUNK, CHUNK)] = weights

        @pl.when(turn > 0)
        def _():
            sending[w - 1, j] = weights

        @pl.when(turn == ENCODE_ORDER.index(1))
        def _():
            plane_copy(1, j).start()

        return 0

    def line_arrive(way, m):
        line_copy(way, m).wait_recv()
        pool[pl.ds(PLANE * flow + way * ROOM + m * STEP, STEP)] = landing[way, m % RING]

    def release(w, r):
        begin, first = due(w, 0) - 5, encoded(ENCODE_ORDER.index(w))
        since = r - begin
        j = since // 5
        now = (since % 5 == 0) & (j >= 0) & (j < chunks)
        if begin < first:
            now = (now & (j > 0)) | (r == first)
            j = jnp.where(r == first, 0, j)

        @pl.when(now)
        def _():
            plane_copy(w, j).start()

    def relay(r):
        for w in range(2, PLANE):
            release(w, r)
        for way in range(2):
            @pl.when(can_recv[way] & (r >= HOP))
            def _():
                line_arrive(way, r - HOP)
        for w in range(1, PLANE):
            if w == 1:
                late = 2 * ENCODE_ORDER.index(w) + 4
                j = (3 * r + 7 - late) // 8
                now = (3 * r + 7 >= late) & ((8 * j + late) // 3 == r)
            else:
                since = r - due(w, 0)
                j = since // 5
                now = (since >= 0) & (since % 5 == 0)

            @pl.when(now & (j < chunks))
            def _():
                plane_copy(w, j).wait_recv()
                pool[pl.ds(w * flow + j * CHUNK, CHUNK)] = landed[w - 1, j]

        for way in range(2):
            @pl.when(can_send[way])
            def _():
                @pl.when(r >= RING)
                def _():
                    line_copy(way, r - RING).wait_send()

                for k in range(STEP):
                    stage[way, r % RING, k] = pool[sends[way, r * STEP + k]]
                line_copy(way, r).start()

    steps = PLANE * chunks

    reached = encoded(steps - 1) + 1
    levels = sums.shape[0] - 1
    group = LAND // (2 * LAST)
    early = rounds - LAST
    seen = (early - HOP + 1) * STEP
    rest = limit - seen

    def swap(level):
        return pltpu.make_async_remote_copy(
            src_ref=sums.at[level], dst_ref=inbox.at[level], send_sem=red_send.at[level],
            recv_sem=red_recv.at[level], device_id={"dom": peer(n >> (level + 1))}, device_id_type=MESH,
        )

    def own_sums():
        lane_head = lax.broadcasted_iota(jnp.int32, (FEAT, HALF), 1) // FEAT
        for a in range(2):
            acc = jnp.zeros((FEAT, HALF), F32)
            for j in range(4):
                part = numer[pl.ds((a * 4 + j) * FEAT, FEAT), pl.ds(a * HALF, HALF)]
                acc = acc + jnp.where(lane_head == j, part, 0.0)
            sums[0, pl.ds(a * FEAT, FEAT), :] = acc
            total = jnp.sum(denom[:, pl.ds(a * HALF, HALF)], axis=0, keepdims=True)
            sums[0, pl.ds(2 * FEAT + a * 8, 8), :] = jnp.broadcast_to(total, (8, HALF))

    def decode(rows):
        deslice = jnp.dot(rows, mixed[...], preferred_element_type=F32).astype(BF16)
        y = (jnp.dot(deslice, wo[...], preferred_element_type=F32) + bo[...]).astype(BF16)
        return y.reshape(rows.shape[0] // TILE, TILE, WIDTH)

    def decode_slots(i, _):
        rows = jnp.concatenate([pool[slots[i * group + k + 1]] for k in range(group)], axis=0)
        held[pl.ds(i * group, group)] = decode(rows)
        return 0

    def one_round(r, _):
        @pl.when(r < reached)
        def _():
            lax.fori_loop(3 * r // 2, jnp.minimum(3 * (r + 1) // 2, steps), encode, 0)

        @pl.when(r == reached)
        def _():
            own_sums()
            swap(0).start()

        for level in range(levels):
            @pl.when(r == reached + 4 * (level + 1))
            def _():
                swap(level).wait()
                sums[level + 1] = sums[level] + inbox[level]
                if level + 1 < levels:
                    swap(level + 1).start()
                else:
                    mixed[...] = mix(sums[levels], qkv, head_ones[...])

        relay(r)

        @pl.when(r >= early)
        def _():
            lax.fori_loop(2 * (r - early), 2 * (r - early) + 2, decode_slots, 0)

        return 0

    lax.fori_loop(0, rounds, one_round, 0)
    final = rest // 2
    blocks = rest // final

    def decode_rest(i, _):
        way, part = i % 2, i // 2
        begin = PLANE * flow + way * ROOM + seen + part * final
        rows = pool[pl.ds(begin, final)].reshape(final * TILE, WIDTH)
        held[pl.ds(LAND + way * rest + part * final, final)] = decode(rows)
        return 0

    lax.fori_loop(0, 2 * (blocks - 1), decode_rest, 0)
    for m in range(rounds - HOP, rounds):
        for way in range(2):
            @pl.when(can_recv[way])
            def _():
                line_arrive(way, m)
    lax.fori_loop(2 * (blocks - 1), 2 * blocks, decode_rest, 0)

    def out_copy(i):
        return pltpu.make_async_copy(
            landed.at[i // chunks, i % chunks], result.at[pl.ds(i * CHUNK, CHUNK)], out_sem.at[i]
        )

    def finish(i, _):
        for k in range(CHUNK):
            at = i * CHUNK + k
            where = slots[at + 1] - PLANE * flow
            way = jnp.where(where >= ROOM, 1, 0)
            pos = where - way * ROOM - seen
            late = (where >= 0) & (pos >= 0)
            landed[i // chunks, i % chunks, k] = held[jnp.where(late, LAND + way * rest + pos, at)]
        out_copy(i).start()
        return 0

    lax.fori_loop(0, LAND // CHUNK, finish, 0)

    for way in range(2):
        @pl.when(can_send[way])
        def _():
            def sent(r, _):
                line_copy(way, r).wait_send()
                return 0

            lax.fori_loop(rounds - RING, rounds, sent, 0)

    def plane_sent(i, _):
        plane_copy(1 + i % (PLANE - 1), i // (PLANE - 1)).wait_send()
        return 0

    lax.fori_loop(0, (PLANE - 1) * chunks, plane_sent, 0)

    def drain(i, _):
        out_copy(i).wait()
        return 0

    lax.fori_loop(0, LAND // CHUNK, drain, 0)


def arrange(destination, own_count, n, me):
    slots = destination.shape[0]
    flow = slots // PLANE
    index = jnp.arange(slots, dtype=jnp.int32)
    live = index < own_count
    target, slot = destination // LAND, destination % LAND
    w = (target % PLANE) ^ (me % PLANE)
    line, own = target // PLANE, me // PLANE
    upper = own >= LINE // 2
    far = jnp.where(upper, LINE - 1 - line, line)
    near = jnp.where(upper, LINE - 1 - own, own)
    rank = jnp.where(
        far > near, LINE - 1 - far, jnp.where(far < near, LINE - 1 - near + far, LINE - 1)
    )
    w = jnp.where(live, w, -1)
    key = rank * slots + index
    earlier = (w[:, None] == w[None, :]) & (key[None, :] < key[:, None])
    place = w * flow + jnp.sum(earlier.astype(jnp.int32), axis=1)
    kind = jnp.where(live, w * LINE + line, -HALF)
    grid = jnp.arange(PLANE * HALF, dtype=jnp.int32)
    row, lane = grid // HALF, grid % HALF
    at = jnp.where(lane < flow, row * flow + lane, -2)
    placed = jnp.where(live, place, -1)
    matches = placed[None, :] == at[:, None]
    source = jnp.sum(jnp.where(matches, index[None, :], 0), axis=1)
    told = jnp.where(
        matches, slot[None, :] + 1, (kind[None, :] == (lane - flow)[:, None]).astype(jnp.int32)
    )
    rows = jnp.sum(told, axis=1) - jnp.where(lane < flow, 1, 0)
    shape = (PLANE, 1, HALF)
    return lax.optimization_barrier((source.reshape(shape), rows.reshape(shape)))


def relayed(n, groups, points, counts, destination, wp, bp, slice_weight, softness, qkv, wo, bo):
    slots = points.shape[0] // TILE
    per_peer = slots // n
    flow = slots // PLANE
    any_spec = pl.BlockSpec(memory_space=pl.ANY)
    vmem = pl.BlockSpec(memory_space=pltpu.VMEM)
    smem = pl.BlockSpec(memory_space=pltpu.SMEM)
    dma = pltpu.SemaphoreType.DMA
    source, rows = arrange(destination, counts[0], n, lax.axis_index("dom"))
    got = pl.pallas_call(
        functools.partial(tell_kernel, n, groups),
        out_shape=jax.ShapeDtypeStruct((groups * n, 1, HALF), jnp.int32),
        in_specs=[any_spec], out_specs=any_spec,
        scratch_shapes=[dma((n * groups,)), dma((n * groups,)), dma],
        compiler_params=pltpu.CompilerParams(collective_id=0, has_side_effects=True),
        name="tell",
    )(rows)
    sends, places, branch = pl.pallas_call(
        functools.partial(table_kernel, n, groups, per_peer),
        out_shape=(
            jax.ShapeDtypeStruct((2, -(-(ROOM + per_peer) // 8) * 8), jnp.int32),
            jax.ShapeDtypeStruct((LAND + 1,), jnp.int32),
            jax.ShapeDtypeStruct((1,), jnp.int32),
        ),
        in_specs=[smem, vmem], out_specs=(smem, smem, smem),
        scratch_shapes=[pltpu.SMEM((2, LINE - 1, PLANE * LINE), jnp.int32)],
        name="table",
    )(got.reshape(groups * n, HALF), got.reshape(groups * n, HALF))

    levels = (n - 1).bit_length()
    stat_rows = 2 * FEAT + 16
    tile = (TILE, WIDTH)

    def relay(limit, at, *_):
        placed = pl.pallas_call(
            functools.partial(relay_kernel, n, per_peer, limit),
            out_shape=jax.ShapeDtypeStruct((LAND,) + tile, BF16),
            in_specs=[smem] * 4 + [any_spec] + [vmem] * 7,
            out_specs=any_spec,
            scratch_shapes=[
                pltpu.VMEM((slots,) + tile, BF16),
                pltpu.VMEM((slots + 2 * ROOM,) + tile, BF16),
                pltpu.VMEM((PLANE - 1, flow // CHUNK, CHUNK) + tile, BF16),
                pltpu.VMEM((PLANE - 1, flow // CHUNK, CHUNK) + tile, BF16),
                pltpu.VMEM((2, RING, STEP) + tile, BF16),
                pltpu.VMEM((2, RING, STEP) + tile, BF16),
                pltpu.VMEM((WIDTH, WIDTH), F32),
                pltpu.VMEM((8, WIDTH), F32),
                pltpu.VMEM((levels + 1, stat_rows, HALF), F32),
                pltpu.VMEM((levels, stat_rows, HALF), F32),
                pltpu.VMEM((WIDTH, WIDTH), BF16),
                pltpu.VMEM((WIDTH, WIDTH), BF16),
                pltpu.VMEM((WIDTH, HALF), BF16),
                pltpu.VMEM((HALF, WIDTH), BF16),
                pltpu.VMEM((WIDTH, WIDTH), BF16),
                pltpu.VMEM((HALF, HALF), F32),
                pltpu.VMEM((3, HALF, HALF), F32),
                dma((LINE,)), dma((PLANE - 1, flow // CHUNK)), dma((PLANE - 1, flow // CHUNK)),
                dma((2, RING)), dma((2, RING)), dma((levels,)), dma((levels,)), dma((LAND // CHUNK,)),
            ],
            compiler_params=pltpu.CompilerParams(
                collective_id=1 + at, has_side_effects=True, vmem_limit_bytes=62 << 20
            ),
            name="relay" + str(limit),
        )(
            source, rows, sends, places, points.reshape((slots,) + tile), wp, bp.reshape(1, WIDTH),
            slice_weight, softness.reshape(1, FEAT), qkv, wo, bo.reshape(1, WIDTH),
        )
        return placed.reshape(LAND * TILE, WIDTH)

    def fallback():
        return direct(n, points, counts, destination, wp, bp, slice_weight, softness, qkv, wo, bo)

    branches = [functools.partial(relay, limit, at) for at, limit in enumerate(LIMITS)]
    return lax.switch(branch[0], branches + [fallback])


def solution(mesh):
    spec = P(("groups", "dom"))
    wide = P(("groups", "dom"), None)
    n, groups = mesh.shape["dom"], mesh.shape["groups"]
    if n == PLANE * LINE and groups == 2:
        body = functools.partial(relayed, n, groups)
    else:
        body = functools.partial(direct, n)
    return jax.shard_map(
        body, mesh=mesh, in_specs=(wide, spec, spec) + (P(),) * 7, out_specs=wide, check_vma=False,
    )
```
